128 devices in a mesh: ctx: 16 (over x, y), tp: 8 (over z, core).
Axes of the slice: x: 4, y: 4, z: 4, core: 2. Of those that a mesh axis runs over, the one named last changes fastest.
Arguments:
- queries: bfloat16 [4096, 8192], P('ctx', 'tp'), may hold values from -160 to 160
- keys: bfloat16 [4096, 1024], P('ctx', 'tp'), may hold values from -4 to 4
- values: bfloat16 [4096, 1024], P('ctx', 'tp'), may hold values from -6 to 6
- positions: int32 [4096], P('ctx'), may hold values from 0 to 4095, as said below
- out_weight: bfloat16 [8192, 8192], P('tp'), may hold values from -0.5 to 0.5
Outputs:
- attn_out: bfloat16 [4096, 8192], P(('ctx', 'tp'))
The draws below stay inside these ranges and needn't reach their ends.
Inputs may be any that keep to these rules, and one draw needn't show every extreme that they name: positions holds every number of 0 to 4095 once; it is made of 32 runs of 128 rows, each run holding ascending consecutive positions that start at a multiple of 128; the order of the runs is arbitrary.
All inputs are finite; a program needn't handle non-finite values.
Results may differ from the reference program's by a relative error of at most 0.015.
Values may be sent and summed in bfloat16 or wider, within the bound.
No kernel may reach another device: no remote copies, remote signals or barrier semaphores. Data moves between devices by JAX's collectives and lax.ppermute only.
A program may use at most 64 MiB of HBM per device.

```python
import jax
import jax.numpy as jnp
from jax import lax

HEADS = 64
KVH = 8
HD = 128
DOUT = 8192
TOK_DEV = 256
SEQ = 4096
SPAN = 128
SPANS = 32
N_TP = 8


def span_positions(key):
    span_order = jax.random.permutation(jax.random.fold_in(key, 11), SPANS)
    layout = span_order[:, None] * SPAN + jnp.arange(SPAN)[None, :]
    return layout.reshape(SEQ).astype(jnp.int32)


def key_rows(key):
    key_field = jax.random.normal(jax.random.fold_in(key, 21), (SEQ, KVH * HD), jnp.float32)
    key_field = jnp.clip(key_field, -4.0, 4.0)
    return key_field


def draw_positions(key, part):
    return span_positions(key)


def draw_keys(key, part):
    return key_rows(key).astype(jnp.bfloat16)


def draw_queries(key, part):
    query_field = jax.random.normal(jax.random.fold_in(key, 31), (SEQ, HEADS * HD), jnp.float32)
    query_field = jnp.clip(query_field, -6.0, 6.0)
    return query_field.astype(jnp.bfloat16)


def shard_levels(rng, extent, cuts, smallest, high):
    factor_of, own = 1.0, jax.random.fold_in(rng, 6)
    for dim, blocks in cuts:
        steps = jnp.exp(jax.random.uniform(jax.random.fold_in(own, dim), (blocks,), jnp.float32, smallest / len(cuts), high / len(cuts)))
        factor_of = factor_of * jnp.repeat(steps, extent[dim] // blocks).reshape([-1 if axis == dim else 1 for axis in range(len(extent))])
    return factor_of


def bell_draw(own_key, dims, width, reach, split=(), dtype=jnp.bfloat16):
    loudness = shard_levels(own_key, dims, split, -0.22, 0.18) if split else 1.0
    drawn = jax.random.normal(own_key, dims, jnp.float32) * width * loudness
    return jnp.minimum(jnp.maximum(drawn, -reach), reach).astype(dtype)


def setup_inputs(seed: int = 0) -> dict:
    arg_keys = jax.random.split(jax.random.key(seed), 6)
    return {
        "queries": draw_queries(jax.random.fold_in(arg_keys[5], 71), 0),
        "keys": draw_keys(jax.random.fold_in(arg_keys[5], 71), 0),
        "values": bell_draw(arg_keys[2], (SEQ, KVH * HD), 1.0, 6.0, ((0, 16), (1, 8))),
        "positions": draw_positions(jax.random.fold_in(arg_keys[5], 71), 0),
        "out_weight": bell_draw(arg_keys[4], (HEADS * HD, DOUT), (HEADS * HD // 64) ** -0.5, 0.5, ((0, 8),)),
    }


def attend(query_block, query_pos, key_block, value_block, key_pos):
    rows_q = query_block.shape[0]
    rows_k = key_block.shape[0]
    groups = key_block.shape[1] // HD
    repeat = query_block.shape[1] // (groups * HD)
    query_heads = query_block.astype(jnp.float32).reshape(rows_q, groups, repeat, HD)
    key_heads = key_block.astype(jnp.float32).reshape(rows_k, groups, HD)
    value_heads = value_block.astype(jnp.float32).reshape(rows_k, groups, HD)
    scores = jnp.einsum("qgrd,kgd->grqk", query_heads, key_heads) * (HD ** -0.5)
    visible = key_pos[None, :] <= query_pos[:, None]
    scores = jnp.where(visible, scores, jnp.float32(-1e30))
    block_max = jnp.max(scores, axis=-1)
    weights = jnp.where(visible, jnp.exp(scores - block_max[..., None]), jnp.float32(0.0))
    block_total = jnp.sum(weights, axis=-1)
    rounded = lax.optimization_barrier(weights.astype(jnp.bfloat16)).astype(jnp.float32)
    summed = jnp.einsum("grqk,kgd->qgrd", rounded, value_heads)
    scaled = summed / jnp.transpose(jnp.maximum(block_total, 1.0), (2, 0, 1))[..., None]
    block_out = lax.optimization_barrier(scaled.reshape(rows_q, groups * repeat * HD).astype(jnp.bfloat16))
    return (block_out, block_max.reshape(groups * repeat, rows_q), block_total.reshape(groups * repeat, rows_q))


def combine_parts(outputs, maxima, totals):
    overall = jnp.max(maxima, axis=0)
    weights = jnp.exp(maxima - overall[None]) * totals
    weights = weights / jnp.sum(weights, axis=0)[None]
    number, tok_rows, head_width = outputs.shape
    head_count = maxima.shape[1]
    spread = outputs.astype(jnp.float32).reshape(number, tok_rows, head_count, head_width // head_count)
    merged = jnp.sum(spread * jnp.transpose(weights, (0, 2, 1))[..., None], axis=0)
    return lax.optimization_barrier(merged.reshape(tok_rows, head_width).astype(jnp.bfloat16))


def reference(queries, keys, values, positions, out_weight):
    blocks = SEQ // TOK_DEV
    query_blocks = queries.reshape(blocks, TOK_DEV, HEADS * HD)
    key_blocks = keys.reshape(blocks, TOK_DEV, KVH * HD)
    value_blocks = values.reshape(blocks, TOK_DEV, KVH * HD)
    position_blocks = positions.reshape(blocks, TOK_DEV)
    group_width = HEADS * HD // N_TP
    weight_groups = out_weight.reshape(N_TP, group_width, DOUT).astype(jnp.float32)

    def one_block(operands):
        query_block, query_pos = operands

        def against(key_operands):
            return attend(query_block, query_pos, key_operands[0], key_operands[1], key_operands[2])

        parts = lax.map(against, (key_blocks, value_blocks, position_blocks))
        merged = combine_parts(parts[0], parts[1], parts[2])
        pieces = merged.astype(jnp.float32).reshape(TOK_DEV, N_TP, group_width)
        group_sums = jnp.einsum("tgw,gwo->gto", pieces, weight_groups)
        group_sums = lax.optimization_barrier(group_sums.astype(jnp.bfloat16)).astype(jnp.float32)
        return jnp.sum(group_sums, axis=0).astype(jnp.bfloat16)

    result = lax.map(one_block, (query_blocks, position_blocks))
    return result.reshape(SEQ, DOUT)
```

```python
import functools
import math

import jax
import jax.numpy as jnp
from jax import lax
from jax.experimental import pallas as pl
from jax.experimental.pallas import tpu as pltpu
from jax.sharding import PartitionSpec as P

HD = 128
SPAN = 128
HEADS = 8
QUAD = 4
PACK = 272
LOG_SCALE = HD ** -0.5 * math.log2(math.e)
NEG = -1e30
NX = 4
NZ = 4
NCORE = 2
PIECE = 16
DOUT = 8192
NCOL = 8


VMEM = pl.BlockSpec(memory_space=pltpu.VMEM)
SMEM = pl.BlockSpec(memory_space=pltpu.SMEM)
ANY = pl.BlockSpec(memory_space=pl.ANY)


def struct(shape, dtype):
    return jax.ShapeDtypeStruct(shape, dtype)


def pack_kernel(pos_ref, k_ref, v_ref, out_ref):
    for s in range(2):
        rows = slice(s * SPAN, (s + 1) * SPAN)
        out_ref[s, 0:128, :] = k_ref[rows, :]
        out_ref[s, 128:256, :] = v_ref[rows, :].T
        span = (pos_ref[s * SPAN] // SPAN).astype(jnp.float32)
        out_ref[s, 256:PACK, :] = jnp.full((16, 128), span, jnp.float32).astype(jnp.bfloat16)


def query_tile(q_ref, chunk, s, quad):
    pieces = []
    for h in range(quad * QUAD, (quad + 1) * QUAD):
        for t in range(4):
            row = s * SPAN + t * 32 + chunk * PIECE
            pieces.append(q_ref[row:row + PIECE, h * HD:(h + 1) * HD])
    return jnp.concatenate(pieces, axis=0)


def softmax_step(scores, m_old, acc_old, vt):
    m_new = jnp.maximum(m_old, jnp.max(scores, axis=0, keepdims=True))
    keep = jnp.exp2((m_old - m_new) * LOG_SCALE)
    probs = jnp.exp2((scores - m_new) * LOG_SCALE).astype(jnp.bfloat16)
    return m_new, acc_old * keep + jnp.dot(vt, probs, preferred_element_type=jnp.float32)


def scores_of(kt, q):
    return lax.dot_general(kt, q, (((1,), (1,)), ((), ())), preferred_element_type=jnp.float32)


def load_keys(kv_ref, slots):
    kt = jnp.concatenate([kv_ref[i, 0:128, :] for i in slots], axis=0)
    vt = jnp.concatenate([kv_ref[i, 128:256, :] for i in slots], axis=1)
    ones = jnp.ones((16, vt.shape[1]), jnp.bfloat16)
    return kt, jnp.concatenate([vt, ones], axis=0)


def span_id(ref, i):
    return jnp.max(ref[i, 256:PACK, :].astype(jnp.float32)).astype(jnp.int32)


def visible_list(list_ref, ids, limit):
    count = jnp.int32(0)
    for i, span in enumerate(ids):
        list_ref[count] = jnp.int32(i)
        count = count + jnp.where(span < limit, 1, 0)
    return count


def walk(kv_ref, list_ref, count, queries, carry, update):
    def group(start, size, carry):
        kt, vt = load_keys(kv_ref, [list_ref[start + i] for i in range(size)])
        return update(kt, vt, carry)

    full = count // 4
    carry = lax.fori_loop(0, full, lambda g, c: group(g * 4, 4, c), carry)
    pair = (count // 2) % 2
    carry = lax.fori_loop(0, pair, lambda g, c: group(full * 4, 2, c), carry)
    single = count % 2
    return lax.fori_loop(0, single, lambda g, c: group(full * 4 + pair * 2, 1, c), carry)


def first_kernel(q_ref, own_ref, x1, x2, x3, y1, y2, y3, m_ref, acc_ref, kv_ref, list_ref):
    others = (x1, x2, x3, y1, y2, y3)
    kv_ref[0:2] = own_ref[...]
    for i, ref in enumerate(others):
        kv_ref[2 * i + 2:2 * i + 4] = ref[...]
    ids = [span_id(kv_ref, i) for i in range(14)]
    for s in range(2):
        units = [(chunk, quad) for chunk in range(2) for quad in range(2)]
        queries = [query_tile(q_ref, chunk, s, quad) for chunk, quad in units]
        kt, vt = load_keys(kv_ref, [s])
        ms = []
        for u, (chunk, quad) in enumerate(units):
            lane = lax.broadcasted_iota(jnp.int32, (SPAN, 256), 1) % 64
            row = (lane // PIECE) * 32 + lane % PIECE + chunk * PIECE
            scores = scores_of(kt, queries[u])
            scores = jnp.where(lax.broadcasted_iota(jnp.int32, (SPAN, 256), 0) <= row, scores, NEG)
            m_new = jnp.max(scores, axis=0, keepdims=True)
            probs = jnp.exp2((scores - m_new) * LOG_SCALE).astype(jnp.bfloat16)
            acc_ref[chunk, s * 2 + quad] = jnp.dot(vt, probs, preferred_element_type=jnp.float32)
            ms.append(m_new)

        def update(kt, vt, ms):
            all_scores = [scores_of(kt, q) for q in queries]
            out = []
            for u, (chunk, quad) in enumerate(units):
                unit = s * 2 + quad
                m_new, acc = softmax_step(all_scores[u], ms[u], acc_ref[chunk, unit], vt)
                acc_ref[chunk, unit] = acc
                out.append(m_new)
            return tuple(out)

        count = visible_list(list_ref, ids, ids[s])
        ms = walk(kv_ref, list_ref, count, queries, tuple(ms), update)
        for u, (chunk, quad) in enumerate(units):
            m_ref[chunk, s * 2 + quad] = jnp.broadcast_to(ms[u], (8, 256))


def second_kernel(chunk, place_ref, q_ref, own_ref, a1, a2, a3, b1, b2, b3, m_ref, acc_in, w_ref,
                  keep_ref, send_ref, kv_ref, list_ref, acc_ref, merged_ref, w_vmem, sems):
    cols = DOUT // NCOL
    copies = [
        pltpu.make_async_copy(
            w_ref.at[:, pl.ds(j * cols, cols)], w_vmem.at[j], sems.at[j]
        )
        for j in range(NCOL)
    ]
    for copy in copies:
        copy.start()
    for i, ref in enumerate((a1, a2, a3, b1, b2, b3)):
        kv_ref[3 * i:3 * i + 3] = ref[...]
    ids = [span_id(kv_ref, i) for i in range(18)]
    acc_ref[...] = acc_in[chunk]
    for s in range(2):
        queries = [query_tile(q_ref, chunk, s, quad) for quad in range(2)]

        def update(kt, vt, ms):
            all_scores = [scores_of(kt, q) for q in queries]
            out = []
            for quad in range(2):
                unit = s * 2 + quad
                m_new, acc = softmax_step(all_scores[quad], ms[quad], acc_ref[unit], vt)
                acc_ref[unit] = acc
                out.append(m_new)
            return tuple(out)

        count = visible_list(list_ref, ids, span_id(own_ref, s))
        ms = tuple(m_ref[chunk, s * 2 + quad, 0:1, :] for quad in range(2))
        walk(kv_ref, list_ref, count, queries, ms, update)
        for quad in range(2):
            acc = acc_ref[s * 2 + quad]
            o = acc[:128] * (1.0 / acc[128:129])
            for half in range(2):
                rows = o[:, half * 128:(half + 1) * 128].T.astype(jnp.bfloat16)
                for i in range(2):
                    h = quad * QUAD + half * 2 + i
                    for t in range(4):
                        where = pl.multiple_of(place_ref[s * 4 + t] * PIECE, PIECE)
                        at = i * 64 + t * PIECE
                        merged_ref[pl.ds(where, PIECE), h * HD:(h + 1) * HD] = rows[at:at + PIECE]
    for j in range(NCOL):
        copies[j].wait()
        part = jnp.dot(merged_ref[...], w_vmem[j], preferred_element_type=jnp.float32)
        part = part.astype(jnp.bfloat16)
        keep_ref[:, j * cols:(j + 1) * cols] = part[:64]
        send_ref[:, j * cols:(j + 1) * cols] = part[64:]


def pair_kernel(keep_ref, got_ref, *out_refs):
    total = keep_ref[...].astype(jnp.float32) + got_ref[...].astype(jnp.float32)
    for d in range(NZ):
        out_refs[d][...] = total[d * PIECE:(d + 1) * PIECE].astype(jnp.bfloat16)


def final_kernel(*refs):
    out_ref = refs[-1]
    for chunk in range(2):
        parts = [r[...].astype(jnp.float32) for r in refs[chunk * NZ:(chunk + 1) * NZ]]
        total = (parts[0] + parts[1]) + (parts[2] + parts[3])
        out_ref[chunk * PIECE:(chunk + 1) * PIECE, :] = total.astype(jnp.bfloat16)


def params(mib):
    return pltpu.CompilerParams(vmem_limit_bytes=mib << 20)


def estimate(flops, traffic):
    return pl.CostEstimate(flops=flops, bytes_accessed=traffic, transcendentals=0)


def ctx_route(dx, dy):
    return [
        (x * NX + y, ((x + dx) % NX) * NX + (y + dy) % NX)
        for x in range(NX) for y in range(NX)
    ]


def tp_route(dz, swap):
    return [
        (z * NCORE + c, ((z + dz) % NZ) * NCORE + (c ^ swap))
        for z in range(NZ) for c in range(NCORE)
    ]


def on_device(queries, keys, values, positions, out_weight):
    bf16, f32 = jnp.bfloat16, jnp.float32
    t = lax.axis_index("tp")
    z, core = t // NCORE, t % NCORE
    owners = jnp.arange(NZ * NCORE, dtype=jnp.int32)
    places = ((owners % NCORE) ^ core) * NZ + (owners // NCORE - z) % NZ

    own = pl.pallas_call(
        pack_kernel, in_specs=[SMEM, VMEM, VMEM], out_specs=VMEM,
        out_shape=struct((2, PACK, 128), bf16), name="pack",
    )(positions, keys, values)

    def shift(block, dx, dy):
        return lax.ppermute(block, "ctx", ctx_route(dx, dy))

    xs = [shift(own, d, 0) for d in (1, 3, 2)]
    ys = [shift(own, 0, d) for d in (1, 3, 2)]
    row = jnp.stack([b[0] for b in xs])
    col = jnp.stack([b[1] for b in ys])
    far = [shift(row, 0, d) for d in (1, 3, 2)] + [shift(col, d, 0) for d in (1, 3, 2)]

    maxima, acc = pl.pallas_call(
        first_kernel, in_specs=[VMEM] * 8, out_specs=[VMEM, VMEM],
        out_shape=[struct((2, 4, 8, 256), f32), struct((2, 4, 144, 256), f32)],
        scratch_shapes=[pltpu.VMEM((14, PACK, 128), bf16), pltpu.SMEM((32,), jnp.int32)],
        compiler_params=params(16), name="first",
        cost_estimate=estimate(4 * 10 ** 9, 1 << 20),
    )(queries, own, *xs, *ys)

    def chunk_sum(chunk):
        return pl.pallas_call(
            functools.partial(second_kernel, chunk),
            in_specs=[SMEM] + [VMEM] * 10 + [ANY],
            out_specs=[VMEM, VMEM],
            out_shape=[struct((64, DOUT), bf16), struct((64, DOUT), bf16)],
            scratch_shapes=[
                pltpu.VMEM((18, PACK, 128), bf16),
                pltpu.SMEM((32,), jnp.int32),
                pltpu.VMEM((4, 144, 256), f32),
                pltpu.VMEM((128, 1024), bf16),
                pltpu.VMEM((NCOL, 1024, DOUT // NCOL), bf16),
                pltpu.SemaphoreType.DMA((NCOL,)),
            ],
            compiler_params=params(36), name=f"second{chunk}",
            cost_estimate=estimate(6 * 10 ** 9, 16 << 20),
        )(places, queries, own, *far, maxima, acc, out_weight)

    def spread(keep, send):
        got = lax.ppermute(send, "tp", tp_route(0, 1))
        parts = pl.pallas_call(
            pair_kernel, in_specs=[VMEM, VMEM], out_specs=[VMEM] * NZ,
            out_shape=[struct((PIECE, DOUT), bf16)] * NZ, name="pair",
        )(keep, got)
        moved = [lax.ppermute(parts[d], "tp", tp_route(d, 0)) for d in (1, 3, 2)]
        return [parts[0]] + moved

    pieces = []
    for chunk in range(2):
        pieces += spread(*chunk_sum(chunk))
    return pl.pallas_call(
        final_kernel, in_specs=[VMEM] * (2 * NZ), out_specs=VMEM,
        out_shape=struct((2 * PIECE, DOUT), bf16), name="final",
    )(*pieces)


def solution(mesh):
    return jax.shard_map(
        on_device,
        mesh=mesh,
        in_specs=(P("ctx", "tp"), P("ctx", "tp"), P("ctx", "tp"), P("ctx"), P("tp", None)),
        out_specs=P(("ctx", "tp"), None),
        check_vma=False,
    )
```

```python
import functools
import math

import jax
import jax.numpy as jnp
from jax import lax
from jax.experimental import pallas as pl
from jax.experimental.pallas import tpu as pltpu
from jax.sharding import PartitionSpec as P


HD = 128
SPAN = 128
QUAD = 4
PACK = 272
LOG_SCALE = HD ** -0.5 * math.log2(math.e)
NEG = -1e30
NX = 4
NZ = 4
NCORE = 2
PIECE = 16
DOUT = 8192
NCOL = 8
GROUP = 4
HEADROOM = 60.0
NW = 4


VMEM = pl.BlockSpec(memory_space=pltpu.VMEM)
SMEM = pl.BlockSpec(memory_space=pltpu.SMEM)
HBM = pl.BlockSpec(memory_space=pltpu.HBM)


def struct(shape, dtype):
    return jax.ShapeDtypeStruct(shape, dtype)


def pack_kernel(pos_hbm, k_hbm, v_hbm, out_ref, pos_ref, k_ref, v_ref, sems):
    copies = [
        pltpu.make_async_copy(src, dst, sems.at[i])
        for i, (src, dst) in enumerate(((v_hbm, v_ref), (k_hbm, k_ref), (pos_hbm, pos_ref)))
    ]
    for copy in copies:
        copy.start()
    for copy in copies:
        copy.wait()
    for s in range(2):
        rows = slice(s * SPAN, (s + 1) * SPAN)
        out_ref[s, 0:128, :] = k_ref[rows, :]
        out_ref[s, 128:256, :] = v_ref[rows, :].T
        span = (pos_ref[s * SPAN] // SPAN).astype(jnp.float32)
        out_ref[s, 256:PACK, :] = jnp.full((16, 128), span, jnp.float32).astype(jnp.bfloat16)


def query_tile(q_ref, chunk, s, quad):
    pieces = []
    for h in range(quad * QUAD, (quad + 1) * QUAD):
        for t in range(4):
            row = s * SPAN + t * 32 + chunk * PIECE
            pieces.append(q_ref[row:row + PIECE, h * HD:(h + 1) * HD])
    return jnp.concatenate(pieces, axis=0)


def scores_of(kt, q):
    return lax.dot_general(kt, q, (((1,), (1,)), ((), ())), preferred_element_type=jnp.float32)


def weighted(vt, probs):
    return jnp.dot(vt, probs, preferred_element_type=jnp.float32)


def store_keys(kv_ref, blocks):
    for i, (ref, j) in enumerate(blocks):
        kv_ref[i, 0:256, :] = ref[j, 0:256, :]
        kv_ref[i, 256:PACK, :] = jnp.ones((16, 128), jnp.bfloat16)
    kv_ref[len(blocks)] = jnp.zeros((PACK, 128), jnp.bfloat16)


def span_id(ref, i):
    return jnp.max(ref[i, 256:PACK, :].astype(jnp.float32)).astype(jnp.int32)


def visible_list(list_ref, ids, limit):
    count = jnp.int32(0)
    for i, span in enumerate(ids):
        list_ref[count] = jnp.int32(i)
        count = count + jnp.where(span < limit, 1, 0)
    for i in range(GROUP):
        list_ref[count + i] = jnp.int32(len(ids))
    return count


def fast_walk(kv_ref, list_ref, count, queries, units, m_ref, peak_ref, acc_ref, probs):
    shifts = [m_ref[u][0:1, :] for u in units]

    def score(g, p_ref):
        slots = [list_ref[g * GROUP + i] for i in range(GROUP)]
        kt = jnp.concatenate([kv_ref[i, 0:128, :] for i in slots], axis=0)
        for n, u in enumerate(units):
            scores = scores_of(kt, queries[n])
            tiles = scores.reshape(GROUP * SPAN // 8, 8, 256)
            peak_ref[u] = jnp.maximum(peak_ref[u], jnp.max(tiles, axis=0))
            p_ref[n] = jnp.exp2((scores - shifts[n]) * LOG_SCALE).astype(jnp.bfloat16)

    def add(g, p_ref):
        slots = [list_ref[g * GROUP + i] for i in range(GROUP)]
        vt = jnp.concatenate([kv_ref[i, 128:PACK, :] for i in slots], axis=1)
        for n, u in enumerate(units):
            acc_ref[u] = acc_ref[u] + weighted(vt, p_ref[n])

    even, odd = probs
    groups = jnp.maximum((count + GROUP - 1) // GROUP, 1)
    score(0, even)

    def pair(i, carry):
        score(2 * i + 1, odd)
        add(2 * i, even)
        score(2 * i + 2, even)
        add(2 * i + 1, odd)
        return carry

    lax.fori_loop(0, (groups - 1) // 2, pair, 0)

    @pl.when(groups % 2 == 1)
    def _():
        add(groups - 1, even)

    @pl.when(groups % 2 == 0)
    def _():
        score(groups - 1, odd)
        add(groups - 2, even)
        add(groups - 1, odd)


def slow_walk(kv_ref, list_ref, count, queries, units, m_ref, acc_ref):
    def step(i, carry):
        slot = list_ref[i]
        for n, u in enumerate(units):
            scores = scores_of(kv_ref[slot, 0:128, :], queries[n])
            m_old = m_ref[u][0:1, :]
            m_new = jnp.maximum(m_old, jnp.max(scores, axis=0, keepdims=True))
            probs = jnp.exp2((scores - m_new) * LOG_SCALE).astype(jnp.bfloat16)
            scale = jnp.exp2((m_old - m_new) * LOG_SCALE)
            acc_ref[u] = acc_ref[u] * scale + weighted(kv_ref[slot, 128:PACK, :], probs)
            m_ref[u] = jnp.broadcast_to(m_new, (8, 256))
        return carry

    lax.fori_loop(0, count, step, 0)


def overshoot(peak_ref, m_ref, units):
    worst = peak_ref[units[0]] - m_ref[units[0]]
    for u in units[1:]:
        worst = jnp.maximum(worst, peak_ref[u] - m_ref[u])
    return jnp.max(worst) * LOG_SCALE > HEADROOM


def first_kernel(q_hbm, w_hbm, own_ref, x1, x2, x3, y1, y2, y3, m_ref, acc_ref, tile_ref, w_ref,
                 q_ref, kv_ref, peak_ref, even_ref, odd_ref, list0, list1, sems):
    fetch_q = pltpu.make_async_copy(q_hbm, q_ref, sems.at[NW])
    fetch_q.start()
    fetch_w = []
    for j in range(NW):
        rows = pl.ds(j * (1024 // NW), 1024 // NW)
        fetch_w.append(pltpu.make_async_copy(w_hbm.at[rows], w_ref.at[rows], sems.at[j]))
        fetch_w[j].start()
    blocks = [(ref, j) for ref in (own_ref, x1, x2, x3, y1, y2, y3) for j in range(2)]
    store_keys(kv_ref, blocks)
    ids = [span_id(ref, j) for ref, j in blocks]
    counts = [visible_list(ref, ids, ids[s]) for s, ref in enumerate((list0, list1))]
    lists = (list0, list1)
    fetch_q.wait()
    for chunk in range(2):
        for s in range(2):
            for quad in range(2):
                tile_ref[chunk * 4 + s * 2 + quad] = query_tile(q_ref, chunk, s, quad)
    units = [[chunk * 4 + s * 2 + quad for chunk in range(2) for quad in range(2)] for s in range(2)]
    queries = [[tile_ref[u] for u in units[s]] for s in range(2)]

    def own_block():
        for s in range(2):
            for n, u in enumerate(units[s]):
                lane = lax.broadcasted_iota(jnp.int32, (SPAN, 256), 1) % 64
                row = (lane // PIECE) * 32 + lane % PIECE + (n // 2) * PIECE
                scores = scores_of(kv_ref[s, 0:128, :], queries[s][n])
                key = lax.broadcasted_iota(jnp.int32, (SPAN, 256), 0)
                scores = jnp.where(key <= row, scores, NEG)
                m_new = jnp.max(scores, axis=0, keepdims=True)
                probs = jnp.exp2((scores - m_new) * LOG_SCALE).astype(jnp.bfloat16)
                acc_ref[u] = weighted(kv_ref[s, 128:PACK, :], probs)
                m_ref[u] = jnp.broadcast_to(m_new, (8, 256))

    own_block()
    peak_ref[...] = m_ref[...]
    for s in range(2):
        fast_walk(kv_ref, lists[s], counts[s], queries[s], units[s], m_ref, peak_ref, acc_ref,
                  (even_ref, odd_ref))

    @pl.when(overshoot(peak_ref, m_ref, units[0] + units[1]))
    def _():
        own_block()
        for s in range(2):
            slow_walk(kv_ref, lists[s], counts[s], queries[s], units[s], m_ref, acc_ref)

    for copy in fetch_w:
        copy.wait()


def rest_of_attention(chunk, spans, tile_ref, own_ref, far, m_in, acc_in, kv_ref, m_ref, peak_ref,
                      acc_ref, even_ref, odd_ref, lists):
    blocks = [(ref, j) for ref in far for j in range(3)]
    store_keys(kv_ref, blocks)
    ids = [span_id(ref, j) for ref, j in blocks]
    counts = [visible_list(lists[n], ids, span_id(own_ref, s)) for n, s in enumerate(spans)]
    queries = [[tile_ref[chunk * 4 + s * 2 + quad] for quad in range(2)] for s in spans]
    units = [(2 * n, 2 * n + 1) for n in range(len(spans))]

    def reset():
        for n, s in enumerate(spans):
            for quad in range(2):
                m_ref[2 * n + quad] = m_in[chunk * 4 + s * 2 + quad]
                acc_ref[2 * n + quad] = acc_in[chunk * 4 + s * 2 + quad]

    reset()
    peak_ref[...] = m_ref[...]
    for n in range(len(spans)):
        fast_walk(kv_ref, lists[n], counts[n], queries[n], units[n], m_ref, peak_ref, acc_ref,
                  (even_ref, odd_ref))

    @pl.when(overshoot(peak_ref, m_ref, range(2 * len(spans))))
    def _():
        reset()
        for n in range(len(spans)):
            slow_walk(kv_ref, lists[n], counts[n], queries[n], units[n], m_ref, acc_ref)


def finish(s, acc_ref, base, place_ref, merged_ref):
    for quad in range(2):
        acc = acc_ref[base + quad]
        o = acc[:128] * (1.0 / acc[128:129])
        for half in range(2):
            rows = o[:, half * 128:(half + 1) * 128].T.astype(jnp.bfloat16)
            for i in range(2):
                h = quad * QUAD + half * 2 + i
                for t in range(4):
                    where = pl.multiple_of(place_ref[s * 4 + t] * PIECE, PIECE)
                    at = i * 64 + t * PIECE
                    merged_ref[pl.ds(where, PIECE), h * HD:(h + 1) * HD] = rows[at:at + PIECE]


def project(merged_ref, w_ref, keep_ref, send_ref):
    cols = DOUT // NCOL
    for j in range(NCOL):
        at = slice(j * cols, (j + 1) * cols)
        part = jnp.dot(merged_ref[...], w_ref[:, at], preferred_element_type=jnp.float32)
        part = part.astype(jnp.bfloat16)
        keep_ref[:, at] = part[:64]
        send_ref[:, at] = part[64:]


def middle_kernel(chunk, spans, tile_ref, own_ref, a1, a2, a3, b1, b2, b3, m_in, acc_in, acc_ref,
                  kv_ref, m_ref, peak_ref, even_ref, odd_ref, list0, list1):
    rest_of_attention(chunk, spans, tile_ref, own_ref, (a1, a2, a3, b1, b2, b3), m_in, acc_in, kv_ref,
                      m_ref, peak_ref, acc_ref, even_ref, odd_ref, (list0, list1))


def last_kernel(chunk, spans, done, place_ref, tile_ref, own_ref, a1, a2, a3, b1, b2, b3, m_in, acc_in,
                w_ref, *refs):
    acc_done = refs[0] if done else None
    (keep_ref, send_ref, acc_ref, merged_ref, kv_ref, m_ref, peak_ref, even_ref, odd_ref,
     list0, list1) = refs[-11:]
    rest_of_attention(chunk, spans, tile_ref, own_ref, (a1, a2, a3, b1, b2, b3), m_in, acc_in, kv_ref,
                      m_ref, peak_ref, acc_ref, even_ref, odd_ref, (list0, list1))
    for n, s in enumerate(spans):
        finish(s, acc_ref, 2 * n, place_ref, merged_ref)
    for n, s in enumerate(done):
        finish(s, acc_done, 2 * n, place_ref, merged_ref)
    project(merged_ref, w_ref, keep_ref, send_ref)


def pair_kernel(keep_ref, got_ref, *out_refs):
    total = keep_ref[...].astype(jnp.float32) + got_ref[...].astype(jnp.float32)
    for d in range(NZ):
        out_refs[d][...] = total[d * PIECE:(d + 1) * PIECE].astype(jnp.bfloat16)


def final_kernel(*refs):
    out_ref = refs[-1]
    for chunk in range(2):
        parts = [r[...].astype(jnp.float32) for r in refs[chunk * NZ:(chunk + 1) * NZ]]
        total = (parts[0] + parts[1]) + (parts[2] + parts[3])
        out_ref[chunk * PIECE:(chunk + 1) * PIECE, :] = total.astype(jnp.bfloat16)


def in_hbm(array):
    return pltpu.with_memory_space_constraint(array, pltpu.HBM)


def params(mib):
    return pltpu.CompilerParams(vmem_limit_bytes=mib << 20)


def estimate(flops, traffic):
    return pl.CostEstimate(flops=flops, bytes_accessed=traffic, transcendentals=0)


def ctx_route(dx, dy):
    return [
        (x * NX + y, ((x + dx) % NX) * NX + (y + dy) % NX)
        for x in range(NX) for y in range(NX)
    ]


def tp_route(dz, swap):
    return [
        (z * NCORE + c, ((z + dz) % NZ) * NCORE + (c ^ swap))
        for z in range(NZ) for c in range(NCORE)
    ]


def on_device(queries, keys, values, positions, out_weight):
    bf16, f32 = jnp.bfloat16, jnp.float32
    t = lax.axis_index("tp")
    z, core = t // NCORE, t % NCORE
    owners = jnp.arange(NZ * NCORE, dtype=jnp.int32)
    places = ((owners % NCORE) ^ core) * NZ + (owners // NCORE - z) % NZ

    own = pl.pallas_call(
        pack_kernel, in_specs=[HBM] * 3, out_specs=VMEM,
        out_shape=struct((2, PACK, 128), bf16), name="pack", compiler_params=params(2),
        scratch_shapes=[
            pltpu.SMEM((2 * SPAN,), jnp.int32), pltpu.VMEM((2 * SPAN, HD), bf16),
            pltpu.VMEM((2 * SPAN, HD), bf16), pltpu.SemaphoreType.DMA((3,)),
        ],
    )(in_hbm(positions), in_hbm(keys), in_hbm(values))

    def shift(block, dx, dy):
        return lax.ppermute(block, "ctx", ctx_route(dx, dy))

    xs = [shift(own, d, 0) for d in (1, 3, 2)]
    ys = [shift(own, 0, d) for d in (1, 3, 2)]
    row = jnp.stack([b[0] for b in xs])
    col = jnp.stack([b[1] for b in ys])
    far = [shift(row, 0, d) for d in (1, 3, 2)] + [shift(col, d, 0) for d in (1, 3, 2)]

    def walk_scratch(slots, units, width):
        return [
            pltpu.VMEM((slots + 1, PACK, 128), bf16),
            pltpu.VMEM((units, 8, 256), f32),
            pltpu.VMEM((units, 8, 256), f32),
            pltpu.VMEM((width, GROUP * SPAN, 256), bf16),
            pltpu.VMEM((width, GROUP * SPAN, 256), bf16),
            pltpu.SMEM((32,), jnp.int32),
            pltpu.SMEM((32,), jnp.int32),
        ]

    scratch = walk_scratch(14, 8, 4)
    maxima, acc, tiles, weight = pl.pallas_call(
        first_kernel, in_specs=[HBM] * 2 + [VMEM] * 7, out_specs=[VMEM] * 4,
        out_shape=[
            struct((8, 8, 256), f32), struct((8, 144, 256), f32),
            struct((8, 256, 128), bf16), struct((1024, DOUT), bf16),
        ],
        scratch_shapes=[pltpu.VMEM((256, 1024), bf16)] + scratch[:1] + scratch[2:]
        + [pltpu.SemaphoreType.DMA((NW + 1,))],
        compiler_params=params(14), name="first",
        cost_estimate=estimate(4 * 10 ** 9, 1 << 20),
    )(in_hbm(queries), in_hbm(out_weight), own, *xs, *ys)

    def middle(chunk, spans, acc):
        n = 2 * len(spans)
        return pl.pallas_call(
            functools.partial(middle_kernel, chunk, spans),
            in_specs=[VMEM] * 10, out_specs=VMEM, out_shape=struct((n, 144, 256), f32),
            scratch_shapes=walk_scratch(18, n, 2),
            compiler_params=params(14), name="middle",
            cost_estimate=estimate(2 * 10 ** 9, 1 << 20),
        )(tiles, own, *far, maxima, acc)

    def last(chunk, spans, acc, done=(), acc_done=()):
        n = 2 * len(spans)
        return pl.pallas_call(
            functools.partial(last_kernel, chunk, spans, done),
            in_specs=[SMEM] + [VMEM] * (11 + len(acc_done)),
            out_specs=[VMEM, VMEM],
            out_shape=[struct((64, DOUT), bf16), struct((64, DOUT), bf16)],
            scratch_shapes=[
                pltpu.VMEM((n, 144, 256), f32), pltpu.VMEM((128, 1024), bf16),
            ] + walk_scratch(18, n, 2),
            compiler_params=params(14),
            cost_estimate=estimate(5 * 10 ** 9, 1 << 20),
        )(places, tiles, own, *far, maxima, acc, weight, *acc_done)

    def pair_sum(keep, got):
        return pl.pallas_call(
            pair_kernel, in_specs=[VMEM, VMEM], out_specs=[VMEM] * NZ,
            out_shape=[struct((PIECE, DOUT), bf16)] * NZ, name="pair",
            compiler_params=params(6),
        )(keep, got)

    def swap(block):
        return lax.ppermute(block, "tp", tp_route(0, 1))

    def exchange(parts):
        return [parts[0]] + [lax.ppermute(parts[d], "tp", tp_route(d, 0)) for d in (1, 3, 2)]

    keep0, send0 = last(0, (0, 1), acc)
    send0, acc1 = lax.optimization_barrier((send0, acc))
    got0 = swap(send0)
    acc_mid = middle(1, (0,), acc1)
    keep0, acc_mid = lax.optimization_barrier((keep0, acc_mid))
    parts0 = pair_sum(keep0, got0)
    *parts0, acc2 = lax.optimization_barrier((*parts0, acc))
    pieces0 = exchange(parts0)
    keep1, send1 = last(1, (1,), acc2, (0,), (acc_mid,))
    pieces1 = exchange(pair_sum(keep1, swap(send1)))
    return pl.pallas_call(
        final_kernel, in_specs=[VMEM] * (2 * NZ), out_specs=VMEM,
        out_shape=struct((2 * PIECE, DOUT), bf16), name="final", compiler_params=params(6),
    )(*pieces0, *pieces1)


def solution(mesh):
    return jax.shard_map(
        on_device,
        mesh=mesh,
        in_specs=(P("ctx", "tp"), P("ctx", "tp"), P("ctx", "tp"), P("ctx"), P("tp", None)),
        out_specs=P(("ctx", "tp"), None),
        check_vma=False,
    )
```

```python
import functools
import math

import jax
import jax.numpy as jnp
from jax import lax
from jax.experimental import pallas as pl
from jax.experimental.pallas import tpu as pltpu
from jax.sharding import PartitionSpec as P


HD = 128
SPAN = 128
QUAD = 4
PACK = 272
LOG_SCALE = HD ** -0.5 * math.log2(math.e)
NEG = -1e30
NX = 4
NZ = 4
NCORE = 2
PIECE = 16
DOUT = 8192
NCOL = 8
GROUP = 4
HEADROOM = 60.0
NW = 4


VMEM = pl.BlockSpec(memory_space=pltpu.VMEM)
SMEM = pl.BlockSpec(memory_space=pltpu.SMEM)
HBM = pl.BlockSpec(memory_space=pltpu.HBM)


def struct(shape, dtype):
    return jax.ShapeDtypeStruct(shape, dtype)


def pack_kernel(index_ref, pos_hbm, k_hbm, v_hbm, out_ref, mine_ref, give_ref, pos_ref, k_ref, v_ref,
                sems):
    core = index_ref[0] % NCORE

    copies = [
        pltpu.make_async_copy(src, dst, sems.at[i])
        for i, (src, dst) in enumerate(((v_hbm, v_ref), (k_hbm, k_ref), (pos_hbm, pos_ref)))
    ]
    for copy in copies:
        copy.start()
    for copy in copies:
        copy.wait()
    for s in range(2):
        rows = slice(s * SPAN, (s + 1) * SPAN)
        span = (pos_ref[s * SPAN] // SPAN).astype(jnp.float32)
        ids = jnp.full((16, 128), span, jnp.float32).astype(jnp.bfloat16)
        vt = v_ref[rows, :].T
        for ref, i in ((out_ref, s), (mine_ref, core ^ s), (give_ref, 1 - (core ^ s))):
            base = pl.multiple_of(i * PACK, 16)
            ref[pl.ds(base, 128), :] = k_ref[rows, :]
            ref[pl.ds(base + 128, 128), :] = vt
            ref[pl.ds(base + 256, 16), :] = ids


def query_tile(q_ref, chunk, s, quad):
    pieces = []
    for h in range(quad * QUAD, (quad + 1) * QUAD):
        for t in range(4):
            row = s * SPAN + t * 32 + chunk * PIECE
            pieces.append(q_ref[row:row + PIECE, h * HD:(h + 1) * HD])
    return jnp.concatenate(pieces, axis=0)


def scores_of(kt, q):
    return lax.dot_general(kt, q, (((1,), (1,)), ((), ())), preferred_element_type=jnp.float32)


def weighted(vt, probs):
    return jnp.dot(vt, probs, preferred_element_type=jnp.float32)


def store_keys(kv_ref, blocks):
    for i, (ref, j) in enumerate(blocks):
        kv_ref[i, 0:256, :] = ref[j * PACK:j * PACK + 256, :]
        kv_ref[i, 256:PACK, :] = jnp.ones((16, 128), jnp.bfloat16)
    kv_ref[len(blocks)] = jnp.zeros((PACK, 128), jnp.bfloat16)


def span_id(ref, i):
    ids = ref[i * PACK + 256:(i + 1) * PACK, :].astype(jnp.float32)
    return jnp.max(ids).astype(jnp.int32)


def visible_list(list_ref, ids, limit):
    count = jnp.int32(0)
    for i, span in enumerate(ids):
        list_ref[count] = jnp.int32(i)
        count = count + jnp.where(span < limit, 1, 0)
    for i in range(GROUP):
        list_ref[count + i] = jnp.int32(len(ids))
    return count


def fast_walk(kv_ref, list_ref, count, queries, units, m_ref, peak_ref, acc_ref, probs):
    shifts = [m_ref[u][0:1, :] for u in units]

    def score(g, p_ref):
        slots = [list_ref[g * GROUP + i] for i in range(GROUP)]
        kt = jnp.concatenate([kv_ref[i, 0:128, :] for i in slots], axis=0)
        for n, u in enumerate(units):
            scores = scores_of(kt, queries[n])
            tiles = scores.reshape(GROUP * SPAN // 8, 8, 256)
            peak_ref[u] = jnp.maximum(peak_ref[u], jnp.max(tiles, axis=0))
            p_ref[n] = jnp.exp2((scores - shifts[n]) * LOG_SCALE).astype(jnp.bfloat16)

    def add(g, p_ref):
        slots = [list_ref[g * GROUP + i] for i in range(GROUP)]
        vt = jnp.concatenate([kv_ref[i, 128:PACK, :] for i in slots], axis=1)
        for n, u in enumerate(units):
            acc_ref[u] = acc_ref[u] + weighted(vt, p_ref[n])

    even, odd = probs
    groups = jnp.maximum((count + GROUP - 1) // GROUP, 1)
    score(0, even)

    def pair(i, carry):
        score(2 * i + 1, odd)
        add(2 * i, even)
        score(2 * i + 2, even)
        add(2 * i + 1, odd)
        return carry

    lax.fori_loop(0, (groups - 1) // 2, pair, 0)

    @pl.when(groups % 2 == 1)
    def _():
        add(groups - 1, even)

    @pl.when(groups % 2 == 0)
    def _():
        score(groups - 1, odd)
        add(groups - 2, even)
        add(groups - 1, odd)


def slow_walk(kv_ref, list_ref, count, queries, units, m_ref, acc_ref):
    def step(i, carry):
        slot = list_ref[i]
        for n, u in enumerate(units):
            scores = scores_of(kv_ref[slot, 0:128, :], queries[n])
            m_old = m_ref[u][0:1, :]
            m_new = jnp.maximum(m_old, jnp.max(scores, axis=0, keepdims=True))
            probs = jnp.exp2((scores - m_new) * LOG_SCALE).astype(jnp.bfloat16)
            scale = jnp.exp2((m_old - m_new) * LOG_SCALE)
            acc_ref[u] = acc_ref[u] * scale + weighted(kv_ref[slot, 128:PACK, :], probs)
            m_ref[u] = jnp.broadcast_to(m_new, (8, 256))
        return carry

    lax.fori_loop(0, count, step, 0)


def overshoot(peak_ref, m_ref, units):
    worst = peak_ref[units[0]] - m_ref[units[0]]
    for u in units[1:]:
        worst = jnp.maximum(worst, peak_ref[u] - m_ref[u])
    return jnp.max(worst) * LOG_SCALE > HEADROOM


def first_kernel(q_hbm, w_hbm, own_ref, n1, n2, n3, other, m_ref, acc_ref, tile_ref, w_ref,
                 q_ref, kv_ref, peak_ref, even_ref, odd_ref, list0, list1, sems):
    fetch_q = pltpu.make_async_copy(q_hbm, q_ref, sems.at[NW])
    fetch_q.start()
    fetch_w = []
    for j in range(NW):
        rows = pl.ds(j * (1024 // NW), 1024 // NW)
        fetch_w.append(pltpu.make_async_copy(w_hbm.at[rows], w_ref.at[rows], sems.at[j]))
        fetch_w[j].start()
    blocks = [(own_ref, j) for j in range(2)]
    blocks += [(ref, j) for ref in (n1, n2, n3) for j in (0, 2)]
    blocks += [(other, j) for j in range(6)]
    store_keys(kv_ref, blocks)
    ids = [span_id(ref, j) for ref, j in blocks]
    counts = [visible_list(ref, ids, ids[s]) for s, ref in enumerate((list0, list1))]
    lists = (list0, list1)
    fetch_q.wait()
    for chunk in range(2):
        for s in range(2):
            for quad in range(2):
                tile_ref[chunk * 4 + s * 2 + quad] = query_tile(q_ref, chunk, s, quad)
    units = [[chunk * 4 + s * 2 + quad for chunk in range(2) for quad in range(2)] for s in range(2)]
    queries = [[tile_ref[u] for u in units[s]] for s in range(2)]

    def own_block():
        for s in range(2):
            for n, u in enumerate(units[s]):
                lane = lax.broadcasted_iota(jnp.int32, (SPAN, 256), 1) % 64
                row = (lane // PIECE) * 32 + lane % PIECE + (n // 2) * PIECE
                scores = scores_of(kv_ref[s, 0:128, :], queries[s][n])
                key = lax.broadcasted_iota(jnp.int32, (SPAN, 256), 0)
                scores = jnp.where(key <= row, scores, NEG)
                m_new = jnp.max(scores, axis=0, keepdims=True)
                probs = jnp.exp2((scores - m_new) * LOG_SCALE).astype(jnp.bfloat16)
                acc_ref[u] = weighted(kv_ref[s, 128:PACK, :], probs)
                m_ref[u] = jnp.broadcast_to(m_new, (8, 256))

    own_block()
    peak_ref[...] = m_ref[...]
    for s in range(2):
        fast_walk(kv_ref, lists[s], counts[s], queries[s], units[s], m_ref, peak_ref, acc_ref,
                  (even_ref, odd_ref))

    @pl.when(overshoot(peak_ref, m_ref, units[0] + units[1]))
    def _():
        own_block()
        for s in range(2):
            slow_walk(kv_ref, lists[s], counts[s], queries[s], units[s], m_ref, acc_ref)

    for copy in fetch_w:
        copy.wait()


def rest_of_attention(chunk, spans, tile_ref, own_ref, far, m_in, acc_in, kv_ref, m_ref, peak_ref,
                      acc_ref, even_ref, odd_ref, lists):
    blocks = [(ref, j) for ref in far for j in range(3)]
    store_keys(kv_ref, blocks)
    ids = [span_id(ref, j) for ref, j in blocks]
    counts = [visible_list(lists[n], ids, span_id(own_ref, s)) for n, s in enumerate(spans)]
    queries = [[tile_ref[chunk * 4 + s * 2 + quad] for quad in range(2)] for s in spans]
    units = [(2 * n, 2 * n + 1) for n in range(len(spans))]

    def reset():
        for n, s in enumerate(spans):
            for quad in range(2):
                m_ref[2 * n + quad] = m_in[chunk * 4 + s * 2 + quad]
                acc_ref[2 * n + quad] = acc_in[chunk * 4 + s * 2 + quad]

    reset()
    peak_ref[...] = m_ref[...]
    for n in range(len(spans)):
        fast_walk(kv_ref, lists[n], counts[n], queries[n], units[n], m_ref, peak_ref, acc_ref,
                  (even_ref, odd_ref))

    @pl.when(overshoot(peak_ref, m_ref, range(2 * len(spans))))
    def _():
        reset()
        for n in range(len(spans)):
            slow_walk(kv_ref, lists[n], counts[n], queries[n], units[n], m_ref, acc_ref)


def finish(s, acc_ref, base, index_ref, merged_ref):
    z, core = index_ref[0] // NCORE, index_ref[0] % NCORE
    for quad in range(2):
        acc = acc_ref[base + quad]
        o = acc[:128] * (1.0 / acc[128:129])
        for half in range(2):
            rows = o[:, half * 128:(half + 1) * 128].T.astype(jnp.bfloat16)
            for i in range(2):
                h = quad * QUAD + half * 2 + i
                for t in range(4):
                    owner = s * 4 + t
                    place = ((owner % NCORE) ^ core) * NZ + (owner // NCORE - z + NZ) % NZ
                    where = pl.multiple_of(place * PIECE, PIECE)
                    at = i * 64 + t * PIECE
                    merged_ref[pl.ds(where, PIECE), h * HD:(h + 1) * HD] = rows[at:at + PIECE]


def project(merged_ref, w_ref, keep_ref, send_ref):
    cols = DOUT // NCOL
    for j in range(NCOL):
        at = slice(j * cols, (j + 1) * cols)
        part = jnp.dot(merged_ref[...], w_ref[:, at], preferred_element_type=jnp.float32)
        part = part.astype(jnp.bfloat16)
        keep_ref[:, at] = part[:64]
        send_ref[:, at] = part[64:]


def middle_kernel(chunk, spans, tile_ref, own_ref, f1, f2, f3, g1, g2, g3, m_in, acc_in, acc_ref,
                  kv_ref, m_ref, peak_ref, even_ref, odd_ref, list0, list1):
    rest_of_attention(chunk, spans, tile_ref, own_ref, (f1, f2, f3, g1, g2, g3), m_in, acc_in, kv_ref,
                      m_ref, peak_ref, acc_ref, even_ref, odd_ref, (list0, list1))


def last_kernel(chunk, spans, done, index_ref, tile_ref, own_ref, f1, f2, f3, g1, g2, g3, m_in, acc_in,
                w_ref, *refs):
    acc_done = refs[0] if done else None
    (keep_ref, send_ref, acc_ref, merged_ref, kv_ref, m_ref, peak_ref, even_ref, odd_ref,
     list0, list1) = refs[-11:]
    rest_of_attention(chunk, spans, tile_ref, own_ref, (f1, f2, f3, g1, g2, g3), m_in, acc_in, kv_ref,
                      m_ref, peak_ref, acc_ref, even_ref, odd_ref, (list0, list1))
    for n, s in enumerate(spans):
        finish(s, acc_ref, 2 * n, index_ref, merged_ref)
    for n, s in enumerate(done):
        finish(s, acc_done, 2 * n, index_ref, merged_ref)
    project(merged_ref, w_ref, keep_ref, send_ref)


def pair_kernel(keep_ref, got_ref, *out_refs):
    total = keep_ref[...].astype(jnp.float32) + got_ref[...].astype(jnp.float32)
    for d in range(NZ):
        out_refs[d][...] = total[d * PIECE:(d + 1) * PIECE].astype(jnp.bfloat16)


def final_kernel(*refs):
    out_ref = refs[-1]
    for chunk in range(2):
        parts = [r[...].astype(jnp.float32) for r in refs[chunk * NZ:(chunk + 1) * NZ]]
        total = (parts[0] + parts[1]) + (parts[2] + parts[3])
        out_ref[chunk * PIECE:(chunk + 1) * PIECE, :] = total.astype(jnp.bfloat16)


def assemble(arrays, plans):
    def kernel(*refs):
        for out_ref, plan in zip(refs[len(arrays):], plans):
            for at, (n, i) in enumerate(plan):
                out_ref[at * PACK:(at + 1) * PACK] = refs[n][i * PACK:(i + 1) * PACK]

    return pl.pallas_call(
        kernel, in_specs=[VMEM] * len(arrays), out_specs=[VMEM] * len(plans),
        out_shape=[struct((len(plan) * PACK, HD), jnp.bfloat16) for plan in plans],
        compiler_params=params(2), name="assemble",
    )(*arrays)


def in_hbm(array):
    return pltpu.with_memory_space_constraint(array, pltpu.HBM)


def params(mib):
    return pltpu.CompilerParams(vmem_limit_bytes=mib << 20)


def estimate(flops, traffic):
    return pl.CostEstimate(flops=flops, bytes_accessed=traffic, transcendentals=0)


def gather_route(distance, phase):
    route = []
    for x in range(NX):
        for y in range(NX):
            for t in range(NZ * NCORE):
                along_x = t % NCORE == phase
                x_to = (x + distance) % NX if along_x else x
                y_to = y if along_x else (y + distance) % NX
                route.append(((x * NX + y) * 8 + t, (x_to * NX + y_to) * 8 + t))
    return route


def tp_route(dz, swap):
    return [
        (z * NCORE + c, ((z + dz) % NZ) * NCORE + (c ^ swap))
        for z in range(NZ) for c in range(NCORE)
    ]


def on_device(queries, keys, values, positions, out_weight):
    bf16, f32 = jnp.bfloat16, jnp.float32
    index = lax.axis_index("tp").reshape(1)

    own, mine, give = pl.pallas_call(
        pack_kernel, in_specs=[SMEM] + [HBM] * 3, out_specs=[VMEM] * 3,
        out_shape=[struct((2 * PACK, HD), bf16)] * 3, name="pack", compiler_params=params(4),
        scratch_shapes=[
            pltpu.SMEM((2 * SPAN,), jnp.int32), pltpu.VMEM((2 * SPAN, HD), bf16),
            pltpu.VMEM((2 * SPAN, HD), bf16), pltpu.SemaphoreType.DMA((3,)),
        ],
    )(index, in_hbm(positions), in_hbm(keys), in_hbm(values))

    def swap(block):
        return lax.ppermute(block, "tp", tp_route(0, 1))

    def shift(block, distance, phase):
        return lax.ppermute(block, ("ctx", "tp"), gather_route(distance, phase))

    got = swap(give)
    both, = assemble([mine, got], [[(0, 0), (1, 0), (0, 1), (1, 1)]])
    near = [shift(both, d, 0) for d in (1, 3, 2)]
    ahead, mate = assemble(near, [
        [(n, i) for i in (0, 1) for n in range(3)],
        [(n, i) for n in range(3) for i in (1, 3)],
    ])
    far = [shift(ahead, d, 1) for d in (1, 3, 2)]
    near_other = swap(mate)
    far_other = [swap(assemble([b], [[(0, 3), (0, 4), (0, 5)]])[0]) for b in far]

    def walk_scratch(slots, units, width):
        return [
            pltpu.VMEM((slots + 1, PACK, 128), bf16),
            pltpu.VMEM((units, 8, 256), f32),
            pltpu.VMEM((units, 8, 256), f32),
            pltpu.VMEM((width, GROUP * SPAN, 256), bf16),
            pltpu.VMEM((width, GROUP * SPAN, 256), bf16),
            pltpu.SMEM((32,), jnp.int32),
            pltpu.SMEM((32,), jnp.int32),
        ]

    scratch = walk_scratch(14, 8, 4)
    first = pl.pallas_call(
        first_kernel, in_specs=[HBM] * 2 + [VMEM] * 5, out_specs=[VMEM] * 4,
        out_shape=[
            struct((8, 8, 256), f32), struct((8, 144, 256), f32),
            struct((8, 256, 128), bf16), struct((1024, DOUT), bf16),
        ],
        scratch_shapes=[pltpu.VMEM((256, 1024), bf16)] + scratch[:1] + scratch[2:]
        + [pltpu.SemaphoreType.DMA((NW + 1,))],
        compiler_params=params(14), name="first",
        cost_estimate=estimate(4 * 10 ** 9, 1 << 20),
    )
    maxima, acc, tiles, weight = first(in_hbm(queries), in_hbm(out_weight), own, *near, near_other)

    def middle(chunk, spans, acc):
        n = 2 * len(spans)
        return pl.pallas_call(
            functools.partial(middle_kernel, chunk, spans),
            in_specs=[VMEM] * 10, out_specs=VMEM, out_shape=struct((n, 144, 256), f32),
            scratch_shapes=walk_scratch(18, n, 2),
            compiler_params=params(14), name="middle",
            cost_estimate=estimate(2 * 10 ** 9, 1 << 20),
        )(tiles, own, *far, *far_other, maxima, acc)

    def last(chunk, spans, acc, done=(), acc_done=()):
        n = 2 * len(spans)
        return pl.pallas_call(
            functools.partial(last_kernel, chunk, spans, done),
            in_specs=[SMEM] + [VMEM] * (11 + len(acc_done)),
            out_specs=[VMEM, VMEM],
            out_shape=[struct((64, DOUT), bf16), struct((64, DOUT), bf16)],
            scratch_shapes=[
                pltpu.VMEM((n, 144, 256), f32), pltpu.VMEM((128, 1024), bf16),
            ] + walk_scratch(18, n, 2),
            compiler_params=params(14),
            cost_estimate=estimate(5 * 10 ** 9, 1 << 20),
        )(index, tiles, own, *far, *far_other, maxima, acc, weight, *acc_done)

    def pair_sum(keep, got):
        return pl.pallas_call(
            pair_kernel, in_specs=[VMEM, VMEM], out_specs=[VMEM] * NZ,
            out_shape=[struct((PIECE, DOUT), bf16)] * NZ, name="pair",
            compiler_params=params(6),
        )(keep, got)

    def exchange(parts):
        return [parts[0]] + [lax.ppermute(parts[d], "tp", tp_route(d, 0)) for d in (1, 3, 2)]

    keep0, send0 = last(0, (0, 1), acc)
    send0, acc1 = lax.optimization_barrier((send0, acc))
    got0 = swap(send0)
    acc_mid = middle(1, (0,), acc1)
    keep0, acc_mid = lax.optimization_barrier((keep0, acc_mid))
    parts0 = pair_sum(keep0, got0)
    *parts0, acc2 = lax.optimization_barrier((*parts0, acc))
    pieces0 = exchange(parts0)
    keep1, send1 = last(1, (1,), acc2, (0,), (acc_mid,))
    pieces1 = exchange(pair_sum(keep1, swap(send1)))
    return pl.pallas_call(
        final_kernel, in_specs=[VMEM] * (2 * NZ), out_specs=VMEM,
        out_shape=struct((2 * PIECE, DOUT), bf16), name="final", compiler_params=params(6),
    )(*pieces0, *pieces1)


def solution(mesh):
    return jax.shard_map(
        on_device,
        mesh=mesh,
        in_specs=(P("ctx", "tp"), P("ctx", "tp"), P("ctx", "tp"), P("ctx"), P("tp", None)),
        out_specs=P(("ctx", "tp"), None),
        check_vma=False,
    )
```

```python
import functools
import math

import jax
import jax.numpy as jnp
from jax import lax
from jax.experimental import pallas as pl
from jax.experimental.pallas import tpu as pltpu
from jax.sharding import PartitionSpec as P


HD = 128
SPAN = 128
QUAD = 4
PACK = 272
LOG_SCALE = HD ** -0.5 * math.log2(math.e)
NEG = -1e30
NX = 4
NZ = 4
NCORE = 2
PIECE = 16
DOUT = 8192
NCOL = 8
GROUP = 4
HEADROOM = 60.0
NW = 4
HOPS = (2, 1, 3)


VMEM = pl.BlockSpec(memory_space=pltpu.VMEM)
SMEM = pl.BlockSpec(memory_space=pltpu.SMEM)
HBM = pl.BlockSpec(memory_space=pltpu.HBM)


def struct(shape, dtype):
    return jax.ShapeDtypeStruct(shape, dtype)


def pack_kernel(pos_hbm, k_hbm, v_hbm, out_ref, half_ref, pos_ref, k_ref, v_ref, sems):
    copies = [
        pltpu.make_async_copy(src, dst, sems.at[i])
        for i, (src, dst) in enumerate(((v_hbm, v_ref), (k_hbm, k_ref), (pos_hbm, pos_ref)))
    ]
    for copy in copies:
        copy.start()
    for copy in copies:
        copy.wait()
    for s in range(2):
        rows = slice(s * SPAN, (s + 1) * SPAN)
        span = (pos_ref[s * SPAN] // SPAN).astype(jnp.float32)
        base = s * PACK
        out_ref[base:base + 128] = k_ref[rows, :]
        out_ref[base + 128:base + 256] = v_ref[rows, :].T
        ids = jnp.full((16, 128), span, jnp.float32).astype(jnp.bfloat16)
        out_ref[base + 256:base + PACK] = ids
    half_ref[...] = out_ref[0:PACK]


def join_kernel(*refs):
    out_ref = refs[-1]
    for i, ref in enumerate(refs[:-1]):
        rows = ref.shape[0]
        out_ref[i * PACK:(i + 1) * PACK] = ref[rows - PACK:rows]


def query_tile(q_ref, chunk, s, quad):
    pieces = []
    for h in range(quad * QUAD, (quad + 1) * QUAD):
        for t in range(4):
            row = s * SPAN + t * 32 + chunk * PIECE
            pieces.append(q_ref[row:row + PIECE, h * HD:(h + 1) * HD])
    return jnp.concatenate(pieces, axis=0)


def scores_of(kt, q):
    return lax.dot_general(kt, q, (((1,), (1,)), ((), ())), preferred_element_type=jnp.float32)


def weighted(vt, probs):
    return jnp.dot(vt, probs, preferred_element_type=jnp.float32)


def store_keys(kv_ref, blocks):
    for i, (ref, j) in enumerate(blocks):
        kv_ref[i, 0:256, :] = ref[j * PACK:j * PACK + 256, :]
        kv_ref[i, 256:PACK, :] = jnp.ones((16, 128), jnp.bfloat16)
    kv_ref[len(blocks)] = jnp.zeros((PACK, 128), jnp.bfloat16)


def span_id(ref, i):
    ids = ref[i * PACK + 256:(i + 1) * PACK, :].astype(jnp.float32)
    return jnp.max(ids).astype(jnp.int32)


def visible_list(list_ref, ids, limit):
    count = jnp.int32(0)
    for i, span in enumerate(ids):
        list_ref[count] = jnp.int32(i)
        count = count + jnp.where(span < limit, 1, 0)
    for i in range(GROUP):
        list_ref[count + i] = jnp.int32(len(ids))
    return count


def fast_walk(kv_ref, list_ref, count, queries, units, m_ref, peak_ref, acc_ref, probs):
    shifts = [m_ref[u][0:1, :] for u in units]

    def score(g, p_ref):
        slots = [list_ref[g * GROUP + i] for i in range(GROUP)]
        kt = jnp.concatenate([kv_ref[i, 0:128, :] for i in slots], axis=0)
        for n, u in enumerate(units):
            scores = scores_of(kt, queries[n])
            tiles = scores.reshape(GROUP * SPAN // 8, 8, 256)
            peak_ref[u] = jnp.maximum(peak_ref[u], jnp.max(tiles, axis=0))
            p_ref[n] = jnp.exp2((scores - shifts[n]) * LOG_SCALE).astype(jnp.bfloat16)

    def add(g, p_ref):
        slots = [list_ref[g * GROUP + i] for i in range(GROUP)]
        vt = jnp.concatenate([kv_ref[i, 128:PACK, :] for i in slots], axis=1)
        for n, u in enumerate(units):
            acc_ref[u] = acc_ref[u] + weighted(vt, p_ref[n])

    even, odd = probs
    groups = jnp.maximum((count + GROUP - 1) // GROUP, 1)
    score(0, even)

    def pair(i, carry):
        score(2 * i + 1, odd)
        add(2 * i, even)
        score(2 * i + 2, even)
        add(2 * i + 1, odd)
        return carry

    lax.fori_loop(0, (groups - 1) // 2, pair, 0)

    @pl.when(groups % 2 == 1)
    def _():
        add(groups - 1, even)

    @pl.when(groups % 2 == 0)
    def _():
        score(groups - 1, odd)
        add(groups - 2, even)
        add(groups - 1, odd)


def slow_walk(kv_ref, list_ref, count, queries, units, m_ref, acc_ref):
    def step(i, carry):
        slot = list_ref[i]
        for n, u in enumerate(units):
            scores = scores_of(kv_ref[slot, 0:128, :], queries[n])
            m_old = m_ref[u][0:1, :]
            m_new = jnp.maximum(m_old, jnp.max(scores, axis=0, keepdims=True))
            probs = jnp.exp2((scores - m_new) * LOG_SCALE).astype(jnp.bfloat16)
            scale = jnp.exp2((m_old - m_new) * LOG_SCALE)
            acc_ref[u] = acc_ref[u] * scale + weighted(kv_ref[slot, 128:PACK, :], probs)
            m_ref[u] = jnp.broadcast_to(m_new, (8, 256))
        return carry

    lax.fori_loop(0, count, step, 0)


def overshoot(peak_ref, m_ref, units):
    worst = peak_ref[units[0]] - m_ref[units[0]]
    for u in units[1:]:
        worst = jnp.maximum(worst, peak_ref[u] - m_ref[u])
    return jnp.max(worst) * LOG_SCALE > HEADROOM


def fetch_half(half, w_hbm, w_ref, sems):
    copies = []
    for j in range(NW):
        rows = pl.ds(j * (1024 // NW), 1024 // NW)
        columns = pl.ds(half * DOUT // 2, DOUT // 2)
        copies.append(pltpu.make_async_copy(w_hbm.at[rows, columns], w_ref.at[rows], sems.at[j]))
        copies[j].start()
    return copies


def first_kernel(q_hbm, w_hbm, own_ref, x1, x2, x3, y1, y2, y3, m_ref, acc_ref, tile_ref, w_ref,
                 q_ref, kv_ref, peak_ref, even_ref, odd_ref, list0, list1, sems):
    fetch_q = pltpu.make_async_copy(q_hbm, q_ref, sems.at[NW])
    fetch_q.start()
    fetch_w = fetch_half(0, w_hbm, w_ref, sems)
    blocks = [(ref, j) for ref in (own_ref, y1, y2, y3) for j in range(2)]
    blocks += [(ref, 0) for ref in (x1, x2, x3)]
    store_keys(kv_ref, blocks)
    ids = [span_id(ref, j) for ref, j in blocks]
    counts = [visible_list(ref, ids, ids[s]) for s, ref in enumerate((list0, list1))]
    lists = (list0, list1)
    fetch_q.wait()
    for chunk in range(2):
        for s in range(2):
            for quad in range(2):
                tile_ref[chunk * 4 + s * 2 + quad] = query_tile(q_ref, chunk, s, quad)
    units = [[chunk * 4 + s * 2 + quad for chunk in range(2) for quad in range(2)] for s in range(2)]
    queries = [[tile_ref[u] for u in units[s]] for s in range(2)]

    def own_block():
        for s in range(2):
            for n, u in enumerate(units[s]):
                lane = lax.broadcasted_iota(jnp.int32, (SPAN, 256), 1) % 64
                row = (lane // PIECE) * 32 + lane % PIECE + (n // 2) * PIECE
                scores = scores_of(kv_ref[s, 0:128, :], queries[s][n])
                key = lax.broadcasted_iota(jnp.int32, (SPAN, 256), 0)
                scores = jnp.where(key <= row, scores, NEG)
                m_new = jnp.max(scores, axis=0, keepdims=True)
                probs = jnp.exp2((scores - m_new) * LOG_SCALE).astype(jnp.bfloat16)
                acc_ref[u] = weighted(kv_ref[s, 128:PACK, :], probs)
                m_ref[u] = jnp.broadcast_to(m_new, (8, 256))

    own_block()
    peak_ref[...] = m_ref[...]
    for s in range(2):
        fast_walk(kv_ref, lists[s], counts[s], queries[s], units[s], m_ref, peak_ref, acc_ref,
                  (even_ref, odd_ref))

    @pl.when(overshoot(peak_ref, m_ref, units[0] + units[1]))
    def _():
        own_block()
        for s in range(2):
            slow_walk(kv_ref, lists[s], counts[s], queries[s], units[s], m_ref, acc_ref)

    for copy in fetch_w:
        copy.wait()


def second_kernel(w_hbm, tile_ref, own_ref, b1, b2, b3, m_in, acc_in, m_ref, acc_ref, w_ref,
                  kv_ref, peak_ref, even_ref, odd_ref, list0, list1, sems):
    fetch_w = fetch_half(1, w_hbm, w_ref, sems)
    blocks = [(ref, j) for ref in (b1, b2, b3) for j in range(4)]
    store_keys(kv_ref, blocks)
    ids = [span_id(ref, j) for ref, j in blocks]
    lists = (list0, list1)
    counts = [visible_list(lists[s], ids, span_id(own_ref, s)) for s in range(2)]
    units = [[chunk * 4 + s * 2 + quad for chunk in range(2) for quad in range(2)] for s in range(2)]
    queries = [[tile_ref[u] for u in units[s]] for s in range(2)]

    def reset():
        m_ref[...] = m_in[...]
        acc_ref[...] = acc_in[...]

    reset()
    peak_ref[...] = m_in[...]
    for s in range(2):
        fast_walk(kv_ref, lists[s], counts[s], queries[s], units[s], m_ref, peak_ref, acc_ref,
                  (even_ref, odd_ref))

    @pl.when(overshoot(peak_ref, m_ref, units[0] + units[1]))
    def _():
        reset()
        for s in range(2):
            slow_walk(kv_ref, lists[s], counts[s], queries[s], units[s], m_ref, acc_ref)

    for copy in fetch_w:
        copy.wait()


def rest_of_attention(chunk, spans, tile_ref, own_ref, far, m_in, acc_in, kv_ref, m_ref, peak_ref,
                      acc_ref, even_ref, odd_ref, lists):
    blocks = [(ref, j) for ref in far for j in range(3)]
    store_keys(kv_ref, blocks)
    ids = [span_id(ref, j) for ref, j in blocks]
    counts = [visible_list(lists[n], ids, span_id(own_ref, s)) for n, s in enumerate(spans)]
    queries = [[tile_ref[chunk * 4 + s * 2 + quad] for quad in range(2)] for s in spans]
    units = [(2 * n, 2 * n + 1) for n in range(len(spans))]

    def reset():
        for n, s in enumerate(spans):
            for quad in range(2):
                m_ref[2 * n + quad] = m_in[chunk * 4 + s * 2 + quad]
                acc_ref[2 * n + quad] = acc_in[chunk * 4 + s * 2 + quad]

    reset()
    peak_ref[...] = m_ref[...]
    for n in range(len(spans)):
        fast_walk(kv_ref, lists[n], counts[n], queries[n], units[n], m_ref, peak_ref, acc_ref,
                  (even_ref, odd_ref))

    @pl.when(overshoot(peak_ref, m_ref, range(2 * len(spans))))
    def _():
        reset()
        for n in range(len(spans)):
            slow_walk(kv_ref, lists[n], counts[n], queries[n], units[n], m_ref, acc_ref)


def finish(s, acc_ref, base, index_ref, merged_ref):
    z, core = index_ref[0] // NCORE, index_ref[0] % NCORE
    for quad in range(2):
        acc = acc_ref[base + quad]
        o = acc[:128] * (1.0 / acc[128:129])
        for half in range(2):
            rows = o[:, half * 128:(half + 1) * 128].T.astype(jnp.bfloat16)
            for i in range(2):
                h = quad * QUAD + half * 2 + i
                for t in range(4):
                    owner = s * 4 + t
                    place = ((owner % NCORE) ^ core) * NZ + (owner // NCORE - z + NZ) % NZ
                    where = pl.multiple_of(place * PIECE, PIECE)
                    at = i * 64 + t * PIECE
                    merged_ref[pl.ds(where, PIECE), h * HD:(h + 1) * HD] = rows[at:at + PIECE]


def project(merged_ref, w_ref, keep_ref, send_ref):
    cols = DOUT // NCOL
    for j in range(NCOL // 2):
        at = slice(j * cols, (j + 1) * cols)
        part = jnp.dot(merged_ref[...], w_ref[:, at], preferred_element_type=jnp.float32)
        part = part.astype(jnp.bfloat16)
        keep_ref[:, at] = part[:64]
        send_ref[:, at] = part[64:]


def middle_kernel(chunk, spans, tile_ref, own_ref, a1, a2, a3, m_in, acc_in, acc_ref,
                  kv_ref, m_ref, peak_ref, even_ref, odd_ref, list0, list1):
    rest_of_attention(chunk, spans, tile_ref, own_ref, (a1, a2, a3), m_in, acc_in, kv_ref,
                      m_ref, peak_ref, acc_ref, even_ref, odd_ref, (list0, list1))


def last_kernel(chunk, spans, done, index_ref, tile_ref, own_ref, a1, a2, a3, m_in, acc_in,
                w_ref, *refs):
    acc_done = refs[0] if done else None
    (keep_ref, send_ref, merged_ref, acc_ref, kv_ref, m_ref, peak_ref, even_ref, odd_ref,
     list0, list1) = refs[-11:]
    rest_of_attention(chunk, spans, tile_ref, own_ref, (a1, a2, a3), m_in, acc_in, kv_ref,
                      m_ref, peak_ref, acc_ref, even_ref, odd_ref, (list0, list1))
    for n, s in enumerate(spans):
        finish(s, acc_ref, 2 * n, index_ref, merged_ref)
    for n, s in enumerate(done):
        finish(s, acc_done, 2 * n, index_ref, merged_ref)
    project(merged_ref, w_ref, keep_ref, send_ref)


def pair_kernel(keep_a, got_a, keep_b, got_b, *out_refs):
    for half, keep_ref, got_ref in ((0, keep_a, got_a), (1, keep_b, got_b)):
        total = keep_ref[...].astype(jnp.float32) + got_ref[...].astype(jnp.float32)
        columns = slice(half * DOUT // 2, (half + 1) * DOUT // 2)
        for d in range(NZ):
            out_refs[d][:, columns] = total[d * PIECE:(d + 1) * PIECE].astype(jnp.bfloat16)


def final_kernel(*refs):
    out_ref = refs[-1]
    for chunk in range(2):
        parts = [r[...].astype(jnp.float32) for r in refs[chunk * NZ:(chunk + 1) * NZ]]
        total = (parts[0] + parts[1]) + (parts[2] + parts[3])
        out_ref[chunk * PIECE:(chunk + 1) * PIECE, :] = total.astype(jnp.bfloat16)


def in_hbm(array):
    return pltpu.with_memory_space_constraint(array, pltpu.HBM)


def params(mib):
    return pltpu.CompilerParams(vmem_limit_bytes=mib << 20)


def estimate(flops, traffic):
    return pl.CostEstimate(flops=flops, bytes_accessed=traffic, transcendentals=0)


def ctx_route(dx, dy):
    return [
        (x * NX + y, ((x + dx) % NX) * NX + (y + dy) % NX)
        for x in range(NX) for y in range(NX)
    ]


def tp_route(dz, swap):
    return [
        (z * NCORE + c, ((z + dz) % NZ) * NCORE + (c ^ swap))
        for z in range(NZ) for c in range(NCORE)
    ]


def on_device(queries, keys, values, positions, out_weight):
    bf16, f32 = jnp.bfloat16, jnp.float32
    index = lax.axis_index("tp").reshape(1)

    own, half = pl.pallas_call(
        pack_kernel, in_specs=[HBM] * 3, out_specs=[VMEM] * 2,
        out_shape=[struct((2 * PACK, HD), bf16), struct((PACK, HD), bf16)],
        name="pack", compiler_params=params(2),
        scratch_shapes=[
            pltpu.SMEM((2 * SPAN,), jnp.int32), pltpu.VMEM((2 * SPAN, HD), bf16),
            pltpu.VMEM((2 * SPAN, HD), bf16), pltpu.SemaphoreType.DMA((3,)),
        ],
    )(in_hbm(positions), in_hbm(keys), in_hbm(values))

    def shifts(block, dx, dy):
        moved = []
        for d in HOPS:
            moved.append(lax.ppermute(block, "ctx", ctx_route(dx * d, dy * d)))
        return moved

    def join(*blocks):
        return pl.pallas_call(
            join_kernel, in_specs=[VMEM] * len(blocks), out_specs=VMEM,
            out_shape=struct((len(blocks) * PACK, HD), bf16), name="join",
            compiler_params=params(2),
        )(*blocks)

    ys = shifts(own, 0, 1)
    xs = shifts(half, 1, 0)
    column = join(own, *ys)
    fb = shifts(column, 1, 0)
    fa = shifts(join(*xs), 0, 1)

    def walk_scratch(slots, units, width):
        return [
            pltpu.VMEM((slots + 1, PACK, 128), bf16),
            pltpu.VMEM((units, 8, 256), f32),
            pltpu.VMEM((units, 8, 256), f32),
            pltpu.VMEM((width, GROUP * SPAN, 256), bf16),
            pltpu.VMEM((width, GROUP * SPAN, 256), bf16),
            pltpu.SMEM((32,), jnp.int32),
            pltpu.SMEM((32,), jnp.int32),
        ]

    scratch = walk_scratch(11, 8, 4)
    first = pl.pallas_call(
        first_kernel, in_specs=[HBM] * 2 + [VMEM] * 7, out_specs=[VMEM] * 4,
        out_shape=[
            struct((8, 8, 256), f32), struct((8, 144, 256), f32),
            struct((8, 256, 128), bf16), struct((1024, DOUT // 2), bf16),
        ],
        scratch_shapes=[pltpu.VMEM((256, 1024), bf16)] + scratch[:1] + scratch[2:]
        + [pltpu.SemaphoreType.DMA((NW + 1,))],
        compiler_params=params(14), name="first",
        cost_estimate=estimate(4 * 10 ** 9, 1 << 20),
    )
    maxima, acc, tiles, weight_a = first(
        in_hbm(queries), in_hbm(out_weight), own, *xs, *ys
    )

    scratch = walk_scratch(12, 8, 4)
    second = pl.pallas_call(
        second_kernel, in_specs=[HBM] + [VMEM] * 7, out_specs=[VMEM] * 3,
        out_shape=[
            struct((8, 8, 256), f32), struct((8, 144, 256), f32), struct((1024, DOUT // 2), bf16),
        ],
        scratch_shapes=scratch[:1] + scratch[2:] + [pltpu.SemaphoreType.DMA((NW,))],
        compiler_params=params(14), name="second",
        cost_estimate=estimate(4 * 10 ** 9, 1 << 20),
    )
    maxima, acc, weight_b = second(in_hbm(out_weight), tiles, own, *fb, maxima, acc)

    def middle(chunk, spans, acc):
        n = 2 * len(spans)
        return pl.pallas_call(
            functools.partial(middle_kernel, chunk, spans),
            in_specs=[VMEM] * 7, out_specs=VMEM, out_shape=struct((n, 144, 256), f32),
            scratch_shapes=walk_scratch(9, n, 2),
            compiler_params=params(14), name="middle",
            cost_estimate=estimate(2 * 10 ** 9, 1 << 20),
        )(tiles, own, *fa, maxima, acc)

    halves = [struct((64, DOUT // 2), bf16)] * 2

    def last(chunk, spans, acc, done=(), acc_done=()):
        n = 2 * len(spans)
        return pl.pallas_call(
            functools.partial(last_kernel, chunk, spans, done),
            in_specs=[SMEM] + [VMEM] * (8 + len(acc_done)),
            out_specs=[VMEM] * 3,
            out_shape=halves + [struct((128, 1024), bf16)],
            scratch_shapes=[pltpu.VMEM((n, 144, 256), f32)] + walk_scratch(9, n, 2),
            compiler_params=params(14),
            cost_estimate=estimate(5 * 10 ** 9, 1 << 20),
        )(index, tiles, own, *fa, maxima, acc, weight_a, *acc_done)

    def rest(merged):
        return pl.pallas_call(
            project, in_specs=[VMEM] * 2, out_specs=[VMEM] * 2, out_shape=halves,
            compiler_params=params(6), name="rest", cost_estimate=estimate(10 ** 9, 1 << 20),
        )(merged, weight_b)

    def pair_sum(*blocks):
        return pl.pallas_call(
            pair_kernel, in_specs=[VMEM] * 4, out_specs=[VMEM] * NZ,
            out_shape=[struct((PIECE, DOUT), bf16)] * NZ, name="pair",
            compiler_params=params(6),
        )(*blocks)

    def swap(block):
        return lax.ppermute(block, "tp", tp_route(0, 1))

    def exchange(parts):
        return [parts[0]] + [lax.ppermute(parts[d], "tp", tp_route(d, 0)) for d in HOPS]

    keep0a, send0a, merged0 = last(0, (0, 1), acc)
    got0a = swap(send0a)
    keep0b, send0b = rest(merged0)
    send0b, acc1 = lax.optimization_barrier((send0b, acc))
    got0b = swap(send0b)
    acc_mid = middle(1, (0,), acc1)
    keep0b, acc_mid = lax.optimization_barrier((keep0b, acc_mid))
    parts0 = pair_sum(keep0a, got0a, keep0b, got0b)
    *parts0, acc2 = lax.optimization_barrier((*parts0, acc))
    pieces0 = exchange(parts0)
    keep1a, send1a, merged1 = last(1, (1,), acc2, (0,), (acc_mid,))
    got1a = swap(send1a)
    keep1b, send1b = rest(merged1)
    pieces1 = exchange(pair_sum(keep1a, got1a, keep1b, swap(send1b)))
    return pl.pallas_call(
        final_kernel, in_specs=[VMEM] * (2 * NZ), out_specs=VMEM,
        out_shape=struct((2 * PIECE, DOUT), bf16), name="final", compiler_params=params(6),
    )(*pieces0, *pieces1)


def solution(mesh):
    return jax.shard_map(
        on_device,
        mesh=mesh,
        in_specs=(P("ctx", "tp"), P("ctx", "tp"), P("ctx", "tp"), P("ctx"), P("tp", None)),
        out_specs=P(("ctx", "tp"), None),
        check_vma=False,
    )
```

```python
import functools
import math

import jax
import jax.numpy as jnp
from jax import lax
from jax.experimental import pallas as pl
from jax.experimental.pallas import tpu as pltpu
from jax.sharding import PartitionSpec as P


HD = 128
SPAN = 128
QUAD = 4
PACK = 272
LOG_SCALE = HD ** -0.5 * math.log2(math.e)
NEG = -1e30
NX = 4
NZ = 4
NCORE = 2
PIECE = 16
DOUT = 8192
NCOL = 8
GROUP = 4
HEADROOM = 60.0
NW = 4
HOPS = (1, 3, 2)


VMEM = pl.BlockSpec(memory_space=pltpu.VMEM)
SMEM = pl.BlockSpec(memory_space=pltpu.SMEM)
HBM = pl.BlockSpec(memory_space=pltpu.HBM)


def struct(shape, dtype):
    return jax.ShapeDtypeStruct(shape, dtype)


def pack_kernel(pos_hbm, k_hbm, v_hbm, out_ref, pos_ref, k_ref, v_ref, sems):
    copies = [
        pltpu.make_async_copy(src, dst, sems.at[i])
        for i, (src, dst) in enumerate(((v_hbm, v_ref), (k_hbm, k_ref), (pos_hbm, pos_ref)))
    ]
    for copy in copies:
        copy.start()
    for copy in copies:
        copy.wait()
    for s in range(2):
        rows = slice(s * SPAN, (s + 1) * SPAN)
        span = (pos_ref[s * SPAN] // SPAN).astype(jnp.float32)
        base = s * PACK
        out_ref[base:base + 128] = k_ref[rows, :]
        out_ref[base + 128:base + 256] = v_ref[rows, :].T
        ids = jnp.full((16, 128), span, jnp.float32).astype(jnp.bfloat16)
        out_ref[base + 256:base + PACK] = ids


def join_kernel(part, *refs):
    out_ref = refs[-1]
    for i, ref in enumerate(refs[:-1]):
        out_ref[i * PACK:(i + 1) * PACK] = ref[part * PACK:(part + 1) * PACK]


def query_tile(q_ref, chunk, s, quad):
    pieces = []
    for h in range(quad * QUAD, (quad + 1) * QUAD):
        for t in range(4):
            row = s * SPAN + t * 32 + chunk * PIECE
            pieces.append(q_ref[row:row + PIECE, h * HD:(h + 1) * HD])
    return jnp.concatenate(pieces, axis=0)


def scores_of(kt, q):
    return lax.dot_general(kt, q, (((1,), (1,)), ((), ())), preferred_element_type=jnp.float32)


def weighted(vt, probs):
    return jnp.dot(vt, probs, preferred_element_type=jnp.float32)


def store_keys(kv_ref, blocks):
    for i, (ref, j) in enumerate(blocks):
        kv_ref[i, 0:256, :] = ref[j * PACK:j * PACK + 256, :]
        kv_ref[i, 256:PACK, :] = jnp.ones((16, 128), jnp.bfloat16)
    kv_ref[len(blocks)] = jnp.zeros((PACK, 128), jnp.bfloat16)


def span_id(ref, i):
    ids = ref[i * PACK + 256:(i + 1) * PACK, :].astype(jnp.float32)
    return jnp.max(ids).astype(jnp.int32)


def visible_list(list_ref, ids, limit):
    count = jnp.int32(0)
    for i, span in enumerate(ids):
        list_ref[count] = jnp.int32(i)
        count = count + jnp.where(span < limit, 1, 0)
    for i in range(GROUP):
        list_ref[count + i] = jnp.int32(len(ids))
    return count


def fast_walk(kv_ref, list_ref, count, queries, units, m_ref, peak_ref, acc_ref, probs):
    shifts = [m_ref[u][0:1, :] for u in units]

    def score(g, p_ref):
        slots = [list_ref[g * GROUP + i] for i in range(GROUP)]
        kt = jnp.concatenate([kv_ref[i, 0:128, :] for i in slots], axis=0)
        for n, u in enumerate(units):
            scores = scores_of(kt, queries[n])
            tiles = scores.reshape(GROUP * SPAN // 8, 8, 256)
            peak_ref[u] = jnp.maximum(peak_ref[u], jnp.max(tiles, axis=0))
            p_ref[n] = jnp.exp2((scores - shifts[n]) * LOG_SCALE).astype(jnp.bfloat16)

    def add(g, p_ref):
        slots = [list_ref[g * GROUP + i] for i in range(GROUP)]
        vt = jnp.concatenate([kv_ref[i, 128:PACK, :] for i in slots], axis=1)
        for n, u in enumerate(units):
            acc_ref[u] = acc_ref[u] + weighted(vt, p_ref[n])

    even, odd = probs
    groups = jnp.maximum((count + GROUP - 1) // GROUP, 1)
    score(0, even)

    def pair(i, carry):
        score(2 * i + 1, odd)
        add(2 * i, even)
        score(2 * i + 2, even)
        add(2 * i + 1, odd)
        return carry

    lax.fori_loop(0, (groups - 1) // 2, pair, 0)

    @pl.when(groups % 2 == 1)
    def _():
        add(groups - 1, even)

    @pl.when(groups % 2 == 0)
    def _():
        score(groups - 1, odd)
        add(groups - 2, even)
        add(groups - 1, odd)


def slow_walk(kv_ref, list_ref, count, queries, units, m_ref, acc_ref):
    def step(i, carry):
        slot = list_ref[i]
        for n, u in enumerate(units):
            scores = scores_of(kv_ref[slot, 0:128, :], queries[n])
            m_old = m_ref[u][0:1, :]
            m_new = jnp.maximum(m_old, jnp.max(scores, axis=0, keepdims=True))
            probs = jnp.exp2((scores - m_new) * LOG_SCALE).astype(jnp.bfloat16)
            scale = jnp.exp2((m_old - m_new) * LOG_SCALE)
            acc_ref[u] = acc_ref[u] * scale + weighted(kv_ref[slot, 128:PACK, :], probs)
            m_ref[u] = jnp.broadcast_to(m_new, (8, 256))
        return carry

    lax.fori_loop(0, count, step, 0)


def overshoot(peak_ref, m_ref, units):
    worst = peak_ref[units[0]] - m_ref[units[0]]
    for u in units[1:]:
        worst = jnp.maximum(worst, peak_ref[u] - m_ref[u])
    return jnp.max(worst) * LOG_SCALE > HEADROOM


def fetch_half(half, w_hbm, w_ref, sems):
    copies = []
    for j in range(NW):
        rows = pl.ds(j * (1024 // NW), 1024 // NW)
        columns = pl.ds(half * DOUT // 2, DOUT // 2)
        copies.append(pltpu.make_async_copy(w_hbm.at[rows, columns], w_ref.at[rows], sems.at[j]))
        copies[j].start()
    return copies


def first_kernel(q_hbm, w_hbm, own_ref, x1, x2, x3, y1, y2, y3, m_ref, acc_ref, tile_ref, w_ref,
                 q_ref, kv_ref, peak_ref, even_ref, odd_ref, list0, list1, sems):
    fetch_q = pltpu.make_async_copy(q_hbm, q_ref, sems.at[NW])
    fetch_q.start()
    fetch_w = fetch_half(0, w_hbm, w_ref, sems)
    blocks = [(ref, j) for ref in (own_ref, x1, x2, x3, y1, y2, y3) for j in range(2)]
    store_keys(kv_ref, blocks)
    ids = [span_id(ref, j) for ref, j in blocks]
    counts = [visible_list(ref, ids, ids[s]) for s, ref in enumerate((list0, list1))]
    lists = (list0, list1)
    fetch_q.wait()
    for chunk in range(2):
        for s in range(2):
            for quad in range(2):
                tile_ref[chunk * 4 + s * 2 + quad] = query_tile(q_ref, chunk, s, quad)
    units = [[chunk * 4 + s * 2 + quad for chunk in range(2) for quad in range(2)] for s in range(2)]
    queries = [[tile_ref[u] for u in units[s]] for s in range(2)]

    def own_block():
        for s in range(2):
            for n, u in enumerate(units[s]):
                lane = lax.broadcasted_iota(jnp.int32, (SPAN, 256), 1) % 64
                row = (lane // PIECE) * 32 + lane % PIECE + (n // 2) * PIECE
                scores = scores_of(kv_ref[s, 0:128, :], queries[s][n])
                key = lax.broadcasted_iota(jnp.int32, (SPAN, 256), 0)
                scores = jnp.where(key <= row, scores, NEG)
                m_new = jnp.max(scores, axis=0, keepdims=True)
                probs = jnp.exp2((scores - m_new) * LOG_SCALE).astype(jnp.bfloat16)
                acc_ref[u] = weighted(kv_ref[s, 128:PACK, :], probs)
                m_ref[u] = jnp.broadcast_to(m_new, (8, 256))

    own_block()
    peak_ref[...] = m_ref[...]
    for s in range(2):
        fast_walk(kv_ref, lists[s], counts[s], queries[s], units[s], m_ref, peak_ref, acc_ref,
                  (even_ref, odd_ref))

    @pl.when(overshoot(peak_ref, m_ref, units[0] + units[1]))
    def _():
        own_block()
        for s in range(2):
            slow_walk(kv_ref, lists[s], counts[s], queries[s], units[s], m_ref, acc_ref)

    for copy in fetch_w:
        copy.wait()


def rest_of_attention(chunk, spans, tile_ref, own_ref, far, m_in, acc_in, kv_ref, m_ref, peak_ref,
                      acc_ref, even_ref, odd_ref, lists):
    blocks = [(ref, j) for ref in far for j in range(3)]
    store_keys(kv_ref, blocks)
    ids = [span_id(ref, j) for ref, j in blocks]
    counts = [visible_list(lists[n], ids, span_id(own_ref, s)) for n, s in enumerate(spans)]
    queries = [[tile_ref[chunk * 4 + s * 2 + quad] for quad in range(2)] for s in spans]
    units = [(2 * n, 2 * n + 1) for n in range(len(spans))]

    def reset():
        for n, s in enumerate(spans):
            for quad in range(2):
                m_ref[2 * n + quad] = m_in[chunk * 4 + s * 2 + quad]
                acc_ref[2 * n + quad] = acc_in[chunk * 4 + s * 2 + quad]

    reset()
    peak_ref[...] = m_ref[...]
    for n in range(len(spans)):
        fast_walk(kv_ref, lists[n], counts[n], queries[n], units[n], m_ref, peak_ref, acc_ref,
                  (even_ref, odd_ref))

    @pl.when(overshoot(peak_ref, m_ref, range(2 * len(spans))))
    def _():
        reset()
        for n in range(len(spans)):
            slow_walk(kv_ref, lists[n], counts[n], queries[n], units[n], m_ref, acc_ref)


def first_partner(z, core):
    return (((z + core) ^ 1) - core + NZ) % NZ


def place_of(z_to, core_to, z, core):
    near = jnp.where(first_partner(z, core_to) == z_to, 2, 1)
    slot = jnp.where(z_to == z, 0, jnp.where((z_to + 2) % NZ == z, 3, near))
    return (core_to ^ core) * NZ + slot


def finish(s, acc_ref, base, index_ref, merged_ref):
    z, core = index_ref[0] // NCORE, index_ref[0] % NCORE
    for quad in range(2):
        acc = acc_ref[base + quad]
        o = acc[:128] * (1.0 / acc[128:129])
        for half in range(2):
            rows = o[:, half * 128:(half + 1) * 128].T.astype(jnp.bfloat16)
            for i in range(2):
                h = quad * QUAD + half * 2 + i
                for t in range(4):
                    owner = s * 4 + t
                    place = place_of(owner // NCORE, owner % NCORE, z, core)
                    where = pl.multiple_of(place * PIECE, PIECE)
                    at = i * 64 + t * PIECE
                    merged_ref[pl.ds(where, PIECE), h * HD:(h + 1) * HD] = rows[at:at + PIECE]


def project(merged_ref, w_ref, keep_ref, send_ref):
    cols = DOUT // NCOL
    for j in range(NCOL // 2):
        at = slice(j * cols, (j + 1) * cols)
        part = jnp.dot(merged_ref[...], w_ref[:, at], preferred_element_type=jnp.float32)
        part = part.astype(jnp.bfloat16)
        keep_ref[:, at] = part[:64]
        send_ref[:, at] = part[64:]


def middle_kernel(chunk, spans, tile_ref, own_ref, a1, a2, a3, b1, b2, b3, m_in, acc_in, acc_ref,
                  kv_ref, m_ref, peak_ref, even_ref, odd_ref, list0, list1):
    rest_of_attention(chunk, spans, tile_ref, own_ref, (a1, a2, a3, b1, b2, b3), m_in, acc_in, kv_ref,
                      m_ref, peak_ref, acc_ref, even_ref, odd_ref, (list0, list1))


def last_kernel(chunk, spans, done, index_ref, tile_ref, own_ref, a1, a2, a3, b1, b2, b3, m_in, acc_in,
                w_ref, *refs):
    if done:
        acc_done = refs[0]
    else:
        w_hbm, w_next, sems = refs[0], refs[4], refs[-1]
        refs = refs[:4] + refs[5:-1]
        fetch_w = fetch_half(1, w_hbm, w_next, sems)
    (keep_ref, send_ref, merged_ref, acc_ref, kv_ref, m_ref, peak_ref, even_ref, odd_ref,
     list0, list1) = refs[-11:]
    rest_of_attention(chunk, spans, tile_ref, own_ref, (a1, a2, a3, b1, b2, b3), m_in, acc_in, kv_ref,
                      m_ref, peak_ref, acc_ref, even_ref, odd_ref, (list0, list1))
    for n, s in enumerate(spans):
        finish(s, acc_ref, 2 * n, index_ref, merged_ref)
    for n, s in enumerate(done):
        finish(s, acc_done, 2 * n, index_ref, merged_ref)
    project(merged_ref, w_ref, keep_ref, send_ref)
    if not done:
        for copy in fetch_w:
            copy.wait()


def pair_kernel(keep_a, got_a, keep_b, got_b, stay_ref, send_ref):
    for half, keep_ref, got_ref in ((0, keep_a, got_a), (1, keep_b, got_b)):
        total = (keep_ref[...].astype(jnp.float32) + got_ref[...]).astype(jnp.bfloat16)
        columns = slice(half * DOUT // 2, (half + 1) * DOUT // 2)
        stay_ref[:, columns] = total[:2 * PIECE]
        send_ref[:, columns] = total[2 * PIECE:]


def fold_kernel(stay_ref, got_ref, mine_ref, send_ref):
    total = (stay_ref[...].astype(jnp.float32) + got_ref[...]).astype(jnp.bfloat16)
    mine_ref[...] = total[:PIECE]
    send_ref[...] = total[PIECE:]


def final_kernel(mine0, got0, mine1, got1, out_ref):
    for chunk, mine_ref, got_ref in ((0, mine0, got0), (1, mine1, got1)):
        total = mine_ref[...].astype(jnp.float32) + got_ref[...]
        out_ref[chunk * PIECE:(chunk + 1) * PIECE, :] = total.astype(jnp.bfloat16)


def in_hbm(array):
    return pltpu.with_memory_space_constraint(array, pltpu.HBM)


def params(mib):
    return pltpu.CompilerParams(vmem_limit_bytes=mib << 20)


def estimate(flops, traffic):
    return pl.CostEstimate(flops=flops, bytes_accessed=traffic, transcendentals=0)


def ctx_route(dx, dy):
    return [
        (x * NX + y, ((x + dx) % NX) * NX + (y + dy) % NX)
        for x in range(NX) for y in range(NX)
    ]


def swap_route():
    return [(t, t ^ 1) for t in range(NZ * NCORE)]


def step_route(step):
    return [
        (z * NCORE + c, first_partner(z, c ^ step) * NCORE + c)
        for z in range(NZ) for c in range(NCORE)
    ]


def on_device(queries, keys, values, positions, out_weight):
    bf16, f32 = jnp.bfloat16, jnp.float32
    index = lax.axis_index("tp").reshape(1)

    own = pl.pallas_call(
        pack_kernel, in_specs=[HBM] * 3, out_specs=VMEM, out_shape=struct((2 * PACK, HD), bf16),
        name="pack", compiler_params=params(2),
        scratch_shapes=[
            pltpu.SMEM((2 * SPAN,), jnp.int32), pltpu.VMEM((2 * SPAN, HD), bf16),
            pltpu.VMEM((2 * SPAN, HD), bf16), pltpu.SemaphoreType.DMA((3,)),
        ],
    )(in_hbm(positions), in_hbm(keys), in_hbm(values))

    def shifts(block, dx, dy):
        moved = []
        for d in HOPS:
            moved.append(lax.ppermute(block, "ctx", ctx_route(dx * d, dy * d)))
        return moved

    def join(part, *blocks):
        return pl.pallas_call(
            functools.partial(join_kernel, part), in_specs=[VMEM] * len(blocks), out_specs=VMEM,
            out_shape=struct((len(blocks) * PACK, HD), bf16), name="join",
            compiler_params=params(2),
        )(*blocks)

    ys = shifts(own, 0, 1)
    xs = shifts(own, 1, 0)
    column = join(1, *ys)
    fb = shifts(column, 1, 0)
    fa = shifts(join(0, *xs), 0, 1)

    def walk_scratch(slots, units, width):
        return [
            pltpu.VMEM((slots + 1, PACK, 128), bf16),
            pltpu.VMEM((units, 8, 256), f32),
            pltpu.VMEM((units, 8, 256), f32),
            pltpu.VMEM((width, GROUP * SPAN, 256), bf16),
            pltpu.VMEM((width, GROUP * SPAN, 256), bf16),
            pltpu.SMEM((32,), jnp.int32),
            pltpu.SMEM((32,), jnp.int32),
        ]

    scratch = walk_scratch(14, 8, 4)
    first = pl.pallas_call(
        first_kernel, in_specs=[HBM] * 2 + [VMEM] * 7, out_specs=[VMEM] * 4,
        out_shape=[
            struct((8, 8, 256), f32), struct((8, 144, 256), f32),
            struct((8, 256, 128), bf16), struct((1024, DOUT // 2), bf16),
        ],
        scratch_shapes=[pltpu.VMEM((256, 1024), bf16)] + scratch[:1] + scratch[2:]
        + [pltpu.SemaphoreType.DMA((NW + 1,))],
        compiler_params=params(14), name="first",
        cost_estimate=estimate(4 * 10 ** 9, 1 << 20),
    )
    maxima, acc, tiles, weight_a = first(
        in_hbm(queries), in_hbm(out_weight), own, *xs, *ys
    )

    def middle(chunk, spans, acc):
        n = 2 * len(spans)
        return pl.pallas_call(
            functools.partial(middle_kernel, chunk, spans),
            in_specs=[VMEM] * 10, out_specs=VMEM, out_shape=struct((n, 144, 256), f32),
            scratch_shapes=walk_scratch(18, n, 2),
            compiler_params=params(14), name="middle",
            cost_estimate=estimate(2 * 10 ** 9, 1 << 20),
        )(tiles, own, *fa, *fb, maxima, acc)

    halves = [struct((64, DOUT // 2), bf16)] * 2

    def last(chunk, spans, acc, done, extra):
        n = 2 * len(spans)
        outs = halves + [struct((128, 1024), bf16)]
        scratch = [pltpu.VMEM((n, 144, 256), f32)] + walk_scratch(18, n, 2)
        if not done:
            outs = outs + [struct((1024, DOUT // 2), bf16)]
            scratch = scratch + [pltpu.SemaphoreType.DMA((NW,))]
        return pl.pallas_call(
            functools.partial(last_kernel, chunk, spans, done),
            in_specs=[SMEM] + [VMEM] * 11 + [VMEM if done else HBM],
            out_specs=[VMEM] * len(outs), out_shape=outs, scratch_shapes=scratch,
            compiler_params=params(14),
            cost_estimate=estimate(5 * 10 ** 9, 1 << 20),
        )(index, tiles, own, *fa, *fb, maxima, acc, weight_a, extra)

    def rest(merged):
        return pl.pallas_call(
            project, in_specs=[VMEM] * 2, out_specs=[VMEM] * 2, out_shape=halves,
            compiler_params=params(6), name="rest", cost_estimate=estimate(10 ** 9, 1 << 20),
        )(merged, weight_b)

    def call(kernel, rows, blocks):
        return pl.pallas_call(
            kernel, in_specs=[VMEM] * len(blocks), out_specs=[VMEM] * len(rows),
            out_shape=[struct((r, DOUT), bf16) for r in rows],
            compiler_params=params(6), cost_estimate=estimate(10 ** 6, 1 << 20),
        )(*blocks)

    def swap(block):
        return lax.ppermute(block, "tp", swap_route())

    def step(number, block):
        return lax.ppermute(block, "tp", step_route(number))

    keep0a, send0a, merged0, weight_b = last(0, (0, 1), acc, (), in_hbm(out_weight))
    got0a = swap(send0a)
    keep0b, send0b = rest(merged0)
    send0b, acc1 = lax.optimization_barrier((send0b, acc))
    got0b = swap(send0b)
    acc_mid = middle(1, (0,), acc1)
    keep0b, acc_mid = lax.optimization_barrier((keep0b, acc_mid))
    stay0, out0 = call(pair_kernel, (32, 32), (keep0a, got0a, keep0b, got0b))
    stay0, out0, acc2 = lax.optimization_barrier((stay0, out0, acc))
    in0 = step(0, out0)
    keep1a, send1a, merged1 = last(1, (1,), acc2, (0,), acc_mid)
    got1a = swap(send1a)
    keep1b, send1b = rest(merged1)
    in0, send1b = lax.optimization_barrier((in0, send1b))
    got1b = swap(send1b)
    mine0, out0 = call(fold_kernel, (16, 16), (stay0, in0))
    in0 = step(1, out0)
    stay1, out1 = call(pair_kernel, (32, 32), (keep1a, got1a, keep1b, got1b))
    in1 = step(0, out1)
    mine1, out1 = call(fold_kernel, (16, 16), (stay1, in1))
    in1 = step(1, out1)
    return call(final_kernel, (32,), (mine0, in0, mine1, in1))[0]


def solution(mesh):
    return jax.shard_map(
        on_device,
        mesh=mesh,
        in_specs=(P("ctx", "tp"), P("ctx", "tp"), P("ctx", "tp"), P("ctx"), P("tp", None)),
        out_specs=P(("ctx", "tp"), None),
        check_vma=False,
    )
```

```python
import functools
import math

import jax
import jax.numpy as jnp
from jax import lax
from jax.experimental import pallas as pl
from jax.experimental.pallas import tpu as pltpu
from jax.sharding import PartitionSpec as P


HD = 128
SPAN = 128
QUAD = 4
PACK = 272
LOG_SCALE = HD ** -0.5 * math.log2(math.e)
NEG = -1e30
NX = 4
NZ = 4
NCORE = 2
PIECE = 16
DOUT = 8192
NCOL = 8
GROUP = 4
HEADROOM = 60.0
NW = 4
HOPS = (1, 3, 2)


VMEM = pl.BlockSpec(memory_space=pltpu.VMEM)
SMEM = pl.BlockSpec(memory_space=pltpu.SMEM)
HBM = pl.BlockSpec(memory_space=pltpu.HBM)


def struct(shape, dtype):
    return jax.ShapeDtypeStruct(shape, dtype)


def pack_kernel(pos_hbm, k_hbm, v_hbm, out_ref, pos_ref, k_ref, v_ref, sems):
    copies = [
        pltpu.make_async_copy(src, dst, sems.at[i])
        for i, (src, dst) in enumerate(((v_hbm, v_ref), (k_hbm, k_ref), (pos_hbm, pos_ref)))
    ]
    for copy in copies:
        copy.start()
    for copy in copies:
        copy.wait()
    for s in range(2):
        rows = slice(s * SPAN, (s + 1) * SPAN)
        span = (pos_ref[s * SPAN] // SPAN).astype(jnp.float32)
        base = s * PACK
        out_ref[base:base + 128] = k_ref[rows, :]
        out_ref[base + 128:base + 256] = v_ref[rows, :].T
        ids = jnp.full((16, 128), span, jnp.float32).astype(jnp.bfloat16)
        out_ref[base + 256:base + PACK] = ids


def join_kernel(part, *refs):
    out_ref = refs[-1]
    for i, ref in enumerate(refs[:-1]):
        out_ref[i * PACK:(i + 1) * PACK] = ref[part * PACK:(part + 1) * PACK]


def query_tile(q_ref, chunk, s, quad):
    pieces = []
    for h in range(quad * QUAD, (quad + 1) * QUAD):
        for t in range(4):
            row = s * SPAN + t * 32 + chunk * PIECE
            pieces.append(q_ref[row:row + PIECE, h * HD:(h + 1) * HD])
    return jnp.concatenate(pieces, axis=0)


def scores_of(kt, q):
    return lax.dot_general(kt, q, (((1,), (1,)), ((), ())), preferred_element_type=jnp.float32)


def weighted(vt, probs):
    return jnp.dot(vt, probs, preferred_element_type=jnp.float32)


def store_keys(kv_ref, blocks):
    for i, (ref, j) in enumerate(blocks):
        kv_ref[i, 0:256, :] = ref[j * PACK:j * PACK + 256, :]
        kv_ref[i, 256:PACK, :] = jnp.ones((16, 128), jnp.bfloat16)
    kv_ref[len(blocks)] = jnp.zeros((PACK, 128), jnp.bfloat16)


def span_id(ref, i):
    ids = ref[i * PACK + 256:(i + 1) * PACK, :].astype(jnp.float32)
    return jnp.max(ids).astype(jnp.int32)


def visible_list(list_ref, ids, limit):
    count = jnp.int32(0)
    for i, span in enumerate(ids):
        list_ref[count] = jnp.int32(i)
        count = count + jnp.where(span < limit, 1, 0)
    for i in range(GROUP):
        list_ref[count + i] = jnp.int32(len(ids))
    return count


def fast_walk(kv_ref, list_ref, count, queries, units, m_ref, peak_ref, acc_ref, probs):
    shifts = [m_ref[u][0:1, :] for u in units]

    def score(g, p_ref):
        slots = [list_ref[g * GROUP + i] for i in range(GROUP)]
        kt = jnp.concatenate([kv_ref[i, 0:128, :] for i in slots], axis=0)
        for n, u in enumerate(units):
            scores = scores_of(kt, queries[n])
            tiles = scores.reshape(GROUP * SPAN // 8, 8, 256)
            peak_ref[u] = jnp.maximum(peak_ref[u], jnp.max(tiles, axis=0))
            p_ref[n] = jnp.exp2((scores - shifts[n]) * LOG_SCALE).astype(jnp.bfloat16)

    def add(g, p_ref):
        slots = [list_ref[g * GROUP + i] for i in range(GROUP)]
        vt = jnp.concatenate([kv_ref[i, 128:PACK, :] for i in slots], axis=1)
        for n, u in enumerate(units):
            acc_ref[u] = acc_ref[u] + weighted(vt, p_ref[n])

    even, odd = probs
    groups = jnp.maximum((count + GROUP - 1) // GROUP, 1)
    score(0, even)

    def pair(i, carry):
        score(2 * i + 1, odd)
        add(2 * i, even)
        score(2 * i + 2, even)
        add(2 * i + 1, odd)
        return carry

    lax.fori_loop(0, (groups - 1) // 2, pair, 0)

    @pl.when(groups % 2 == 1)
    def _():
        add(groups - 1, even)

    @pl.when(groups % 2 == 0)
    def _():
        score(groups - 1, odd)
        add(groups - 2, even)
        add(groups - 1, odd)


def slow_walk(kv_ref, list_ref, count, queries, units, m_ref, acc_ref):
    def step(i, carry):
        slot = list_ref[i]
        for n, u in enumerate(units):
            scores = scores_of(kv_ref[slot, 0:128, :], queries[n])
            m_old = m_ref[u][0:1, :]
            m_new = jnp.maximum(m_old, jnp.max(scores, axis=0, keepdims=True))
            probs = jnp.exp2((scores - m_new) * LOG_SCALE).astype(jnp.bfloat16)
            scale = jnp.exp2((m_old - m_new) * LOG_SCALE)
            acc_ref[u] = acc_ref[u] * scale + weighted(kv_ref[slot, 128:PACK, :], probs)
            m_ref[u] = jnp.broadcast_to(m_new, (8, 256))
        return carry

    lax.fori_loop(0, count, step, 0)


def overshoot(peak_ref, m_ref, units):
    worst = peak_ref[units[0]] - m_ref[units[0]]
    for u in units[1:]:
        worst = jnp.maximum(worst, peak_ref[u] - m_ref[u])
    return jnp.max(worst) * LOG_SCALE > HEADROOM


def fetch_half(half, w_hbm, w_ref, sems):
    copies = []
    for j in range(NW):
        rows = pl.ds(j * (1024 // NW), 1024 // NW)
        columns = pl.ds(half * DOUT // 2, DOUT // 2)
        copies.append(pltpu.make_async_copy(w_hbm.at[rows, columns], w_ref.at[rows], sems.at[j]))
        copies[j].start()
    return copies


def first_kernel(q_hbm, w_hbm, own_ref, x1, x2, x3, y1, y2, y3, m_ref, acc_ref, tile_ref, w_ref,
                 q_ref, kv_ref, peak_ref, even_ref, odd_ref, list0, list1, sems):
    fetch_q = pltpu.make_async_copy(q_hbm, q_ref, sems.at[NW])
    fetch_q.start()
    fetch_w = fetch_half(0, w_hbm, w_ref, sems)
    blocks = [(ref, j) for ref in (own_ref, x1, x2, x3, y1, y2, y3) for j in range(2)]
    store_keys(kv_ref, blocks)
    ids = [span_id(ref, j) for ref, j in blocks]
    counts = [visible_list(ref, ids, ids[s]) for s, ref in enumerate((list0, list1))]
    lists = (list0, list1)
    fetch_q.wait()
    for chunk in range(2):
        for s in range(2):
            for quad in range(2):
                tile_ref[chunk * 4 + s * 2 + quad] = query_tile(q_ref, chunk, s, quad)
    units = [[chunk * 4 + s * 2 + quad for chunk in range(2) for quad in range(2)] for s in range(2)]
    queries = [[tile_ref[u] for u in units[s]] for s in range(2)]

    def own_block():
        for s in range(2):
            for n, u in enumerate(units[s]):
                lane = lax.broadcasted_iota(jnp.int32, (SPAN, 256), 1) % 64
                row = (lane // PIECE) * 32 + lane % PIECE + (n // 2) * PIECE
                scores = scores_of(kv_ref[s, 0:128, :], queries[s][n])
                key = lax.broadcasted_iota(jnp.int32, (SPAN, 256), 0)
                scores = jnp.where(key <= row, scores, NEG)
                m_new = jnp.max(scores, axis=0, keepdims=True)
                probs = jnp.exp2((scores - m_new) * LOG_SCALE).astype(jnp.bfloat16)
                acc_ref[u] = weighted(kv_ref[s, 128:PACK, :], probs)
                m_ref[u] = jnp.broadcast_to(m_new, (8, 256))

    own_block()
    peak_ref[...] = m_ref[...]
    for s in range(2):
        fast_walk(kv_ref, lists[s], counts[s], queries[s], units[s], m_ref, peak_ref, acc_ref,
                  (even_ref, odd_ref))

    @pl.when(overshoot(peak_ref, m_ref, units[0] + units[1]))
    def _():
        own_block()
        for s in range(2):
            slow_walk(kv_ref, lists[s], counts[s], queries[s], units[s], m_ref, acc_ref)

    for copy in fetch_w:
        copy.wait()


def rest_of_attention(chunk, spans, tile_ref, own_ref, far, m_in, acc_in, kv_ref, m_ref, peak_ref,
                      acc_ref, even_ref, odd_ref, lists):
    blocks = [(ref, j) for ref in far for j in range(3)]
    store_keys(kv_ref, blocks)
    ids = [span_id(ref, j) for ref, j in blocks]
    counts = [visible_list(lists[n], ids, span_id(own_ref, s)) for n, s in enumerate(spans)]
    queries = [[tile_ref[chunk * 4 + s * 2 + quad] for quad in range(2)] for s in spans]
    units = [(2 * n, 2 * n + 1) for n in range(len(spans))]

    def reset():
        for n, s in enumerate(spans):
            for quad in range(2):
                m_ref[2 * n + quad] = m_in[chunk * 4 + s * 2 + quad]
                acc_ref[2 * n + quad] = acc_in[chunk * 4 + s * 2 + quad]

    reset()
    peak_ref[...] = m_ref[...]
    for n in range(len(spans)):
        fast_walk(kv_ref, lists[n], counts[n], queries[n], units[n], m_ref, peak_ref, acc_ref,
                  (even_ref, odd_ref))

    @pl.when(overshoot(peak_ref, m_ref, range(2 * len(spans))))
    def _():
        reset()
        for n in range(len(spans)):
            slow_walk(kv_ref, lists[n], counts[n], queries[n], units[n], m_ref, acc_ref)


def place_of(z_to, core_to, z, core):
    slot = jnp.where((z ^ 1) == z_to, 2, 1)
    slot = jnp.where(z_to == z, 0, jnp.where((z_to + 2) % NZ == z, 3, slot))
    return (core_to ^ core) * NZ + slot


def finish(s, acc_ref, base, index_ref, merged_ref):
    z, core = index_ref[0] // NCORE, index_ref[0] % NCORE
    for quad in range(2):
        acc = acc_ref[base + quad]
        o = acc[:128] * (1.0 / acc[128:129])
        for half in range(2):
            rows = o[:, half * 128:(half + 1) * 128].T.astype(jnp.bfloat16)
            for i in range(2):
                h = quad * QUAD + half * 2 + i
                for t in range(4):
                    owner = s * 4 + t
                    place = place_of(owner // NCORE, owner % NCORE, z, core)
                    where = pl.multiple_of(place * PIECE, PIECE)
                    at = i * 64 + t * PIECE
                    merged_ref[pl.ds(where, PIECE), h * HD:(h + 1) * HD] = rows[at:at + PIECE]


def project(merged_ref, w_ref, keep_ref, send_ref):
    cols = DOUT // NCOL
    for j in range(NCOL // 2):
        at = slice(j * cols, (j + 1) * cols)
        part = jnp.dot(merged_ref[...], w_ref[:, at], preferred_element_type=jnp.float32)
        part = part.astype(jnp.bfloat16)
        keep_ref[:, at] = part[:64]
        send_ref[:, at] = part[64:]


def last_kernel(chunk, index_ref, tile_ref, own_ref, f1, f2, f3, f4, f5, f6, m_in, acc_in, w_ref,
                *refs):
    if chunk == 0:
        w_hbm, w_next, sems = refs[0], refs[4], refs[-1]
        refs = refs[1:4] + refs[5:-1]
        fetch_w = fetch_half(1, w_hbm, w_next, sems)
    (keep_ref, send_ref, merged_ref, acc_ref, kv_ref, m_ref, peak_ref, even_ref, odd_ref,
     list0, list1) = refs
    spans = (0, 1)
    rest_of_attention(chunk, spans, tile_ref, own_ref, (f1, f2, f3, f4, f5, f6), m_in, acc_in,
                      kv_ref, m_ref, peak_ref, acc_ref, even_ref, odd_ref, (list0, list1))
    for s in spans:
        finish(s, acc_ref, 2 * s, index_ref, merged_ref)
    project(merged_ref, w_ref, keep_ref, send_ref)
    if chunk == 0:
        for copy in fetch_w:
            copy.wait()


def pair_kernel(half, keep_ref, got_ref, stay_ref, send_ref):
    stay, send = ((0, 1), (2, 3)) if half == 0 else ((0, 2), (1, 3))
    for out_ref, slots in ((stay_ref, stay), (send_ref, send)):
        for i, slot in enumerate(slots):
            rows = slice(slot * PIECE, (slot + 1) * PIECE)
            total = keep_ref[rows].astype(jnp.float32) + got_ref[rows]
            out_ref[i * PIECE:(i + 1) * PIECE] = total.astype(jnp.bfloat16)


def fold_kernel(stay_ref, got_ref, mine_ref, send_ref):
    total = (stay_ref[...].astype(jnp.float32) + got_ref[...]).astype(jnp.bfloat16)
    mine_ref[...] = total[:PIECE]
    send_ref[...] = total[PIECE:]


def final_kernel(*refs):
    out_ref = refs[-1]
    for i in range(4):
        chunk, half = i // 2, i % 2
        total = refs[2 * i][...].astype(jnp.float32) + refs[2 * i + 1][...]
        columns = slice(half * DOUT // 2, (half + 1) * DOUT // 2)
        out_ref[chunk * PIECE:(chunk + 1) * PIECE, columns] = total.astype(jnp.bfloat16)


def in_hbm(array):
    return pltpu.with_memory_space_constraint(array, pltpu.HBM)


def params(mib):
    return pltpu.CompilerParams(vmem_limit_bytes=mib << 20)


def estimate(flops, traffic):
    return pl.CostEstimate(flops=flops, bytes_accessed=traffic, transcendentals=0)


def ctx_route(dx, dy):
    return [
        (x * NX + y, ((x + dx) % NX) * NX + (y + dy) % NX)
        for x in range(NX) for y in range(NX)
    ]


def swap_route():
    return [(t, t ^ 1) for t in range(NZ * NCORE)]


def step_route(pairing):
    return [
        (z * NCORE + c, ((((z + pairing) ^ 1) - pairing) % NZ) * NCORE + c)
        for z in range(NZ) for c in range(NCORE)
    ]


def on_device(queries, keys, values, positions, out_weight):
    bf16, f32 = jnp.bfloat16, jnp.float32
    index = lax.axis_index("tp").reshape(1)

    own = pl.pallas_call(
        pack_kernel, in_specs=[HBM] * 3, out_specs=VMEM, out_shape=struct((2 * PACK, HD), bf16),
        name="pack", compiler_params=params(2),
        scratch_shapes=[
            pltpu.SMEM((2 * SPAN,), jnp.int32), pltpu.VMEM((2 * SPAN, HD), bf16),
            pltpu.VMEM((2 * SPAN, HD), bf16), pltpu.SemaphoreType.DMA((3,)),
        ],
    )(in_hbm(positions), in_hbm(keys), in_hbm(values))

    def shifts(block, dx, dy):
        moved = []
        for d in HOPS:
            moved.append(lax.ppermute(block, "ctx", ctx_route(dx * d, dy * d)))
        return moved

    def join(part, *blocks):
        return pl.pallas_call(
            functools.partial(join_kernel, part), in_specs=[VMEM] * len(blocks), out_specs=VMEM,
            out_shape=struct((len(blocks) * PACK, HD), bf16), name="join",
            compiler_params=params(2),
        )(*blocks)

    ys = shifts(own, 0, 1)
    xs = shifts(own, 1, 0)
    column = join(1, *ys)
    fb = shifts(column, 1, 0)
    fa = shifts(join(0, *xs), 0, 1)

    def walk_scratch(slots, units, width):
        return [
            pltpu.VMEM((slots + 1, PACK, 128), bf16),
            pltpu.VMEM((units, 8, 256), f32),
            pltpu.VMEM((units, 8, 256), f32),
            pltpu.VMEM((width, GROUP * SPAN, 256), bf16),
            pltpu.VMEM((width, GROUP * SPAN, 256), bf16),
            pltpu.SMEM((32,), jnp.int32),
            pltpu.SMEM((32,), jnp.int32),
        ]

    scratch = walk_scratch(14, 8, 4)
    first = pl.pallas_call(
        first_kernel, in_specs=[HBM] * 2 + [VMEM] * 7, out_specs=[VMEM] * 4,
        out_shape=[
            struct((8, 8, 256), f32), struct((8, 144, 256), f32),
            struct((8, 256, 128), bf16), struct((1024, DOUT // 2), bf16),
        ],
        scratch_shapes=[pltpu.VMEM((256, 1024), bf16)] + scratch[:1] + scratch[2:]
        + [pltpu.SemaphoreType.DMA((NW + 1,))],
        compiler_params=params(14), name="first",
        cost_estimate=estimate(4 * 10 ** 9, 1 << 20),
    )
    maxima, acc, tiles, weight_a = first(
        in_hbm(queries), in_hbm(out_weight), own, *xs, *ys
    )

    halves = [struct((64, DOUT // 2), bf16)] * 2

    def last(chunk, acc, *w_hbm):
        outs = halves + [struct((128, 1024), bf16)]
        scratch = [pltpu.VMEM((4, 144, 256), f32)] + walk_scratch(18, 4, 2)
        if w_hbm:
            outs = outs + [struct((1024, DOUT // 2), bf16)]
            scratch = scratch + [pltpu.SemaphoreType.DMA((NW,))]
        return pl.pallas_call(
            functools.partial(last_kernel, chunk),
            in_specs=[SMEM] + [VMEM] * 11 + [HBM] * len(w_hbm),
            out_specs=[VMEM] * len(outs), out_shape=outs, scratch_shapes=scratch,
            compiler_params=params(14),
            cost_estimate=estimate(5 * 10 ** 9, 1 << 20),
        )(index, tiles, own, *fa, *fb, maxima, acc, weight_a, *w_hbm)

    def rest(merged, weight):
        return pl.pallas_call(
            project, in_specs=[VMEM] * 2, out_specs=[VMEM] * 2, out_shape=halves,
            compiler_params=params(6), name="rest", cost_estimate=estimate(10 ** 9, 1 << 20),
        )(merged, weight)

    def call(kernel, rows, columns, *blocks):
        return pl.pallas_call(
            kernel, in_specs=[VMEM] * len(blocks), out_specs=[VMEM] * len(rows),
            out_shape=[struct((r, columns), bf16) for r in rows],
            compiler_params=params(6), cost_estimate=estimate(10 ** 6, 1 << 20),
        )(*blocks)

    def swap(block):
        return lax.ppermute(block, "tp", swap_route())

    def step(pairing, block):
        return lax.ppermute(block, "tp", step_route(pairing))

    def pair(half, keep, got):
        kernel = functools.partial(pair_kernel, half)
        return call(kernel, (32, 32), DOUT // 2, keep, got)

    def chunk_parts(chunk, acc, *w_hbm):
        keep_a, send_a, merged, *w_next = last(chunk, acc, *w_hbm)
        got_a = swap(send_a)
        w_half = w_next[0] if w_next else weight_b
        keep_b, send_b = rest(merged, w_half)
        got_b = swap(send_b)
        stay_a, out_a = pair(0, keep_a, got_a)
        in_a = step(0, out_a)
        stay_b, out_b = pair(1, keep_b, got_b)
        in_b = step(1, out_b)
        return stay_a, in_a, stay_b, in_b, out_b, w_half

    def second_step(half, stay, got):
        mine, out = call(fold_kernel, (16, 16), DOUT // 2, stay, got)
        return mine, step(1 - half, out)

    *early, out_b0, weight_b = chunk_parts(0, acc, in_hbm(out_weight))
    out_b0, acc = lax.optimization_barrier((out_b0, acc))
    *late, out_b1, _ = chunk_parts(1, acc)
    *early, out_b1 = lax.optimization_barrier((*early, out_b1))
    blocks = []
    for stay_a, in_a, stay_b, in_b in (early, late):
        blocks += second_step(0, stay_a, in_a)
        blocks += second_step(1, stay_b, in_b)
    return call(final_kernel, (32,), DOUT, *blocks)[0]


def solution(mesh):
    return jax.shard_map(
        on_device,
        mesh=mesh,
        in_specs=(P("ctx", "tp"), P("ctx", "tp"), P("ctx", "tp"), P("ctx"), P("tp", None)),
        out_specs=P(("ctx", "tp"), None),
        check_vma=False,
    )
```

```python
import functools
import math

import jax
import jax.numpy as jnp
from jax import lax
from jax.experimental import pallas as pl
from jax.experimental.pallas import tpu as pltpu
from jax.sharding import PartitionSpec as P


HD = 128
SPAN = 128
HEADS = 8
SLICE = 8
CHUNKS = ((0, 1, 2), (3,))
PACK = 272
LOG_SCALE = HD ** -0.5 * math.log2(math.e)
NEG = -1e30
NX = 4
NZ = 4
NCORE = 2
DOUT = 8192
NCOL = 8
GROUP = 4
HEADROOM = 60.0
NW = 4
HOPS = (1, 3, 2)


VMEM = pl.BlockSpec(memory_space=pltpu.VMEM)
SMEM = pl.BlockSpec(memory_space=pltpu.SMEM)
HBM = pl.BlockSpec(memory_space=pltpu.HBM)


def struct(shape, dtype):
    return jax.ShapeDtypeStruct(shape, dtype)


def pack_kernel(pos_hbm, k_hbm, v_hbm, out_ref, pos_ref, k_ref, v_ref, sems):
    copies = [
        pltpu.make_async_copy(src, dst, sems.at[i])
        for i, (src, dst) in enumerate(((v_hbm, v_ref), (k_hbm, k_ref), (pos_hbm, pos_ref)))
    ]
    for copy in copies:
        copy.start()
    for copy in copies:
        copy.wait()
    for s in range(2):
        rows = slice(s * SPAN, (s + 1) * SPAN)
        span = (pos_ref[s * SPAN] // SPAN).astype(jnp.float32)
        base = s * PACK
        out_ref[base:base + 128] = k_ref[rows, :]
        out_ref[base + 128:base + 256] = v_ref[rows, :].T
        ids = jnp.full((16, 128), span, jnp.float32).astype(jnp.bfloat16)
        out_ref[base + 256:base + PACK] = ids


def join_kernel(part, *refs):
    out_ref = refs[-1]
    for i, ref in enumerate(refs[:-1]):
        out_ref[i * PACK:(i + 1) * PACK] = ref[part * PACK:(part + 1) * PACK]


def query_tile(q_ref, s, j):
    pieces = []
    for h in range(HEADS):
        for t in range(4):
            row = s * SPAN + t * 32 + j * SLICE
            pieces.append(q_ref[row:row + SLICE, h * HD:(h + 1) * HD])
    return jnp.concatenate(pieces, axis=0)


def scores_of(kt, q):
    return lax.dot_general(kt, q, (((1,), (1,)), ((), ())), preferred_element_type=jnp.float32)


def weighted(vt, probs):
    return jnp.dot(vt, probs, preferred_element_type=jnp.float32)


def store_keys(kv_ref, blocks):
    for i, (ref, j) in enumerate(blocks):
        kv_ref[i, 0:256, :] = ref[j * PACK:j * PACK + 256, :]
        kv_ref[i, 256:PACK, :] = jnp.ones((16, 128), jnp.bfloat16)
    kv_ref[len(blocks)] = jnp.zeros((PACK, 128), jnp.bfloat16)


def span_id(ref, i):
    ids = ref[i * PACK + 256:(i + 1) * PACK, :].astype(jnp.float32)
    return jnp.max(ids).astype(jnp.int32)


def visible_list(list_ref, ids, limit):
    count = jnp.int32(0)
    for i, span in enumerate(ids):
        list_ref[count] = jnp.int32(i)
        count = count + jnp.where(span < limit, 1, 0)
    for i in range(GROUP):
        list_ref[count + i] = jnp.int32(len(ids))
    return count


def fast_walk(kv_ref, list_ref, count, queries, units, m_ref, peak_ref, acc_ref, probs):
    shifts = [m_ref[u][0:1, :] for u in units]

    def score(g, p_ref):
        slots = [list_ref[g * GROUP + i] for i in range(GROUP)]
        kt = jnp.concatenate([kv_ref[i, 0:128, :] for i in slots], axis=0)
        for n, u in enumerate(units):
            scores = scores_of(kt, queries[n])
            tiles = scores.reshape(GROUP * SPAN // 8, 8, 256)
            peak_ref[u] = jnp.maximum(peak_ref[u], jnp.max(tiles, axis=0))
            p_ref[n] = jnp.exp2((scores - shifts[n]) * LOG_SCALE).astype(jnp.bfloat16)

    def add(g, p_ref):
        slots = [list_ref[g * GROUP + i] for i in range(GROUP)]
        vt = jnp.concatenate([kv_ref[i, 128:PACK, :] for i in slots], axis=1)
        for n, u in enumerate(units):
            acc_ref[u] = acc_ref[u] + weighted(vt, p_ref[n])

    even, odd = probs
    groups = jnp.maximum((count + GROUP - 1) // GROUP, 1)
    score(0, even)

    def pair(i, carry):
        score(2 * i + 1, odd)
        add(2 * i, even)
        score(2 * i + 2, even)
        add(2 * i + 1, odd)
        return carry

    lax.fori_loop(0, (groups - 1) // 2, pair, 0)

    @pl.when(groups % 2 == 1)
    def _():
        add(groups - 1, even)

    @pl.when(groups % 2 == 0)
    def _():
        score(groups - 1, odd)
        add(groups - 2, even)
        add(groups - 1, odd)


def slow_walk(kv_ref, list_ref, count, queries, units, m_ref, acc_ref):
    def step(i, carry):
        slot = list_ref[i]
        for n, u in enumerate(units):
            scores = scores_of(kv_ref[slot, 0:128, :], queries[n])
            m_old = m_ref[u][0:1, :]
            m_new = jnp.maximum(m_old, jnp.max(scores, axis=0, keepdims=True))
            probs = jnp.exp2((scores - m_new) * LOG_SCALE).astype(jnp.bfloat16)
            scale = jnp.exp2((m_old - m_new) * LOG_SCALE)
            acc_ref[u] = acc_ref[u] * scale + weighted(kv_ref[slot, 128:PACK, :], probs)
            m_ref[u] = jnp.broadcast_to(m_new, (8, 256))
        return carry

    lax.fori_loop(0, count, step, 0)


def overshoot(peak_ref, m_ref, units):
    worst = peak_ref[units[0]] - m_ref[units[0]]
    for u in units[1:]:
        worst = jnp.maximum(worst, peak_ref[u] - m_ref[u])
    return jnp.max(worst) * LOG_SCALE > HEADROOM


def fetch_half(half, w_hbm, w_ref, sems):
    copies = []
    for j in range(NW):
        rows = pl.ds(j * (1024 // NW), 1024 // NW)
        columns = pl.ds(half * DOUT // 2, DOUT // 2)
        copies.append(pltpu.make_async_copy(w_hbm.at[rows, columns], w_ref.at[rows], sems.at[j]))
        copies[j].start()
    return copies


def first_kernel(q_hbm, w_hbm, own_ref, x1, x2, x3, y1, y2, y3, m_ref, acc_ref, tile_ref, w_ref,
                 q_ref, kv_ref, peak_ref, even_ref, odd_ref, list0, list1, sems):
    fetch_q = pltpu.make_async_copy(q_hbm, q_ref, sems.at[NW])
    fetch_q.start()
    fetch_w = fetch_half(0, w_hbm, w_ref, sems)
    blocks = [(ref, j) for ref in (own_ref, x1, x2, x3, y1, y2, y3) for j in range(2)]
    store_keys(kv_ref, blocks)
    ids = [span_id(ref, j) for ref, j in blocks]
    counts = [visible_list(ref, ids, ids[s]) for s, ref in enumerate((list0, list1))]
    lists = (list0, list1)
    fetch_q.wait()
    for s in range(2):
        for j in range(4):
            tile_ref[s * 4 + j] = query_tile(q_ref, s, j)
    units = [[s * 4 + j for j in range(4)] for s in range(2)]
    queries = [[tile_ref[u] for u in units[s]] for s in range(2)]

    def own_block():
        for s in range(2):
            for n, u in enumerate(units[s]):
                lane = lax.broadcasted_iota(jnp.int32, (SPAN, 256), 1) % 32
                row = (lane // SLICE) * 32 + lane % SLICE + n * SLICE
                scores = scores_of(kv_ref[s, 0:128, :], queries[s][n])
                key = lax.broadcasted_iota(jnp.int32, (SPAN, 256), 0)
                scores = jnp.where(key <= row, scores, NEG)
                m_new = jnp.max(scores, axis=0, keepdims=True)
                probs = jnp.exp2((scores - m_new) * LOG_SCALE).astype(jnp.bfloat16)
                acc_ref[u] = weighted(kv_ref[s, 128:PACK, :], probs)
                m_ref[u] = jnp.broadcast_to(m_new, (8, 256))

    own_block()
    peak_ref[...] = m_ref[...]
    for s in range(2):
        fast_walk(kv_ref, lists[s], counts[s], queries[s], units[s], m_ref, peak_ref, acc_ref,
                  (even_ref, odd_ref))

    @pl.when(overshoot(peak_ref, m_ref, units[0] + units[1]))
    def _():
        own_block()
        for s in range(2):
            slow_walk(kv_ref, lists[s], counts[s], queries[s], units[s], m_ref, acc_ref)

    for copy in fetch_w:
        copy.wait()


def rest_of_attention(chunk, tile_ref, own_ref, far, m_in, acc_in, kv_ref, m_ref, peak_ref,
                      acc_ref, even_ref, odd_ref, lists):
    blocks = [(ref, j) for ref in far for j in range(3)]
    store_keys(kv_ref, blocks)
    ids = [span_id(ref, j) for ref, j in blocks]
    counts = [visible_list(lists[s], ids, span_id(own_ref, s)) for s in range(2)]
    slices = CHUNKS[chunk]
    width = len(slices)
    queries = [[tile_ref[s * 4 + j] for j in slices] for s in range(2)]
    units = [[s * width + n for n in range(width)] for s in range(2)]

    def reset():
        for s in range(2):
            for n, j in enumerate(slices):
                m_ref[s * width + n] = m_in[s * 4 + j]
                acc_ref[s * width + n] = acc_in[s * 4 + j]

    reset()
    peak_ref[...] = m_ref[...]
    for s in range(2):
        fast_walk(kv_ref, lists[s], counts[s], queries[s], units[s], m_ref, peak_ref, acc_ref,
                  (even_ref, odd_ref))

    @pl.when(overshoot(peak_ref, m_ref, range(2 * width)))
    def _():
        reset()
        for s in range(2):
            slow_walk(kv_ref, lists[s], counts[s], queries[s], units[s], m_ref, acc_ref)


def place_of(z_to, core_to, z, core):
    slot = jnp.where((z ^ 1) == z_to, 2, 1)
    slot = jnp.where(z_to == z, 0, jnp.where((z_to + 2) % NZ == z, 3, slot))
    return (core_to ^ core) * NZ + slot


def finish(acc_ref, width, index_ref, merged_ref):
    z, core = index_ref[0] // NCORE, index_ref[0] % NCORE
    for s in range(2):
        starts = []
        for t in range(4):
            owner = s * 4 + t
            place = place_of(owner // NCORE, owner % NCORE, z, core)
            starts.append(pl.multiple_of(place * (width * SLICE), SLICE))
        for n in range(width):
            acc = acc_ref[s * width + n]
            o = acc[:128] * (1.0 / acc[128:129])
            for half in range(2):
                rows = o[:, half * 128:(half + 1) * 128].T.astype(jnp.bfloat16)
                for i in range(4):
                    columns = slice((half * 4 + i) * HD, (half * 4 + i + 1) * HD)
                    for t in range(4):
                        at = i * 32 + t * SLICE
                        where = pl.ds(starts[t] + n * SLICE, SLICE)
                        merged_ref[where, columns] = rows[at:at + SLICE]


def project(merged_ref, w_ref, keep_ref, send_ref):
    cols = DOUT // NCOL
    for j in range(NCOL // 2):
        at = slice(j * cols, (j + 1) * cols)
        part = jnp.dot(merged_ref[...], w_ref[:, at], preferred_element_type=jnp.float32)
        part = part.astype(jnp.bfloat16)
        rows = part.shape[0] // 2
        keep_ref[:, at] = part[:rows]
        send_ref[:, at] = part[rows:]


def last_kernel(chunk, index_ref, tile_ref, own_ref, f1, f2, f3, f4, f5, f6, m_in, acc_in, w_ref,
                *refs):
    if chunk == 0:
        w_hbm, w_next, sems = refs[0], refs[4], refs[-1]
        refs = refs[1:4] + refs[5:-1]
        fetch_w = fetch_half(1, w_hbm, w_next, sems)
    (keep_ref, send_ref, merged_ref, acc_ref, kv_ref, m_ref, peak_ref, even_ref, odd_ref,
     list0, list1) = refs
    rest_of_attention(chunk, tile_ref, own_ref, (f1, f2, f3, f4, f5, f6), m_in, acc_in,
                      kv_ref, m_ref, peak_ref, acc_ref, even_ref, odd_ref, (list0, list1))
    finish(acc_ref, len(CHUNKS[chunk]), index_ref, merged_ref)
    project(merged_ref, w_ref, keep_ref, send_ref)
    if chunk == 0:
        for copy in fetch_w:
            copy.wait()


def pair_kernel(half, keep_ref, got_ref, stay_ref, send_ref):
    stay, send = ((0, 1), (2, 3)) if half == 0 else ((0, 2), (1, 3))
    size = keep_ref.shape[0] // NZ
    for out_ref, slots in ((stay_ref, stay), (send_ref, send)):
        for i, slot in enumerate(slots):
            rows = slice(slot * size, (slot + 1) * size)
            total = keep_ref[rows].astype(jnp.float32) + got_ref[rows]
            out_ref[i * size:(i + 1) * size] = total.astype(jnp.bfloat16)


def fold_kernel(stay_ref, got_ref, mine_ref, send_ref):
    total = (stay_ref[...].astype(jnp.float32) + got_ref[...]).astype(jnp.bfloat16)
    size = total.shape[0] // 2
    mine_ref[...] = total[:size]
    send_ref[...] = total[size:]


def final_kernel(*refs):
    out_ref = refs[-1]
    for i in range(4):
        chunk, half = i // 2, i % 2
        total = refs[2 * i][...].astype(jnp.float32) + refs[2 * i + 1][...]
        columns = slice(half * DOUT // 2, (half + 1) * DOUT // 2)
        rows = slice(CHUNKS[chunk][0] * SLICE, (CHUNKS[chunk][-1] + 1) * SLICE)
        out_ref[rows, columns] = total.astype(jnp.bfloat16)


def in_hbm(array):
    return pltpu.with_memory_space_constraint(array, pltpu.HBM)


def params(mib):
    return pltpu.CompilerParams(vmem_limit_bytes=mib << 20)


def estimate(flops, traffic):
    return pl.CostEstimate(flops=flops, bytes_accessed=traffic, transcendentals=0)


def ctx_route(dx, dy):
    return [
        (x * NX + y, ((x + dx) % NX) * NX + (y + dy) % NX)
        for x in range(NX) for y in range(NX)
    ]


def swap_route():
    return [(t, t ^ 1) for t in range(NZ * NCORE)]


def step_route(pairing):
    return [
        (z * NCORE + c, ((((z + pairing) ^ 1) - pairing) % NZ) * NCORE + c)
        for z in range(NZ) for c in range(NCORE)
    ]


def on_device(queries, keys, values, positions, out_weight):
    bf16, f32 = jnp.bfloat16, jnp.float32
    index = lax.axis_index("tp").reshape(1)

    own = pl.pallas_call(
        pack_kernel, in_specs=[HBM] * 3, out_specs=VMEM, out_shape=struct((2 * PACK, HD), bf16),
        name="pack", compiler_params=params(2),
        scratch_shapes=[
            pltpu.SMEM((2 * SPAN,), jnp.int32), pltpu.VMEM((2 * SPAN, HD), bf16),
            pltpu.VMEM((2 * SPAN, HD), bf16), pltpu.SemaphoreType.DMA((3,)),
        ],
    )(in_hbm(positions), in_hbm(keys), in_hbm(values))

    def shifts(block, dx, dy):
        moved = []
        for d in HOPS:
            moved.append(lax.ppermute(block, "ctx", ctx_route(dx * d, dy * d)))
        return moved

    def join(part, *blocks):
        return pl.pallas_call(
            functools.partial(join_kernel, part), in_specs=[VMEM] * len(blocks), out_specs=VMEM,
            out_shape=struct((len(blocks) * PACK, HD), bf16), name="join",
            compiler_params=params(2),
        )(*blocks)

    ys = shifts(own, 0, 1)
    xs = shifts(own, 1, 0)
    column = join(1, *ys)
    fb = shifts(column, 1, 0)
    fa = shifts(join(0, *xs), 0, 1)

    def walk_scratch(slots, units, width):
        return [
            pltpu.VMEM((slots + 1, PACK, 128), bf16),
            pltpu.VMEM((units, 8, 256), f32),
            pltpu.VMEM((units, 8, 256), f32),
            pltpu.VMEM((width, GROUP * SPAN, 256), bf16),
            pltpu.VMEM((width, GROUP * SPAN, 256), bf16),
            pltpu.SMEM((32,), jnp.int32),
            pltpu.SMEM((32,), jnp.int32),
        ]

    scratch = walk_scratch(14, 8, 4)
    first = pl.pallas_call(
        first_kernel, in_specs=[HBM] * 2 + [VMEM] * 7, out_specs=[VMEM] * 4,
        out_shape=[
            struct((8, 8, 256), f32), struct((8, 144, 256), f32),
            struct((8, 256, 128), bf16), struct((1024, DOUT // 2), bf16),
        ],
        scratch_shapes=[pltpu.VMEM((256, 1024), bf16)] + scratch[:1] + scratch[2:]
        + [pltpu.SemaphoreType.DMA((NW + 1,))],
        compiler_params=params(14), name="first",
        cost_estimate=estimate(4 * 10 ** 9, 1 << 20),
    )
    maxima, acc, tiles, weight_a = first(
        in_hbm(queries), in_hbm(out_weight), own, *xs, *ys
    )

    def halves(chunk):
        return [struct((NZ * SLICE * len(CHUNKS[chunk]), DOUT // 2), bf16)] * 2

    def last(chunk, acc, *w_hbm):
        width = len(CHUNKS[chunk])
        rows = 2 * NZ * SLICE * width
        outs = halves(chunk) + [struct((rows, 1024), bf16)]
        scratch = [pltpu.VMEM((2 * width, 144, 256), f32)] + walk_scratch(18, 2 * width, width)
        if w_hbm:
            outs = outs + [struct((1024, DOUT // 2), bf16)]
            scratch = scratch + [pltpu.SemaphoreType.DMA((NW,))]
        return pl.pallas_call(
            functools.partial(last_kernel, chunk),
            in_specs=[SMEM] + [VMEM] * 11 + [HBM] * len(w_hbm),
            out_specs=[VMEM] * len(outs), out_shape=outs, scratch_shapes=scratch,
            compiler_params=params(14),
            cost_estimate=estimate(5 * 10 ** 9, 1 << 20),
        )(index, tiles, own, *fa, *fb, maxima, acc, weight_a, *w_hbm)

    def rest(chunk, merged, weight):
        return pl.pallas_call(
            project, in_specs=[VMEM] * 2, out_specs=[VMEM] * 2, out_shape=halves(chunk),
            compiler_params=params(8), cost_estimate=estimate(10 ** 9, 1 << 20),
        )(merged, weight)

    def call(kernel, rows, columns, *blocks):
        return pl.pallas_call(
            kernel, in_specs=[VMEM] * len(blocks), out_specs=[VMEM] * len(rows),
            out_shape=[struct((r, columns), bf16) for r in rows],
            compiler_params=params(6), cost_estimate=estimate(10 ** 6, 1 << 20),
        )(*blocks)

    def swap(block):
        return lax.ppermute(block, "tp", swap_route())

    def step(pairing, block):
        return lax.ppermute(block, "tp", step_route(pairing))

    def pair(half, keep, got):
        kernel = functools.partial(pair_kernel, half)
        rows = keep.shape[0] // 2
        return call(kernel, (rows, rows), DOUT // 2, keep, got)

    def chunk_parts(chunk, acc, *w_hbm):
        keep_a, send_a, merged, *w_next = last(chunk, acc, *w_hbm)
        got_a = swap(send_a)
        w_half = w_next[0] if w_next else weight_b
        keep_b, send_b = rest(chunk, merged, w_half)
        got_b = swap(send_b)
        stay_a, out_a = pair(0, keep_a, got_a)
        in_a = step(0, out_a)
        stay_b, out_b = pair(1, keep_b, got_b)
        in_b = step(1, out_b)
        return stay_a, in_a, stay_b, in_b, out_b, w_half

    def second_step(half, stay, got):
        rows = stay.shape[0] // 2
        mine, out = call(fold_kernel, (rows, rows), DOUT // 2, stay, got)
        return mine, step(1 - half, out)

    *early, out_b0, weight_b = chunk_parts(0, acc, in_hbm(out_weight))
    out_b0, acc = lax.optimization_barrier((out_b0, acc))
    *late, out_b1, _ = chunk_parts(1, acc)
    *early, out_b1 = lax.optimization_barrier((*early, out_b1))
    blocks = []
    for stay_a, in_a, stay_b, in_b in (early, late):
        blocks += second_step(0, stay_a, in_a)
        blocks += second_step(1, stay_b, in_b)
    return call(final_kernel, (32,), DOUT, *blocks)[0]


def solution(mesh):
    return jax.shard_map(
        on_device,
        mesh=mesh,
        in_specs=(P("ctx", "tp"), P("ctx", "tp"), P("ctx", "tp"), P("ctx"), P("tp", None)),
        out_specs=P(("ctx", "tp"), None),
        check_vma=False,
    )
```

```python
import functools
import math

import jax
import jax.numpy as jnp
from jax import lax
from jax.experimental import pallas as pl
from jax.experimental.pallas import tpu as pltpu
from jax.sharding import PartitionSpec as P


HD = 128
SPAN = 128
HEADS = 8
SLICE = 8
WIDTH = 4
QUARTERS = 4
PACK = 272
LOG_SCALE = HD ** -0.5 * math.log2(math.e)
NEG = -1e30
NX = 4
NZ = 4
NCORE = 2
DOUT = 8192
QCOLS = DOUT // QUARTERS
GROUP = 4
HEADROOM = 60.0
TILE = 1024
NW = 4
HOPS = (1, 3, 2)


VMEM = pl.BlockSpec(memory_space=pltpu.VMEM)
SMEM = pl.BlockSpec(memory_space=pltpu.SMEM)
HBM = pl.BlockSpec(memory_space=pltpu.HBM)


def struct(shape, dtype):
    return jax.ShapeDtypeStruct(shape, dtype)


def pack_kernel(pos_hbm, k_hbm, v_hbm, out_ref, pos_ref, k_ref, v_ref, sems):
    copies = [
        pltpu.make_async_copy(src, dst, sems.at[i])
        for i, (src, dst) in enumerate(((v_hbm, v_ref), (k_hbm, k_ref), (pos_hbm, pos_ref)))
    ]
    for copy in copies:
        copy.start()
    for copy in copies:
        copy.wait()
    for s in range(2):
        rows = slice(s * SPAN, (s + 1) * SPAN)
        span = (pos_ref[s * SPAN] // SPAN).astype(jnp.float32)
        base = s * PACK
        out_ref[base:base + 128] = k_ref[rows, :]
        out_ref[base + 128:base + 256] = v_ref[rows, :].T
        ids = jnp.full((16, 128), span, jnp.float32).astype(jnp.bfloat16)
        out_ref[base + 256:base + PACK] = ids


def join_kernel(part, *refs):
    out_ref = refs[-1]
    for i, ref in enumerate(refs[:-1]):
        out_ref[i * PACK:(i + 1) * PACK] = ref[part * PACK:(part + 1) * PACK]


def query_tile(q_ref, s, j):
    pieces = []
    for h in range(HEADS):
        for t in range(4):
            row = s * SPAN + t * 32 + j * SLICE
            pieces.append(q_ref[row:row + SLICE, h * HD:(h + 1) * HD])
    return jnp.concatenate(pieces, axis=0)


def scores_of(kt, q):
    return lax.dot_general(kt, q, (((1,), (1,)), ((), ())), preferred_element_type=jnp.float32)


def weighted(vt, probs):
    return jnp.dot(vt, probs, preferred_element_type=jnp.float32)


def store_keys(kv_ref, blocks):
    for i, (ref, j) in enumerate(blocks):
        kv_ref[i, 0:256, :] = ref[j * PACK:j * PACK + 256, :]
        kv_ref[i, 256:PACK, :] = jnp.ones((16, 128), jnp.bfloat16)
    kv_ref[len(blocks)] = jnp.zeros((PACK, 128), jnp.bfloat16)


def span_id(ref, i):
    ids = ref[i * PACK + 256:(i + 1) * PACK, :].astype(jnp.float32)
    return jnp.max(ids).astype(jnp.int32)


def visible_list(list_ref, ids, limit):
    count = jnp.int32(0)
    for i, span in enumerate(ids):
        list_ref[count] = jnp.int32(i)
        count = count + jnp.where(span < limit, 1, 0)
    for i in range(GROUP):
        list_ref[count + i] = jnp.int32(len(ids))
    return count


def fast_walk(kv_ref, list_ref, count, queries, units, m_ref, peak_ref, acc_ref, probs):
    shifts = [m_ref[u][0:1, :] for u in units]

    def score(g, p_ref):
        slots = [list_ref[g * GROUP + i] for i in range(GROUP)]
        kt = jnp.concatenate([kv_ref[i, 0:128, :] for i in slots], axis=0)
        for n, u in enumerate(units):
            scores = scores_of(kt, queries[n])
            tiles = scores.reshape(GROUP * SPAN // 8, 8, 256)
            peak_ref[u] = jnp.maximum(peak_ref[u], jnp.max(tiles, axis=0))
            p_ref[n] = jnp.exp2((scores - shifts[n]) * LOG_SCALE).astype(jnp.bfloat16)

    def add(g, p_ref):
        slots = [list_ref[g * GROUP + i] for i in range(GROUP)]
        vt = jnp.concatenate([kv_ref[i, 128:PACK, :] for i in slots], axis=1)
        for n, u in enumerate(units):
            acc_ref[u] = acc_ref[u] + weighted(vt, p_ref[n])

    even, odd = probs
    groups = jnp.maximum((count + GROUP - 1) // GROUP, 1)
    score(0, even)

    def pair(i, carry):
        score(2 * i + 1, odd)
        add(2 * i, even)
        score(2 * i + 2, even)
        add(2 * i + 1, odd)
        return carry

    lax.fori_loop(0, (groups - 1) // 2, pair, 0)

    @pl.when(groups % 2 == 1)
    def _():
        add(groups - 1, even)

    @pl.when(groups % 2 == 0)
    def _():
        score(groups - 1, odd)
        add(groups - 2, even)
        add(groups - 1, odd)


def slow_walk(kv_ref, list_ref, count, queries, units, m_ref, acc_ref):
    def step(i, carry):
        slot = list_ref[i]
        for n, u in enumerate(units):
            scores = scores_of(kv_ref[slot, 0:128, :], queries[n])
            m_old = m_ref[u][0:1, :]
            m_new = jnp.maximum(m_old, jnp.max(scores, axis=0, keepdims=True))
            probs = jnp.exp2((scores - m_new) * LOG_SCALE).astype(jnp.bfloat16)
            scale = jnp.exp2((m_old - m_new) * LOG_SCALE)
            acc_ref[u] = acc_ref[u] * scale + weighted(kv_ref[slot, 128:PACK, :], probs)
            m_ref[u] = jnp.broadcast_to(m_new, (8, 256))
        return carry

    lax.fori_loop(0, count, step, 0)


def overshoot(peak_ref, m_ref, units):
    worst = peak_ref[units[0]] - m_ref[units[0]]
    for u in units[1:]:
        worst = jnp.maximum(worst, peak_ref[u] - m_ref[u])
    return jnp.max(worst) * LOG_SCALE > HEADROOM


def fetch_half(half, w_hbm, w_ref, sems):
    copies = []
    for j in range(NW):
        rows = pl.ds(j * (1024 // NW), 1024 // NW)
        columns = pl.ds(half * DOUT // 2, DOUT // 2)
        copies.append(pltpu.make_async_copy(w_hbm.at[rows, columns], w_ref.at[rows], sems.at[j]))
        copies[j].start()
    return copies


def first_kernel(q_hbm, w_hbm, own_ref, x1, x2, x3, y1, y2, y3, m_ref, acc_ref, tile_ref, w_ref,
                 q_ref, kv_ref, peak_ref, even_ref, odd_ref, list0, list1, sems):
    fetch_q = pltpu.make_async_copy(q_hbm, q_ref, sems.at[NW])
    fetch_q.start()
    fetch_w = fetch_half(0, w_hbm, w_ref, sems)
    blocks = [(ref, j) for ref in (own_ref, x1, x2, x3, y1, y2, y3) for j in range(2)]
    store_keys(kv_ref, blocks)
    ids = [span_id(ref, j) for ref, j in blocks]
    counts = [visible_list(ref, ids, ids[s]) for s, ref in enumerate((list0, list1))]
    lists = (list0, list1)
    fetch_q.wait()
    for s in range(2):
        for j in range(4):
            tile_ref[s * 4 + j] = query_tile(q_ref, s, j)
    units = [[s * 4 + j for j in range(4)] for s in range(2)]
    queries = [[tile_ref[u] for u in units[s]] for s in range(2)]

    def own_block():
        for s in range(2):
            for n, u in enumerate(units[s]):
                lane = lax.broadcasted_iota(jnp.int32, (SPAN, 256), 1) % 32
                row = (lane // SLICE) * 32 + lane % SLICE + n * SLICE
                scores = scores_of(kv_ref[s, 0:128, :], queries[s][n])
                key = lax.broadcasted_iota(jnp.int32, (SPAN, 256), 0)
                scores = jnp.where(key <= row, scores, NEG)
                m_new = jnp.max(scores, axis=0, keepdims=True)
                probs = jnp.exp2((scores - m_new) * LOG_SCALE).astype(jnp.bfloat16)
                acc_ref[u] = weighted(kv_ref[s, 128:PACK, :], probs)
                m_ref[u] = jnp.broadcast_to(m_new, (8, 256))

    own_block()
    peak_ref[...] = m_ref[...]
    for s in range(2):
        fast_walk(kv_ref, lists[s], counts[s], queries[s], units[s], m_ref, peak_ref, acc_ref,
                  (even_ref, odd_ref))

    @pl.when(overshoot(peak_ref, m_ref, units[0] + units[1]))
    def _():
        own_block()
        for s in range(2):
            slow_walk(kv_ref, lists[s], counts[s], queries[s], units[s], m_ref, acc_ref)

    for copy in fetch_w:
        copy.wait()


def rest_of_attention(tile_ref, own_ref, far, m_in, acc_in, kv_ref, m_ref, peak_ref,
                      acc_ref, even_ref, odd_ref, lists):
    blocks = [(ref, j) for ref in far for j in range(3)]
    store_keys(kv_ref, blocks)
    ids = [span_id(ref, j) for ref, j in blocks]
    counts = [visible_list(lists[s], ids, span_id(own_ref, s)) for s in range(2)]
    units = [[s * WIDTH + n for n in range(WIDTH)] for s in range(2)]
    queries = [[tile_ref[u] for u in units[s]] for s in range(2)]

    def reset():
        m_ref[...] = m_in[...]
        acc_ref[...] = acc_in[...]

    reset()
    peak_ref[...] = m_ref[...]
    for s in range(2):
        fast_walk(kv_ref, lists[s], counts[s], queries[s], units[s], m_ref, peak_ref, acc_ref,
                  (even_ref, odd_ref))

    @pl.when(overshoot(peak_ref, m_ref, range(2 * WIDTH)))
    def _():
        reset()
        for s in range(2):
            slow_walk(kv_ref, lists[s], counts[s], queries[s], units[s], m_ref, acc_ref)


def place_of(z_to, core_to, z, core):
    slot = jnp.where((z ^ 1) == z_to, 2, 1)
    slot = jnp.where(z_to == z, 0, jnp.where((z_to + 2) % NZ == z, 3, slot))
    return (core_to ^ core) * NZ + slot


def finish(acc_ref, index_ref, merged_ref):
    z, core = index_ref[0] // NCORE, index_ref[0] % NCORE
    for s in range(2):
        starts = []
        for t in range(4):
            owner = s * 4 + t
            place = place_of(owner // NCORE, owner % NCORE, z, core)
            starts.append(pl.multiple_of(place * (WIDTH * SLICE), SLICE))
        for n in range(WIDTH):
            acc = acc_ref[s * WIDTH + n]
            o = acc[:128] * (1.0 / acc[128:129])
            for half in range(2):
                rows = o[:, half * 128:(half + 1) * 128].T.astype(jnp.bfloat16)
                for i in range(4):
                    columns = slice((half * 4 + i) * HD, (half * 4 + i + 1) * HD)
                    for t in range(4):
                        at = i * 32 + t * SLICE
                        where = pl.ds(starts[t] + n * SLICE, SLICE)
                        merged_ref[where, columns] = rows[at:at + SLICE]


def project(quarter, merged_ref, w_ref, keep_ref, send_ref):
    rows = keep_ref.shape[0]
    for j in range(QCOLS // TILE):
        at = slice(j * TILE, (j + 1) * TILE)
        start = quarter % 2 * QCOLS + j * TILE
        part = jnp.dot(
            merged_ref[...], w_ref[:, start:start + TILE], preferred_element_type=jnp.float32
        ).astype(jnp.bfloat16)
        keep_ref[:, at] = part[:rows]
        send_ref[:, at] = part[rows:]


def last_kernel(index_ref, tile_ref, own_ref, f1, f2, f3, f4, f5, f6, m_in, acc_in, w_ref, w_hbm,
                keep_ref, send_ref, merged_ref, w_next, acc_ref, kv_ref, m_ref, peak_ref, even_ref,
                odd_ref, list0, list1, sems):
    fetch_w = fetch_half(1, w_hbm, w_next, sems)
    rest_of_attention(tile_ref, own_ref, (f1, f2, f3, f4, f5, f6), m_in, acc_in, kv_ref, m_ref,
                      peak_ref, acc_ref, even_ref, odd_ref, (list0, list1))
    finish(acc_ref, index_ref, merged_ref)
    project(0, merged_ref, w_ref, keep_ref, send_ref)
    for copy in fetch_w:
        copy.wait()


def pair_kernel(pairing, keep_ref, got_ref, stay_ref, send_ref):
    stay, send = ((0, 1), (2, 3)) if pairing == 0 else ((0, 2), (1, 3))
    size = keep_ref.shape[0] // NZ
    for out_ref, slots in ((stay_ref, stay), (send_ref, send)):
        for i, slot in enumerate(slots):
            rows = slice(slot * size, (slot + 1) * size)
            total = keep_ref[rows].astype(jnp.float32) + got_ref[rows]
            out_ref[i * size:(i + 1) * size] = total.astype(jnp.bfloat16)


def fold_kernel(stay_ref, got_ref, mine_ref, send_ref):
    total = (stay_ref[...].astype(jnp.float32) + got_ref[...]).astype(jnp.bfloat16)
    size = total.shape[0] // 2
    mine_ref[...] = total[:size]
    send_ref[...] = total[size:]


def final_kernel(*refs):
    out_ref = refs[-1]
    for q in range(QUARTERS):
        total = refs[2 * q][...].astype(jnp.float32) + refs[2 * q + 1][...]
        out_ref[:, q * QCOLS:(q + 1) * QCOLS] = total.astype(jnp.bfloat16)


def in_hbm(array):
    return pltpu.with_memory_space_constraint(array, pltpu.HBM)


def params(mib):
    return pltpu.CompilerParams(vmem_limit_bytes=mib << 20)


def estimate(flops, traffic):
    return pl.CostEstimate(flops=flops, bytes_accessed=traffic, transcendentals=0)


def ctx_route(dx, dy):
    return [
        (x * NX + y, ((x + dx) % NX) * NX + (y + dy) % NX)
        for x in range(NX) for y in range(NX)
    ]


def swap_route():
    return [(t, t ^ 1) for t in range(NZ * NCORE)]


def step_route(pairing):
    return [
        (z * NCORE + c, ((((z + pairing) ^ 1) - pairing) % NZ) * NCORE + c)
        for z in range(NZ) for c in range(NCORE)
    ]


def on_device(queries, keys, values, positions, out_weight):
    bf16, f32 = jnp.bfloat16, jnp.float32
    index = lax.axis_index("tp").reshape(1)

    own = pl.pallas_call(
        pack_kernel, in_specs=[HBM] * 3, out_specs=VMEM, out_shape=struct((2 * PACK, HD), bf16),
        name="pack", compiler_params=params(2),
        scratch_shapes=[
            pltpu.SMEM((2 * SPAN,), jnp.int32), pltpu.VMEM((2 * SPAN, HD), bf16),
            pltpu.VMEM((2 * SPAN, HD), bf16), pltpu.SemaphoreType.DMA((3,)),
        ],
    )(in_hbm(positions), in_hbm(keys), in_hbm(values))

    def shifts(block, dx, dy):
        moved = []
        for d in HOPS:
            moved.append(lax.ppermute(block, "ctx", ctx_route(dx * d, dy * d)))
        return moved

    def join(part, *blocks):
        return pl.pallas_call(
            functools.partial(join_kernel, part), in_specs=[VMEM] * len(blocks), out_specs=VMEM,
            out_shape=struct((len(blocks) * PACK, HD), bf16), name="join",
            compiler_params=params(2),
        )(*blocks)

    ys = shifts(own, 0, 1)
    xs = shifts(own, 1, 0)
    column = join(1, *ys)
    fb = shifts(column, 1, 0)
    fa = shifts(join(0, *xs), 0, 1)

    def walk_scratch(slots, units, width):
        return [
            pltpu.VMEM((slots + 1, PACK, 128), bf16),
            pltpu.VMEM((units, 8, 256), f32),
            pltpu.VMEM((units, 8, 256), f32),
            pltpu.VMEM((width, GROUP * SPAN, 256), bf16),
            pltpu.VMEM((width, GROUP * SPAN, 256), bf16),
            pltpu.SMEM((32,), jnp.int32),
            pltpu.SMEM((32,), jnp.int32),
        ]

    scratch = walk_scratch(14, 8, 4)
    first = pl.pallas_call(
        first_kernel, in_specs=[HBM] * 2 + [VMEM] * 7, out_specs=[VMEM] * 4,
        out_shape=[
            struct((8, 8, 256), f32), struct((8, 144, 256), f32),
            struct((8, 256, 128), bf16), struct((1024, DOUT // 2), bf16),
        ],
        scratch_shapes=[pltpu.VMEM((256, 1024), bf16)] + scratch[:1] + scratch[2:]
        + [pltpu.SemaphoreType.DMA((NW + 1,))],
        compiler_params=params(14), name="first",
        cost_estimate=estimate(4 * 10 ** 9, 1 << 20),
    )
    maxima, acc, tiles, weight_a = first(
        in_hbm(queries), in_hbm(out_weight), own, *xs, *ys
    )

    rows = NZ * WIDTH * SLICE
    piece = [struct((rows, QCOLS), bf16)] * 2
    scratch = walk_scratch(18, 2 * WIDTH, WIDTH)
    last = pl.pallas_call(
        last_kernel, in_specs=[SMEM] + [VMEM] * 11 + [HBM], out_specs=[VMEM] * 4,
        out_shape=piece + [struct((2 * rows, 1024), bf16), struct((1024, DOUT // 2), bf16)],
        scratch_shapes=[pltpu.VMEM((2 * WIDTH, 144, 256), f32)] + scratch
        + [pltpu.SemaphoreType.DMA((NW,))],
        compiler_params=params(16), name="last", cost_estimate=estimate(5 * 10 ** 9, 1 << 20),
    )

    def rest(quarter, merged, weight):
        return pl.pallas_call(
            functools.partial(project, quarter), in_specs=[VMEM] * 2, out_specs=[VMEM] * 2,
            out_shape=piece, compiler_params=params(8),
            cost_estimate=estimate(10 ** 9, 1 << 20),
        )(merged, weight)

    def call(kernel, rows, columns, *blocks):
        return pl.pallas_call(
            kernel, in_specs=[VMEM] * len(blocks), out_specs=[VMEM] * len(rows),
            out_shape=[struct((r, columns), bf16) for r in rows],
            compiler_params=params(6), cost_estimate=estimate(10 ** 6, 1 << 20),
        )(*blocks)

    def move(block, route):
        return lax.ppermute(block, "tp", route)

    keep, send, merged, weight_b = last(
        index, tiles, own, *fa, *fb, maxima, acc, weight_a, in_hbm(out_weight)
    )
    stays, blocks = [], []
    for q in range(QUARTERS):
        if q > 0:
            keep, send = rest(q, merged, weight_a if q < 2 else weight_b)
        got = move(send, swap_route())
        kernel = functools.partial(pair_kernel, q % 2)
        stay, out = call(kernel, (rows // 2,) * 2, QCOLS, keep, got)
        stays.append((stay, move(out, step_route(q % 2))))
    for q, (stay, got) in enumerate(stays):
        mine, out = call(fold_kernel, (rows // 4,) * 2, QCOLS, stay, got)
        blocks += [mine, move(out, step_route(1 - q % 2))]
    return call(final_kernel, (rows // 4,), DOUT, *blocks)[0]


def solution(mesh):
    return jax.shard_map(
        on_device,
        mesh=mesh,
        in_specs=(P("ctx", "tp"), P("ctx", "tp"), P("ctx", "tp"), P("ctx"), P("tp", None)),
        out_specs=P(("ctx", "tp"), None),
        check_vma=False,
    )
```

```python
import functools
import math

import jax
import jax.numpy as jnp
from jax import lax
from jax.experimental import pallas as pl
from jax.experimental.pallas import tpu as pltpu
from jax.sharding import PartitionSpec as P


HD = 128
SPAN = 128
HEADS = 8
SLICE = 8
WIDTH = 4
COLUMNS = (2048, 2048, 2560, 1536)
PACK = 264
SLOT = 272
LOG_SCALE = HD ** -0.5 * math.log2(math.e)
NEG = -1e30
NX = 4
NZ = 4
NCORE = 2
DOUT = 8192
STARTS_AT = (0, 2048, 4096, 6656)
GROUP = 4
HEADROOM = 60.0
TILE = 512
NW = 4
HOPS = (1, 3, 2)


VMEM = pl.BlockSpec(memory_space=pltpu.VMEM)
SMEM = pl.BlockSpec(memory_space=pltpu.SMEM)
HBM = pl.BlockSpec(memory_space=pltpu.HBM)


def struct(shape, dtype):
    return jax.ShapeDtypeStruct(shape, dtype)


def pack_kernel(pos_hbm, k_hbm, v_hbm, out_ref, pos_ref, k_ref, v_ref, sems):
    copies = [
        pltpu.make_async_copy(src, dst, sems.at[i])
        for i, (src, dst) in enumerate(((v_hbm, v_ref), (k_hbm, k_ref), (pos_hbm, pos_ref)))
    ]
    for copy in copies:
        copy.start()
    for copy in copies:
        copy.wait()
    for s in range(2):
        rows = slice(s * SPAN, (s + 1) * SPAN)
        span = (pos_ref[s * SPAN] // SPAN).astype(jnp.float32)
        base = s * PACK
        out_ref[base:base + 128] = k_ref[rows, :]
        out_ref[base + 128:base + 256] = v_ref[rows, :].T
        ids = jnp.full((PACK - 256, 128), span, jnp.float32).astype(jnp.bfloat16)
        out_ref[base + 256:base + PACK] = ids


def join_kernel(part, *refs):
    out_ref = refs[-1]
    for i, ref in enumerate(refs[:-1]):
        out_ref[i * PACK:(i + 1) * PACK] = ref[part * PACK:(part + 1) * PACK]


def query_tile(q_ref, s, j):
    pieces = []
    for h in range(HEADS):
        for t in range(4):
            row = s * SPAN + t * 32 + j * SLICE
            pieces.append(q_ref[row:row + SLICE, h * HD:(h + 1) * HD])
    return jnp.concatenate(pieces, axis=0)


def scores_of(kt, q):
    return lax.dot_general(kt, q, (((1,), (1,)), ((), ())), preferred_element_type=jnp.float32)


def weighted(vt, probs):
    return jnp.dot(vt, probs, preferred_element_type=jnp.float32)


def store_keys(kv_ref, blocks):
    for i, (ref, j) in enumerate(blocks):
        kv_ref[i, 0:256, :] = ref[j * PACK:j * PACK + 256, :]
        kv_ref[i, 256:SLOT, :] = jnp.ones((16, 128), jnp.bfloat16)
    kv_ref[len(blocks)] = jnp.zeros((SLOT, 128), jnp.bfloat16)


def span_id(ref, i):
    ids = ref[i * PACK + 256:(i + 1) * PACK, :].astype(jnp.float32)
    return jnp.max(ids).astype(jnp.int32)


def visible_list(list_ref, ids, limit):
    count = jnp.int32(0)
    for i, span in enumerate(ids):
        list_ref[count] = jnp.int32(i)
        count = count + jnp.where(span < limit, 1, 0)
    for i in range(GROUP):
        list_ref[count + i] = jnp.int32(len(ids))
    return count


def fast_walk(kv_ref, list_ref, count, queries, units, m_ref, peak_ref, acc_ref, probs):
    shifts = [m_ref[u][0:1, :] for u in units]

    def score(g, p_ref):
        slots = [list_ref[g * GROUP + i] for i in range(GROUP)]
        kt = jnp.concatenate([kv_ref[i, 0:128, :] for i in slots], axis=0)
        for n, u in enumerate(units):
            scores = scores_of(kt, queries[n])
            tiles = scores.reshape(GROUP * SPAN // 8, 8, 256)
            peak_ref[u] = jnp.maximum(peak_ref[u], jnp.max(tiles, axis=0))
            p_ref[n] = jnp.exp2((scores - shifts[n]) * LOG_SCALE).astype(jnp.bfloat16)

    def add(g, p_ref):
        slots = [list_ref[g * GROUP + i] for i in range(GROUP)]
        vt = jnp.concatenate([kv_ref[i, 128:SLOT, :] for i in slots], axis=1)
        for n, u in enumerate(units):
            acc_ref[u] = acc_ref[u] + weighted(vt, p_ref[n])

    even, odd = probs
    groups = jnp.maximum((count + GROUP - 1) // GROUP, 1)
    score(0, even)

    def pair(i, carry):
        score(2 * i + 1, odd)
        add(2 * i, even)
        score(2 * i + 2, even)
        add(2 * i + 1, odd)
        return carry

    lax.fori_loop(0, (groups - 1) // 2, pair, 0)

    @pl.when(groups % 2 == 1)
    def _():
        add(groups - 1, even)

    @pl.when(groups % 2 == 0)
    def _():
        score(groups - 1, odd)
        add(groups - 2, even)
        add(groups - 1, odd)


def slow_walk(kv_ref, list_ref, count, queries, units, m_ref, acc_ref):
    def step(i, carry):
        slot = list_ref[i]
        for n, u in enumerate(units):
            scores = scores_of(kv_ref[slot, 0:128, :], queries[n])
            m_old = m_ref[u][0:1, :]
            m_new = jnp.maximum(m_old, jnp.max(scores, axis=0, keepdims=True))
            probs = jnp.exp2((scores - m_new) * LOG_SCALE).astype(jnp.bfloat16)
            scale = jnp.exp2((m_old - m_new) * LOG_SCALE)
            acc_ref[u] = acc_ref[u] * scale + weighted(kv_ref[slot, 128:SLOT, :], probs)
            m_ref[u] = jnp.broadcast_to(m_new, (8, 256))
        return carry

    lax.fori_loop(0, count, step, 0)


def overshoot(peak_ref, m_ref, units):
    worst = peak_ref[units[0]] - m_ref[units[0]]
    for u in units[1:]:
        worst = jnp.maximum(worst, peak_ref[u] - m_ref[u])
    return jnp.max(worst) * LOG_SCALE > HEADROOM


def fetch_half(half, w_hbm, w_ref, sems):
    copies = []
    for j in range(NW):
        rows = pl.ds(j * (1024 // NW), 1024 // NW)
        columns = pl.ds(half * DOUT // 2, DOUT // 2)
        copies.append(pltpu.make_async_copy(w_hbm.at[rows, columns], w_ref.at[rows], sems.at[j]))
        copies[j].start()
    return copies


def first_kernel(q_hbm, w_hbm, own_ref, x1, x2, x3, y1, y2, y3, m_ref, acc_ref, tile_ref, w_ref,
                 q_ref, kv_ref, peak_ref, even_ref, odd_ref, list0, list1, sems):
    fetch_q = pltpu.make_async_copy(q_hbm, q_ref, sems.at[NW])
    fetch_q.start()
    fetch_w = fetch_half(0, w_hbm, w_ref, sems)
    blocks = [(ref, j) for ref in (own_ref, x1, x2, x3, y1, y2, y3) for j in range(2)]
    store_keys(kv_ref, blocks)
    ids = [span_id(ref, j) for ref, j in blocks]
    counts = [visible_list(ref, ids, ids[s]) for s, ref in enumerate((list0, list1))]
    lists = (list0, list1)
    fetch_q.wait()
    for s in range(2):
        for j in range(4):
            tile_ref[s * 4 + j] = query_tile(q_ref, s, j)
    units = [[s * 4 + j for j in range(4)] for s in range(2)]
    queries = [[tile_ref[u] for u in units[s]] for s in range(2)]

    def own_block():
        for s in range(2):
            for n, u in enumerate(units[s]):
                lane = lax.broadcasted_iota(jnp.int32, (SPAN, 256), 1) % 32
                row = (lane // SLICE) * 32 + lane % SLICE + n * SLICE
                scores = scores_of(kv_ref[s, 0:128, :], queries[s][n])
                key = lax.broadcasted_iota(jnp.int32, (SPAN, 256), 0)
                scores = jnp.where(key <= row, scores, NEG)
                m_new = jnp.max(scores, axis=0, keepdims=True)
                probs = jnp.exp2((scores - m_new) * LOG_SCALE).astype(jnp.bfloat16)
                acc_ref[u] = weighted(kv_ref[s, 128:SLOT, :], probs)
                m_ref[u] = jnp.broadcast_to(m_new, (8, 256))

    own_block()
    peak_ref[...] = m_ref[...]
    for s in range(2):
        fast_walk(kv_ref, lists[s], counts[s], queries[s], units[s], m_ref, peak_ref, acc_ref,
                  (even_ref, odd_ref))

    @pl.when(overshoot(peak_ref, m_ref, units[0] + units[1]))
    def _():
        own_block()
        for s in range(2):
            slow_walk(kv_ref, lists[s], counts[s], queries[s], units[s], m_ref, acc_ref)

    for copy in fetch_w:
        copy.wait()


def rest_of_attention(tile_ref, own_ref, far, m_in, acc_in, kv_ref, m_ref, peak_ref,
                      acc_ref, even_ref, odd_ref, lists):
    blocks = [(ref, j) for ref in far for j in range(3)]
    store_keys(kv_ref, blocks)
    ids = [span_id(ref, j) for ref, j in blocks]
    counts = [visible_list(lists[s], ids, span_id(own_ref, s)) for s in range(2)]
    units = [[s * WIDTH + n for n in range(WIDTH)] for s in range(2)]
    queries = [[tile_ref[u] for u in units[s]] for s in range(2)]

    def reset():
        m_ref[...] = m_in[...]
        acc_ref[...] = acc_in[...]

    reset()
    peak_ref[...] = m_ref[...]
    for s in range(2):
        fast_walk(kv_ref, lists[s], counts[s], queries[s], units[s], m_ref, peak_ref, acc_ref,
                  (even_ref, odd_ref))

    @pl.when(overshoot(peak_ref, m_ref, range(2 * WIDTH)))
    def _():
        reset()
        for s in range(2):
            slow_walk(kv_ref, lists[s], counts[s], queries[s], units[s], m_ref, acc_ref)


def place_of(z_to, core_to, z, core):
    slot = jnp.where((z ^ 1) == z_to, 2, 1)
    slot = jnp.where(z_to == z, 0, jnp.where((z_to + 2) % NZ == z, 3, slot))
    return (core_to ^ core) * NZ + slot


def finish(acc_ref, index_ref, merged_ref):
    z, core = index_ref[0] // NCORE, index_ref[0] % NCORE
    for s in range(2):
        starts = []
        for t in range(4):
            owner = s * 4 + t
            place = place_of(owner // NCORE, owner % NCORE, z, core)
            starts.append(pl.multiple_of(place * (WIDTH * SLICE), SLICE))
        for n in range(WIDTH):
            acc = acc_ref[s * WIDTH + n]
            o = acc[:128] * (1.0 / acc[128:129])
            for half in range(2):
                rows = o[:, half * 128:(half + 1) * 128].T.astype(jnp.bfloat16)
                for i in range(4):
                    columns = slice((half * 4 + i) * HD, (half * 4 + i + 1) * HD)
                    for t in range(4):
                        at = i * 32 + t * SLICE
                        where = pl.ds(starts[t] + n * SLICE, SLICE)
                        merged_ref[where, columns] = rows[at:at + SLICE]


def project(quarter, merged_ref, w_ref, keep_ref, send_ref):
    rows = keep_ref.shape[0]
    first = STARTS_AT[quarter] - quarter // 2 * (DOUT // 2)
    for j in range(COLUMNS[quarter] // TILE):
        at = slice(j * TILE, (j + 1) * TILE)
        w = w_ref[:, first + j * TILE:first + (j + 1) * TILE]
        part = jnp.dot(merged_ref[...], w, preferred_element_type=jnp.float32)
        part = part.astype(jnp.bfloat16)
        keep_ref[:, at] = part[:rows]
        send_ref[:, at] = part[rows:]


def last_kernel(index_ref, tile_ref, own_ref, f1, f2, f3, f4, f5, f6, m_in, acc_in, w_ref, w_hbm,
                keep_ref, send_ref, merged_ref, w_next, acc_ref, kv_ref, m_ref, peak_ref, even_ref,
                odd_ref, list0, list1, sems):
    fetch_w = fetch_half(1, w_hbm, w_next, sems)
    rest_of_attention(tile_ref, own_ref, (f1, f2, f3, f4, f5, f6), m_in, acc_in, kv_ref, m_ref,
                      peak_ref, acc_ref, even_ref, odd_ref, (list0, list1))
    finish(acc_ref, index_ref, merged_ref)
    project(0, merged_ref, w_ref, keep_ref, send_ref)
    for copy in fetch_w:
        copy.wait()


def pair_kernel(pairing, keep_ref, got_ref, stay_ref, send_ref):
    stay, send = ((0, 1), (2, 3)) if pairing == 0 else ((0, 2), (1, 3))
    size = keep_ref.shape[0] // NZ
    for out_ref, slots in ((stay_ref, stay), (send_ref, send)):
        for i, slot in enumerate(slots):
            rows = slice(slot * size, (slot + 1) * size)
            total = keep_ref[rows].astype(jnp.float32) + got_ref[rows]
            out_ref[i * size:(i + 1) * size] = total.astype(jnp.bfloat16)


def fold_kernel(stay_ref, got_ref, mine_ref, send_ref):
    total = (stay_ref[...].astype(jnp.float32) + got_ref[...]).astype(jnp.bfloat16)
    size = total.shape[0] // 2
    mine_ref[...] = total[:size]
    send_ref[...] = total[size:]


def final_kernel(*refs):
    out_ref = refs[-1]
    for q, (start, width) in enumerate(zip(STARTS_AT, COLUMNS)):
        total = refs[2 * q][...].astype(jnp.float32) + refs[2 * q + 1][...]
        out_ref[:, start:start + width] = total.astype(jnp.bfloat16)


def in_hbm(array):
    return pltpu.with_memory_space_constraint(array, pltpu.HBM)


def params(mib):
    return pltpu.CompilerParams(vmem_limit_bytes=mib << 20)


def estimate(flops, traffic):
    return pl.CostEstimate(flops=flops, bytes_accessed=traffic, transcendentals=0)


def ctx_route(dx, dy):
    return [
        (x * NX + y, ((x + dx) % NX) * NX + (y + dy) % NX)
        for x in range(NX) for y in range(NX)
    ]


def swap_route():
    return [(t, t ^ 1) for t in range(NZ * NCORE)]


def step_route(pairing):
    return [
        (z * NCORE + c, ((((z + pairing) ^ 1) - pairing) % NZ) * NCORE + c)
        for z in range(NZ) for c in range(NCORE)
    ]


def on_device(queries, keys, values, positions, out_weight):
    bf16, f32 = jnp.bfloat16, jnp.float32
    index = lax.axis_index("tp").reshape(1)

    own = pl.pallas_call(
        pack_kernel, in_specs=[HBM] * 3, out_specs=VMEM, out_shape=struct((2 * PACK, HD), bf16),
        name="pack", compiler_params=params(2),
        scratch_shapes=[
            pltpu.SMEM((2 * SPAN,), jnp.int32), pltpu.VMEM((2 * SPAN, HD), bf16),
            pltpu.VMEM((2 * SPAN, HD), bf16), pltpu.SemaphoreType.DMA((3,)),
        ],
    )(in_hbm(positions), in_hbm(keys), in_hbm(values))

    def shifts(block, dx, dy):
        moved = []
        for d in HOPS:
            moved.append(lax.ppermute(block, "ctx", ctx_route(dx * d, dy * d)))
        return moved

    def join(part, *blocks):
        return pl.pallas_call(
            functools.partial(join_kernel, part), in_specs=[VMEM] * len(blocks), out_specs=VMEM,
            out_shape=struct((len(blocks) * PACK, HD), bf16), name="join",
            compiler_params=params(2),
        )(*blocks)

    ys = shifts(own, 0, 1)
    xs = shifts(own, 1, 0)
    column = join(1, *ys)
    fb = shifts(column, 1, 0)
    fa = shifts(join(0, *xs), 0, 1)

    def walk_scratch(slots, units, width):
        return [
            pltpu.VMEM((slots + 1, SLOT, 128), bf16),
            pltpu.VMEM((units, 8, 256), f32),
            pltpu.VMEM((units, 8, 256), f32),
            pltpu.VMEM((width, GROUP * SPAN, 256), bf16),
            pltpu.VMEM((width, GROUP * SPAN, 256), bf16),
            pltpu.SMEM((32,), jnp.int32),
            pltpu.SMEM((32,), jnp.int32),
        ]

    scratch = walk_scratch(14, 8, 4)
    first = pl.pallas_call(
        first_kernel, in_specs=[HBM] * 2 + [VMEM] * 7, out_specs=[VMEM] * 4,
        out_shape=[
            struct((8, 8, 256), f32), struct((8, 144, 256), f32),
            struct((8, 256, 128), bf16), struct((1024, DOUT // 2), bf16),
        ],
        scratch_shapes=[pltpu.VMEM((256, 1024), bf16)] + scratch[:1] + scratch[2:]
        + [pltpu.SemaphoreType.DMA((NW + 1,))],
        compiler_params=params(14), name="first",
        cost_estimate=estimate(4 * 10 ** 9, 1 << 20),
    )
    maxima, acc, tiles, weight_a = first(
        in_hbm(queries), in_hbm(out_weight), own, *xs, *ys
    )

    rows = NZ * WIDTH * SLICE

    def piece(quarter):
        return [struct((rows, COLUMNS[quarter]), bf16)] * 2

    scratch = walk_scratch(18, 2 * WIDTH, WIDTH)
    last = pl.pallas_call(
        last_kernel, in_specs=[SMEM] + [VMEM] * 11 + [HBM], out_specs=[VMEM] * 4,
        out_shape=piece(0) + [struct((2 * rows, 1024), bf16), struct((1024, DOUT // 2), bf16)],
        scratch_shapes=[pltpu.VMEM((2 * WIDTH, 144, 256), f32)] + scratch
        + [pltpu.SemaphoreType.DMA((NW,))],
        compiler_params=params(16), name="last", cost_estimate=estimate(5 * 10 ** 9, 1 << 20),
    )

    def rest(quarter, merged, weight):
        return pl.pallas_call(
            functools.partial(project, quarter), in_specs=[VMEM] * 2, out_specs=[VMEM] * 2,
            out_shape=piece(quarter), compiler_params=params(8),
            cost_estimate=estimate(10 ** 9, 1 << 20),
        )(merged, weight)

    def call(kernel, rows, columns, *blocks):
        return pl.pallas_call(
            kernel, in_specs=[VMEM] * len(blocks), out_specs=[VMEM] * len(rows),
            out_shape=[struct((r, columns), bf16) for r in rows],
            compiler_params=params(6), cost_estimate=estimate(10 ** 6, 1 << 20),
        )(*blocks)

    def move(block, route):
        return lax.ppermute(block, "tp", route)

    keep, send, merged, weight_b = last(
        index, tiles, own, *fa, *fb, maxima, acc, weight_a, in_hbm(out_weight)
    )
    stays, blocks = [], []
    for q in range(4):
        if q > 0:
            keep, send = rest(q, merged, weight_a if q < 2 else weight_b)
        got = move(send, swap_route())
        kernel = functools.partial(pair_kernel, q % 2)
        stay, out = call(kernel, (rows // 2,) * 2, COLUMNS[q], keep, got)
        stays.append((stay, move(out, step_route(q % 2))))
    for q, (stay, got) in enumerate(stays):
        mine, out = call(fold_kernel, (rows // 4,) * 2, COLUMNS[q], stay, got)
        blocks += [mine, move(out, step_route(1 - q % 2))]
    return call(final_kernel, (rows // 4,), DOUT, *blocks)[0]


def solution(mesh):
    return jax.shard_map(
        on_device,
        mesh=mesh,
        in_specs=(P("ctx", "tp"), P("ctx", "tp"), P("ctx", "tp"), P("ctx"), P("tp", None)),
        out_specs=P(("ctx", "tp"), None),
        check_vma=False,
    )
```

```python
import functools
import math

import jax
import jax.numpy as jnp
from jax import lax
from jax.experimental import pallas as pl
from jax.experimental.pallas import tpu as pltpu
from jax.sharding import PartitionSpec as P


HD = 128
SPAN = 128
HEADS = 8
SLICE = 8
WIDTH = 4
COLUMNS = (2048, 2048, 2560, 1536)
PACK = 264
SLOT = 272
LOG_SCALE = HD ** -0.5 * math.log2(math.e)
NEG = -1e30
NX = 4
NZ = 4
NCORE = 2
DOUT = 8192
STARTS_AT = (0, 2048, 4096, 6656)
GROUP = 4
HEADROOM = 60.0
TILE = 512
NW = 4
HOPS = (1, 3, 2)


VMEM = pl.BlockSpec(memory_space=pltpu.VMEM)
SMEM = pl.BlockSpec(memory_space=pltpu.SMEM)
HBM = pl.BlockSpec(memory_space=pltpu.HBM)


def struct(shape, dtype):
    return jax.ShapeDtypeStruct(shape, dtype)


def pack_kernel(pos_hbm, k_hbm, v_hbm, out_ref, pos_ref, k_ref, v_ref, sems):
    copies = [
        pltpu.make_async_copy(src, dst, sems.at[i])
        for i, (src, dst) in enumerate(((v_hbm, v_ref), (k_hbm, k_ref), (pos_hbm, pos_ref)))
    ]
    for copy in copies:
        copy.start()
    for copy in copies:
        copy.wait()
    for s in range(2):
        rows = slice(s * SPAN, (s + 1) * SPAN)
        span = (pos_ref[s * SPAN] // SPAN).astype(jnp.float32)
        base = s * PACK
        out_ref[base:base + 128] = k_ref[rows, :]
        out_ref[base + 128:base + 256] = v_ref[rows, :].T
        ids = jnp.full((PACK - 256, 128), span, jnp.float32).astype(jnp.bfloat16)
        out_ref[base + 256:base + PACK] = ids


def join_kernel(part, *refs):
    out_ref = refs[-1]
    for i, ref in enumerate(refs[:-1]):
        out_ref[i * PACK:(i + 1) * PACK] = ref[part * PACK:(part + 1) * PACK]


def query_tile(q_ref, s, j):
    pieces = []
    for h in range(HEADS):
        for t in range(4):
            row = s * SPAN + t * 32 + j * SLICE
            pieces.append(q_ref[row:row + SLICE, h * HD:(h + 1) * HD])
    return jnp.concatenate(pieces, axis=0)


def scores_of(kt, q):
    return lax.dot_general(kt, q, (((1,), (1,)), ((), ())), preferred_element_type=jnp.float32)


def weighted(vt, probs):
    return jnp.dot(vt, probs, preferred_element_type=jnp.float32)


def store_keys(kv_ref, blocks):
    for i, (ref, j) in enumerate(blocks):
        kv_ref[i, 0:256, :] = ref[j * PACK:j * PACK + 256, :]
        kv_ref[i, 256:SLOT, :] = jnp.ones((16, 128), jnp.bfloat16)
    kv_ref[len(blocks)] = jnp.zeros((SLOT, 128), jnp.bfloat16)


def span_id(ref, i):
    ids = ref[i * PACK + 256:(i + 1) * PACK, :].astype(jnp.float32)
    return jnp.max(ids).astype(jnp.int32)


def visible_list(list_ref, ids, limit):
    count = jnp.int32(0)
    for i, span in enumerate(ids):
        list_ref[count] = jnp.int32(i)
        count = count + jnp.where(span < limit, 1, 0)
    for i in range(GROUP):
        list_ref[count + i] = jnp.int32(len(ids))
    return count


def fast_walk(kv_ref, list_ref, count, queries, units, m_ref, peak_ref, acc_ref, probs):
    shifts = [m_ref[u][0:1, :] for u in units]

    def score(g, p_ref):
        slots = [list_ref[g * GROUP + i] for i in range(GROUP)]
        kt = jnp.concatenate([kv_ref[i, 0:128, :] for i in slots], axis=0)
        for n, u in enumerate(units):
            scores = scores_of(kt, queries[n])
            tiles = scores.reshape(GROUP * SPAN // 8, 8, 256)
            peak_ref[u] = jnp.maximum(peak_ref[u], jnp.max(tiles, axis=0))
            p_ref[n] = jnp.exp2((scores - shifts[n]) * LOG_SCALE).astype(jnp.bfloat16)

    def add(g, p_ref):
        slots = [list_ref[g * GROUP + i] for i in range(GROUP)]
        vt = jnp.concatenate([kv_ref[i, 128:SLOT, :] for i in slots], axis=1)
        for n, u in enumerate(units):
            acc_ref[u] = acc_ref[u] + weighted(vt, p_ref[n])

    even, odd = probs
    groups = jnp.maximum((count + GROUP - 1) // GROUP, 1)
    score(0, even)

    def pair(i, carry):
        score(2 * i + 1, odd)
        add(2 * i, even)
        score(2 * i + 2, even)
        add(2 * i + 1, odd)
        return carry

    lax.fori_loop(0, (groups - 1) // 2, pair, 0)

    @pl.when(groups % 2 == 1)
    def _():
        add(groups - 1, even)

    @pl.when(groups % 2 == 0)
    def _():
        score(groups - 1, odd)
        add(groups - 2, even)
        add(groups - 1, odd)


def slow_walk(kv_ref, list_ref, count, queries, units, m_ref, acc_ref):
    def step(i, carry):
        slot = list_ref[i]
        for n, u in enumerate(units):
            scores = scores_of(kv_ref[slot, 0:128, :], queries[n])
            m_old = m_ref[u][0:1, :]
            m_new = jnp.maximum(m_old, jnp.max(scores, axis=0, keepdims=True))
            probs = jnp.exp2((scores - m_new) * LOG_SCALE).astype(jnp.bfloat16)
            scale = jnp.exp2((m_old - m_new) * LOG_SCALE)
            acc_ref[u] = acc_ref[u] * scale + weighted(kv_ref[slot, 128:SLOT, :], probs)
            m_ref[u] = jnp.broadcast_to(m_new, (8, 256))
        return carry

    lax.fori_loop(0, count, step, 0)


def overshoot(peak_ref, m_ref, units):
    worst = peak_ref[units[0]] - m_ref[units[0]]
    for u in units[1:]:
        worst = jnp.maximum(worst, peak_ref[u] - m_ref[u])
    return jnp.max(worst) * LOG_SCALE > HEADROOM


def fetch_half(half, w_hbm, w_ref, sems):
    copies = []
    for j in range(NW):
        rows = pl.ds(j * (1024 // NW), 1024 // NW)
        columns = pl.ds(half * DOUT // 2, DOUT // 2)
        copies.append(pltpu.make_async_copy(w_hbm.at[rows, columns], w_ref.at[rows], sems.at[j]))
        copies[j].start()
    return copies


def first_kernel(q_hbm, w_hbm, own_ref, x1, x2, x3, y1, y2, y3, m_ref, acc_ref, tile_ref, w_ref,
                 q_ref, kv_ref, peak_ref, even_ref, odd_ref, list0, list1, sems):
    fetch_q = pltpu.make_async_copy(q_hbm, q_ref, sems.at[NW])
    fetch_q.start()
    fetch_w = fetch_half(0, w_hbm, w_ref, sems)
    blocks = [(ref, j) for ref in (own_ref, x1, x2, x3, y1, y2, y3) for j in range(2)]
    store_keys(kv_ref, blocks)
    ids = [span_id(ref, j) for ref, j in blocks]
    counts = [visible_list(ref, ids, ids[s]) for s, ref in enumerate((list0, list1))]
    lists = (list0, list1)
    fetch_q.wait()
    for s in range(2):
        for j in range(4):
            tile_ref[s * 4 + j] = query_tile(q_ref, s, j)
    units = [[s * 4 + j for j in range(4)] for s in range(2)]
    queries = [[tile_ref[u] for u in units[s]] for s in range(2)]

    def own_block():
        for s in range(2):
            for n, u in enumerate(units[s]):
                lane = lax.broadcasted_iota(jnp.int32, (SPAN, 256), 1) % 32
                row = (lane // SLICE) * 32 + lane % SLICE + n * SLICE
                scores = scores_of(kv_ref[s, 0:128, :], queries[s][n])
                key = lax.broadcasted_iota(jnp.int32, (SPAN, 256), 0)
                scores = jnp.where(key <= row, scores, NEG)
                m_new = jnp.max(scores, axis=0, keepdims=True)
                probs = jnp.exp2((scores - m_new) * LOG_SCALE).astype(jnp.bfloat16)
                acc_ref[u] = weighted(kv_ref[s, 128:SLOT, :], probs)
                m_ref[u] = jnp.broadcast_to(m_new, (8, 256))

    own_block()
    peak_ref[...] = m_ref[...]
    for s in range(2):
        fast_walk(kv_ref, lists[s], counts[s], queries[s], units[s], m_ref, peak_ref, acc_ref,
                  (even_ref, odd_ref))

    @pl.when(overshoot(peak_ref, m_ref, units[0] + units[1]))
    def _():
        own_block()
        for s in range(2):
            slow_walk(kv_ref, lists[s], counts[s], queries[s], units[s], m_ref, acc_ref)

    for copy in fetch_w:
        copy.wait()


def rest_of_attention(tile_ref, own_ref, far, m_in, acc_in, kv_ref, m_ref, peak_ref,
                      acc_ref, even_ref, odd_ref, lists):
    blocks = [(ref, j) for ref in far for j in range(3)]
    store_keys(kv_ref, blocks)
    ids = [span_id(ref, j) for ref, j in blocks]
    counts = [visible_list(lists[s], ids, span_id(own_ref, s)) for s in range(2)]
    units = [[s * WIDTH + n for n in range(WIDTH)] for s in range(2)]
    queries = [[tile_ref[u] for u in units[s]] for s in range(2)]

    def reset():
        m_ref[...] = m_in[...]
        acc_ref[...] = acc_in[...]

    reset()
    peak_ref[...] = m_ref[...]
    for s in range(2):
        fast_walk(kv_ref, lists[s], counts[s], queries[s], units[s], m_ref, peak_ref, acc_ref,
                  (even_ref, odd_ref))

    @pl.when(overshoot(peak_ref, m_ref, range(2 * WIDTH)))
    def _():
        reset()
        for s in range(2):
            slow_walk(kv_ref, lists[s], counts[s], queries[s], units[s], m_ref, acc_ref)


def place_of(z_to, core_to, z, core):
    slot = jnp.where((z ^ 1) == z_to, 2, 1)
    slot = jnp.where(z_to == z, 0, jnp.where((z_to + 2) % NZ == z, 3, slot))
    return (core_to ^ core) * NZ + slot


def finish(acc_ref, index_ref, merged_ref):
    z, core = index_ref[0] // NCORE, index_ref[0] % NCORE
    for s in range(2):
        starts = []
        for t in range(4):
            owner = s * 4 + t
            place = place_of(owner // NCORE, owner % NCORE, z, core)
            starts.append(pl.multiple_of(place * (WIDTH * SLICE), SLICE))
        for n in range(WIDTH):
            acc = acc_ref[s * WIDTH + n]
            o = acc[:128] * (1.0 / acc[128:129])
            for half in range(2):
                rows = o[:, half * 128:(half + 1) * 128].T.astype(jnp.bfloat16)
                for i in range(4):
                    columns = slice((half * 4 + i) * HD, (half * 4 + i + 1) * HD)
                    for t in range(4):
                        at = i * 32 + t * SLICE
                        where = pl.ds(starts[t] + n * SLICE, SLICE)
                        merged_ref[where, columns] = rows[at:at + SLICE]


def project(quarter, merged_ref, w_ref, keep_ref, send_ref):
    rows = keep_ref.shape[0]
    first = STARTS_AT[quarter] - quarter // 2 * (DOUT // 2)
    for j in range(COLUMNS[quarter] // TILE):
        at = slice(j * TILE, (j + 1) * TILE)
        w = w_ref[:, first + j * TILE:first + (j + 1) * TILE]
        part = jnp.dot(merged_ref[...], w, preferred_element_type=jnp.float32)
        part = part.astype(jnp.bfloat16)
        keep_ref[:, at] = part[:rows]
        send_ref[:, at] = part[rows:]


def second_kernel(tile_ref, own_ref, f1, f2, f3, m_in, acc_in, m_ref, acc_ref, kv_ref, peak_ref,
                  even_ref, odd_ref, list0, list1):
    rest_of_attention(tile_ref, own_ref, (f1, f2, f3), m_in, acc_in, kv_ref, m_ref, peak_ref,
                      acc_ref, even_ref, odd_ref, (list0, list1))


def last_kernel(index_ref, tile_ref, own_ref, f1, f2, f3, m_in, acc_in, w_ref, w_hbm,
                keep_ref, send_ref, merged_ref, w_next, acc_ref, kv_ref, m_ref, peak_ref, even_ref,
                odd_ref, list0, list1, sems):
    fetch_w = fetch_half(1, w_hbm, w_next, sems)
    rest_of_attention(tile_ref, own_ref, (f1, f2, f3), m_in, acc_in, kv_ref, m_ref,
                      peak_ref, acc_ref, even_ref, odd_ref, (list0, list1))
    finish(acc_ref, index_ref, merged_ref)
    project(0, merged_ref, w_ref, keep_ref, send_ref)
    for copy in fetch_w:
        copy.wait()


def pair_kernel(pairing, keep_ref, got_ref, stay_ref, send_ref):
    stay, send = ((0, 1), (2, 3)) if pairing == 0 else ((0, 2), (1, 3))
    size = keep_ref.shape[0] // NZ
    for out_ref, slots in ((stay_ref, stay), (send_ref, send)):
        for i, slot in enumerate(slots):
            rows = slice(slot * size, (slot + 1) * size)
            total = keep_ref[rows].astype(jnp.float32) + got_ref[rows]
            out_ref[i * size:(i + 1) * size] = total.astype(jnp.bfloat16)


def fold_kernel(stay_ref, got_ref, mine_ref, send_ref):
    total = (stay_ref[...].astype(jnp.float32) + got_ref[...]).astype(jnp.bfloat16)
    size = total.shape[0] // 2
    mine_ref[...] = total[:size]
    send_ref[...] = total[size:]


def final_kernel(*refs):
    out_ref = refs[-1]
    for q, (start, width) in enumerate(zip(STARTS_AT, COLUMNS)):
        total = refs[2 * q][...].astype(jnp.float32) + refs[2 * q + 1][...]
        out_ref[:, start:start + width] = total.astype(jnp.bfloat16)


def in_hbm(array):
    return pltpu.with_memory_space_constraint(array, pltpu.HBM)


def params(mib):
    return pltpu.CompilerParams(vmem_limit_bytes=mib << 20)


def estimate(flops, traffic):
    return pl.CostEstimate(flops=flops, bytes_accessed=traffic, transcendentals=0)


def ctx_route(dx, dy):
    return [
        (x * NX + y, ((x + dx) % NX) * NX + (y + dy) % NX)
        for x in range(NX) for y in range(NX)
    ]


def swap_route():
    return [(t, t ^ 1) for t in range(NZ * NCORE)]


def step_route(pairing):
    return [
        (z * NCORE + c, ((((z + pairing) ^ 1) - pairing) % NZ) * NCORE + c)
        for z in range(NZ) for c in range(NCORE)
    ]


def on_device(queries, keys, values, positions, out_weight):
    bf16, f32 = jnp.bfloat16, jnp.float32
    index = lax.axis_index("tp").reshape(1)

    own = pl.pallas_call(
        pack_kernel, in_specs=[HBM] * 3, out_specs=VMEM, out_shape=struct((2 * PACK, HD), bf16),
        name="pack", compiler_params=params(2),
        scratch_shapes=[
            pltpu.SMEM((2 * SPAN,), jnp.int32), pltpu.VMEM((2 * SPAN, HD), bf16),
            pltpu.VMEM((2 * SPAN, HD), bf16), pltpu.SemaphoreType.DMA((3,)),
        ],
    )(in_hbm(positions), in_hbm(keys), in_hbm(values))

    def shifts(block, dx, dy):
        moved = []
        for d in HOPS:
            moved.append(lax.ppermute(block, "ctx", ctx_route(dx * d, dy * d)))
        return moved

    def join(part, *blocks):
        return pl.pallas_call(
            functools.partial(join_kernel, part), in_specs=[VMEM] * len(blocks), out_specs=VMEM,
            out_shape=struct((len(blocks) * PACK, HD), bf16), name="join",
            compiler_params=params(2),
        )(*blocks)

    ys = shifts(own, 0, 1)
    xs = shifts(own, 1, 0)
    column = join(1, *ys)
    fb = shifts(column, 1, 0)
    fa = shifts(join(0, *xs), 0, 1)

    def walk_scratch(slots, units, width):
        return [
            pltpu.VMEM((slots + 1, SLOT, 128), bf16),
            pltpu.VMEM((units, 8, 256), f32),
            pltpu.VMEM((units, 8, 256), f32),
            pltpu.VMEM((width, GROUP * SPAN, 256), bf16),
            pltpu.VMEM((width, GROUP * SPAN, 256), bf16),
            pltpu.SMEM((32,), jnp.int32),
            pltpu.SMEM((32,), jnp.int32),
        ]

    scratch = walk_scratch(14, 8, 4)
    first = pl.pallas_call(
        first_kernel, in_specs=[HBM] * 2 + [VMEM] * 7, out_specs=[VMEM] * 4,
        out_shape=[
            struct((8, 8, 256), f32), struct((8, 144, 256), f32),
            struct((8, 256, 128), bf16), struct((1024, DOUT // 2), bf16),
        ],
        scratch_shapes=[pltpu.VMEM((256, 1024), bf16)] + scratch[:1] + scratch[2:]
        + [pltpu.SemaphoreType.DMA((NW + 1,))],
        compiler_params=params(14), name="first",
        cost_estimate=estimate(4 * 10 ** 9, 1 << 20),
    )
    maxima, acc, tiles, weight_a = first(
        in_hbm(queries), in_hbm(out_weight), own, *xs, *ys
    )

    rows = NZ * WIDTH * SLICE

    def piece(quarter):
        return [struct((rows, COLUMNS[quarter]), bf16)] * 2

    scratch = walk_scratch(9, 2 * WIDTH, WIDTH)
    second = pl.pallas_call(
        second_kernel, in_specs=[VMEM] * 7, out_specs=[VMEM] * 2,
        out_shape=[struct((8, 8, 256), f32), struct((8, 144, 256), f32)],
        scratch_shapes=scratch[:1] + scratch[2:], compiler_params=params(14), name="second",
        cost_estimate=estimate(3 * 10 ** 9, 1 << 20),
    )
    maxima, acc = second(tiles, own, *fb, maxima, acc)
    last = pl.pallas_call(
        last_kernel, in_specs=[SMEM] + [VMEM] * 8 + [HBM], out_specs=[VMEM] * 4,
        out_shape=piece(0) + [struct((2 * rows, 1024), bf16), struct((1024, DOUT // 2), bf16)],
        scratch_shapes=[pltpu.VMEM((2 * WIDTH, 144, 256), f32)] + scratch
        + [pltpu.SemaphoreType.DMA((NW,))],
        compiler_params=params(16), name="last", cost_estimate=estimate(5 * 10 ** 9, 1 << 20),
    )

    def rest(quarter, merged, weight):
        return pl.pallas_call(
            functools.partial(project, quarter), in_specs=[VMEM] * 2, out_specs=[VMEM] * 2,
            out_shape=piece(quarter), compiler_params=params(8),
            cost_estimate=estimate(10 ** 9, 1 << 20),
        )(merged, weight)

    def call(kernel, rows, columns, *blocks):
        return pl.pallas_call(
            kernel, in_specs=[VMEM] * len(blocks), out_specs=[VMEM] * len(rows),
            out_shape=[struct((r, columns), bf16) for r in rows],
            compiler_params=params(6), cost_estimate=estimate(10 ** 6, 1 << 20),
        )(*blocks)

    def move(block, route):
        return lax.ppermute(block, "tp", route)

    keep, send, merged, weight_b = last(
        index, tiles, own, *fa, maxima, acc, weight_a, in_hbm(out_weight)
    )
    stays, blocks = [], []
    for q in range(4):
        if q > 0:
            keep, send = rest(q, merged, weight_a if q < 2 else weight_b)
        got = move(send, swap_route())
        kernel = functools.partial(pair_kernel, q % 2)
        stay, out = call(kernel, (rows // 2,) * 2, COLUMNS[q], keep, got)
        stays.append((stay, move(out, step_route(q % 2))))
    for q, (stay, got) in enumerate(stays):
        mine, out = call(fold_kernel, (rows // 4,) * 2, COLUMNS[q], stay, got)
        blocks += [mine, move(out, step_route(1 - q % 2))]
    return call(final_kernel, (rows // 4,), DOUT, *blocks)[0]


def solution(mesh):
    return jax.shard_map(
        on_device,
        mesh=mesh,
        in_specs=(P("ctx", "tp"), P("ctx", "tp"), P("ctx", "tp"), P("ctx"), P("tp", None)),
        out_specs=P(("ctx", "tp"), None),
        check_vma=False,
    )
```
